32 devices in a mesh: ctx: 4 (over z), seq: 4 (over x, core), wsh: 2 (over y).
Axes of the slice: x: 2, y: 2, z: 4, core: 2. Of those that a mesh axis runs over, the one named last changes fastest.
Arguments:
- states: bfloat16 [8, 1536, 512], P(('seq', 'wsh'), 'ctx'), may hold values from -6 to 6
- remaining: float32 [8, 1536], P(('seq', 'wsh'), 'ctx'), may hold values from 0.2 to 1
- moa_ids: int32 [8, 1536, 4], P(('seq', 'wsh'), 'ctx'), may hold values from 0 to 23, all different within a row
- ffn_ids: int32 [8, 1536, 2], P(('seq', 'wsh'), 'ctx'), may hold values from 0 to 7, all different within a row; in each aligned block of 384 rows (0 to 383, 384 to 767, ..., all dimensions but the last counted through in order) at most 192 rows name the same one
- out_cotangent: float32 [8, 1536, 512], P(('seq', 'wsh'), 'ctx'), may hold values from -6 to 6
- left_cotangent: float32 [8, 1536], P(('seq', 'wsh'), 'ctx'), may hold values from -6 to 6
- query_weight: bfloat16 [512, 1536], P(('seq', 'wsh')), may hold values from -0.5 to 0.5
- keyval_weight: bfloat16 [512, 128], P(('seq', 'wsh')), may hold values from -0.25 to 0.25
- project_weight: bfloat16 [1536, 512], P(('seq', 'wsh')), may hold values from -6 to 6
- chooser: bfloat16 [512, 24], P(('seq', 'wsh')), may hold values from -0.125 to 0.125
- selector: bfloat16 [512, 8], P(('seq', 'wsh')), may hold values from -0.1875 to 0.1875
- gain_one: bfloat16 [512], P(('seq', 'wsh')), may hold values from 0.099609375 to 1.8984375
- bias_one: bfloat16 [512], P(('seq', 'wsh')), may hold values from -1 to 1
- gain_two: bfloat16 [512], P(('seq', 'wsh')), may hold values from 0.099609375 to 1.8984375
- bias_two: bfloat16 [512], P(('seq', 'wsh')), may hold values from -1 to 1
- halt_weight: bfloat16 [512], P(('seq', 'wsh')), may hold values from -0.25 to 0.25
- expert_in: bfloat16 [8, 512, 2048], P('ctx', ('seq', 'wsh')), may hold values from -0.25 to 0.25
- expert_out: bfloat16 [8, 2048, 512], P('ctx', ('seq', 'wsh')), may hold values from -0.25 to 0.25
Outputs:
- new_states: bfloat16 [8, 1536, 512], P(('seq', 'wsh'), 'ctx')
- remaining_next: float32 [8, 1536], P(('seq', 'wsh'), 'ctx')
- grad_states: float32 [8, 1536, 512], P(('seq', 'wsh'), 'ctx')
- grad_remaining: float32 [8, 1536], P(('seq', 'wsh'), 'ctx')
- grad_query: float32 [512, 1536], P(('seq', 'wsh'))
- grad_keyval: float32 [512, 128], P(('seq', 'wsh'))
- grad_project: float32 [1536, 512], P(('seq', 'wsh'))
- grad_chooser: float32 [512, 24], P(('seq', 'wsh'))
- grad_selector: float32 [512, 8], P(('seq', 'wsh'))
- grad_gain_one: float32 [512], P(('seq', 'wsh'))
- grad_bias_one: float32 [512], P(('seq', 'wsh'))
- grad_gain_two: float32 [512], P(('seq', 'wsh'))
- grad_bias_two: float32 [512], P(('seq', 'wsh'))
- grad_halt: float32 [512], P(('seq', 'wsh'))
- grad_expert_in: float32 [8, 512, 2048], P('ctx', ('seq', 'wsh'))
- grad_expert_out: float32 [8, 2048, 512], P('ctx', ('seq', 'wsh'))
The draws below stay inside these ranges and needn't reach their ends.
Inputs may be any that keep to these rules, and one draw needn't show every extreme that they name: `moa_ids`: each row names 4 different attention experts. `ffn_ids`: within the rows of one device (aligned blocks of 384 positions) no expert is named more than 192 times, and in every draw some expert is named exactly 192 times by one device's rows. A row names two different experts.
All inputs are finite; a program needn't handle non-finite values.
Results may differ from the reference program's by a relative error of at most 0.025.
Values may be sent and summed in bfloat16 or wider, within the bound.
A program may use at most 192 MiB of HBM per device.

```python
import math
import jax
import jax.numpy as jnp
import numpy as np
from jax import lax

D = 512
HS = 64
MOA_EXPERTS = 24
MOA_TOP = 4
FF = 2048
FFN_TOP = 2
TOK_DEV = 384
LENGTH = 1536
SEQS = 8
EXPERTS = 8
CAP = 192


def block_scale(own_key, extent, split, low, top_value):
    def one(dim, shards_of):
        draws = jax.random.uniform(jax.random.fold_in(jax.random.fold_in(own_key, 6), dim), (shards_of,), jnp.float32, low / len(split), top_value / len(split))
        return jnp.repeat(jnp.exp(draws), extent[dim] // shards_of).reshape((-1,) + (1,) * (len(extent) - dim - 1))

    factor_of = one(*split[0])
    for cut in split[1:]:
        factor_of = factor_of * one(*cut)
    return factor_of


def different_ones(own_key, rows, number_of, top, lift):
    sequence = jax.random.permutation(jax.random.fold_in(own_key, 1), number_of)
    boost = sequence
    for power in range(3):
        boost = boost * boost // number_of
    boost = boost * lift // number_of
    tickets = jax.random.randint(jax.random.fold_in(own_key, 2), (rows, number_of), 0, 4096) + boost
    holders = jax.random.permutation(jax.random.fold_in(own_key, 3), rows)[jnp.arange(number_of) % rows]
    tickets = jnp.where(jnp.arange(rows)[:, None] == holders[None, :], 1 << 14, tickets)
    priority = tickets * number_of + jnp.arange(number_of)
    return lax.top_k(priority.astype(jnp.int32), top)[1].astype(jnp.int32)


def assign_block(rng, own, number, rows, amount, top, bound, lean):
    ranking = jax.random.permutation(rng, amount)
    heavy_load, usual = shares(amount, rows * top, bound, lean, True), shares(amount, rows * top, bound, lean, False)
    places = jnp.arange(amount)

    def named(lengths, turn):
        used = int((lengths > 0).sum())
        fixed = max(1, used // 4)
        shifted = fixed + (places - fixed + turn * (used - fixed)) % max(1, amount - fixed)
        return jnp.zeros((amount,), jnp.int32).at[ranking[jnp.where(places < fixed, places, shifted)]].set(jnp.asarray(lengths, jnp.int32))

    lengths = jnp.where(number % 4 == 0, named(heavy_load, number // 4), named(usual, number - number // 4 - 1))
    mixed = jax.random.permutation(jax.random.fold_in(own, 3), amount)
    source_of, receiver = mixed[0:amount // 2 * 2:2], mixed[1:amount // 2 * 2:2]
    slack = jnp.minimum(lengths[source_of] - 1, bound - lengths[receiver]) // 2
    slack = jnp.where((source_of == ranking[0]) | (receiver == ranking[0]) | (lengths[receiver] == 0), 0, jnp.maximum(slack, 0))
    shifted = jax.random.randint(jax.random.fold_in(own, 4), (amount // 2,), 0, 1 << 20) % (slack + 1)
    lengths = lengths.at[source_of].add(-shifted).at[receiver].add(shifted)
    labels = jnp.searchsorted(jnp.cumsum(lengths), jnp.arange(rows * top), side="right").astype(jnp.int32)
    table = labels.reshape(top, rows).T
    table = table[jax.random.permutation(jax.random.fold_in(own, 1), rows)]
    turn = jax.random.randint(jax.random.fold_in(own, 2), (rows, 1), 0, top)
    return jnp.take_along_axis(table, (jnp.arange(top)[None, :] + turn) % top, axis=1)


def shares(count, total, bound, lean, full):
    loads = [(1 << 20) // math.isqrt(standing ** lean) + 1 for standing in range(1, count + 1)]
    largest = bound if full else min(bound, max(-(-total // count), total * loads[0] // sum(loads)))
    least = 1 if total - largest >= count - 1 else 0
    given, spare = [largest] + [least] * (count - 1), total - largest - least * (count - 1)
    while spare > 0:
        free = [i for i in range(1, count) if given[i] < largest] or [i for i in range(1, count) if given[i] < bound]
        mass, left = sum([loads[i] for i in free]), spare
        for i in free:
            extra = min(bound - given[i], max(1, left * loads[i] // mass), spare)
            given[i] = given[i] + extra
            spare = spare - extra
    return np.array(given)


def gaussian(rng, dims, deviation, bound, shards=(), kind=jnp.bfloat16):
    array = deviation * jax.random.normal(rng, dims, jnp.float32)
    if shards:
        array = array * block_scale(rng, dims, shards, -0.22, 0.18)
    return jnp.clip(array, -bound, bound).astype(kind)


def setup_inputs(seed: int = 0) -> dict:
    key_list = jax.random.split(jax.random.key(seed), 19)
    states = gaussian(key_list[0], (SEQS, LENGTH, D), 1.0, 6.0, ((0, 8), (1, 4)))
    remaining = jnp.clip(0.2 + 0.8 * jax.random.uniform(key_list[1], (SEQS, LENGTH), jnp.float32) ** block_scale(key_list[1], (SEQS, LENGTH), ((0, 8), (1, 4)), -0.2, 0.2), 0.2, 1.0)
    moa_ids = different_ones(key_list[2], SEQS * LENGTH, MOA_EXPERTS, MOA_TOP, 0).reshape((SEQS, LENGTH, MOA_TOP))
    ffn_ids_keys = jax.random.split(jax.random.fold_in(key_list[3], 1), SEQS * LENGTH // TOK_DEV)
    ffn_ids_turns = jax.random.permutation(jax.random.fold_in(key_list[3], 3), SEQS * LENGTH // TOK_DEV)
    ffn_ids = jax.vmap(lambda own, number: assign_block(jax.random.fold_in(key_list[3], 2), own, number, TOK_DEV, EXPERTS, FFN_TOP, CAP, 2))(ffn_ids_keys, ffn_ids_turns).reshape((SEQS, LENGTH, FFN_TOP))
    out_cotangent = gaussian(key_list[4], (SEQS, LENGTH, D), 1.0, 6.0, ((0, 8), (1, 4)), jnp.float32)
    left_cotangent = gaussian(key_list[5], (SEQS, LENGTH), 1.0, 6.0, ((0, 8), (1, 4)), jnp.float32)
    query_weight = gaussian(key_list[6], (D, MOA_EXPERTS * HS), (D // 4) ** -0.5, 0.5, ((0, 8),))
    keyval_weight = gaussian(key_list[7], (D, 2 * HS), D ** -0.5, 0.25, ((0, 8),))
    project_weight = gaussian(key_list[8], (MOA_EXPERTS * HS, D), 1 ** -0.5, 6.0, ((0, 8),))
    chooser = gaussian(key_list[9], (D, MOA_EXPERTS), (4 * D) ** -0.5, 0.125, ((0, 8),))
    selector = gaussian(key_list[10], (D, EXPERTS), (2 * D) ** -0.5, 0.1875, ((0, 8),))
    gain_one = jnp.clip(1.0 + 0.18 * jax.random.normal(key_list[11], (D,), jnp.float32), 0.099609375, 1.8984375).astype(jnp.bfloat16)
    bias_one = gaussian(key_list[12], (D,), 0.2, 1.0, ((0, 8),))
    gain_two = jnp.clip(1.0 + 0.18 * jax.random.normal(key_list[13], (D,), jnp.float32), 0.099609375, 1.8984375).astype(jnp.bfloat16)
    bias_two = gaussian(key_list[14], (D,), 0.2, 1.0, ((0, 8),))
    halt_weight = gaussian(key_list[15], (D,), D ** -0.5, 0.25, ((0, 8),))
    expert_in = gaussian(key_list[16], (EXPERTS, D, FF), D ** -0.5, 0.25, ((0, 4), (1, 8)))
    expert_out = gaussian(key_list[17], (EXPERTS, FF, D), (FF // 4) ** -0.5, 0.25, ((0, 4), (1, 8)))
    return {"states": states, "remaining": remaining, "moa_ids": moa_ids, "ffn_ids": ffn_ids, "out_cotangent": out_cotangent, "left_cotangent": left_cotangent, "query_weight": query_weight, "keyval_weight": keyval_weight, "project_weight": project_weight, "chooser": chooser, "selector": selector, "gain_one": gain_one, "bias_one": bias_one, "gain_two": gain_two, "bias_two": bias_two, "halt_weight": halt_weight, "expert_in": expert_in, "expert_out": expert_out}


@jax.custom_vjp
def low(v):
    return lax.optimization_barrier(v.astype(jnp.bfloat16)).astype(jnp.float32)

@jax.custom_vjp
def low_back(v):
    return v

def low_keep(v):
    return (low(v), None)

def low_pass(kept, grad):
    return (grad,)

def back_keep(v):
    return (v, None)

def back_low(kept, grad):
    return (low(grad),)
low.defvjp(low_keep, low_pass)
low_back.defvjp(back_keep, back_low)
EPS = 1e-05
HIGH = lax.Precision.HIGHEST

def product(left, right):
    return jnp.dot(left, right, precision=HIGH)

def layer_norm(values, gain, bias):
    centred = values - lax.optimization_barrier(jnp.mean(values, -1, keepdims=True))
    variance = lax.optimization_barrier(jnp.mean(centred * centred, -1, keepdims=True))
    return centred * lax.rsqrt(variance + EPS) * gain + bias

def one_hot(index, count):
    return (index[..., None] == jnp.arange(count, dtype=jnp.int32)).astype(jnp.float32)

def block_slots(block_ids):
    flat_ids = block_ids.reshape(-1)
    table = (flat_ids[:, None] == jnp.arange(EXPERTS, dtype=jnp.int32)[None, :]).astype(jnp.int32)
    earlier = jnp.cumsum(table, 0).astype(jnp.int32) - table
    return lax.optimization_barrier(jnp.sum(earlier * table, 1)).astype(jnp.int32).reshape(block_ids.shape)

def attend_sequence(queries, keys_seq, values_seq):
    block_size = min(512, LENGTH)
    grouped = queries.reshape(LENGTH // block_size, block_size * MOA_TOP, HS)

    def one_block(query_block):
        scores = low_back(product(query_block, keys_seq.T)) * HS ** (-0.5)
        weights = low(jax.nn.softmax(scores, -1))
        return product(weights, values_seq)
    return lax.map(jax.checkpoint(one_block), grouped).reshape(LENGTH, MOA_TOP, HS)

def forward(resident, remaining, query_weight, keyval_weight, project_weight, chooser, selector, gain_one, bias_one, gain_two, bias_two, halt_weight, expert_in, expert_out, head_ids, route_ids):
    token_count = resident.shape[0]
    acted = low(layer_norm(resident, gain_one, bias_one))
    query_all = low(low_back(product(acted, query_weight))).reshape(token_count, MOA_EXPERTS, HS)
    query_sel = jnp.take_along_axis(query_all, head_ids[:, :, None], axis=1)
    keyval = low(low_back(product(acted, keyval_weight)))
    chosen = one_hot(head_ids, MOA_EXPERTS)
    head_logits = lax.optimization_barrier(jnp.sum(chosen * product(acted, chooser)[:, None, :], -1))
    head_gates = jax.nn.softmax(head_logits, -1)
    heads_out = lax.map(lambda items: attend_sequence(items[0], items[1], items[2]), (query_sel.reshape(SEQS, LENGTH, MOA_TOP, HS), keyval[:, :HS].reshape(SEQS, LENGTH, HS), keyval[:, HS:].reshape(SEQS, LENGTH, HS)))
    heads_out = low_back(heads_out.reshape(token_count, MOA_TOP, HS))
    mixed_sel = low(head_gates[:, :, None] * heads_out)
    mixed = jnp.einsum('tje,tjd->ted', chosen, mixed_sel, precision=HIGH).reshape(token_count, MOA_EXPERTS * HS)
    middle = resident + low_back(product(mixed, project_weight))
    entering = low(layer_norm(middle, gain_two, bias_two))
    picked = one_hot(route_ids, EXPERTS)
    expert_logits = lax.optimization_barrier(jnp.sum(picked * product(entering, selector)[:, None, :], -1))
    expert_gates = jax.nn.softmax(expert_logits, -1)
    blocks = token_count // TOK_DEV
    slots = jax.vmap(block_slots)(route_ids.reshape(blocks, TOK_DEV, FFN_TOP)).reshape(token_count, FFN_TOP)
    block_of = (jnp.arange(token_count, dtype=jnp.int32) // TOK_DEV)[:, None]
    destination = ((route_ids * blocks + block_of) * CAP + slots).astype(jnp.int32)
    buffer = jnp.zeros((EXPERTS * blocks * CAP, D), jnp.float32)
    for column in range(FFN_TOP):
        buffer = buffer.at[destination[:, column]].set(low_back(entering))
    grouped_rows = buffer.reshape(EXPERTS, blocks * CAP, D)

    def run_expert(items):
        before = low_back(product(items[0], items[1]))
        activated = low(jax.nn.gelu(before, approximate=False))
        return product(activated, items[2])
    results = lax.map(jax.checkpoint(run_expert), (grouped_rows, expert_in, expert_out))
    results = low(low_back(results.reshape(-1, D)))
    final = middle
    for column in range(FFN_TOP):
        final = final + expert_gates[:, column:column + 1] * results[destination[:, column]]
    halting = jax.nn.sigmoid(jnp.dot(final, halt_weight, precision=HIGH))
    stopped = remaining * halting
    outputs = stopped[:, None] * resident + (1.0 - stopped)[:, None] * final
    return (outputs, remaining * (1.0 - halting))

def reference(states, remaining, moa_ids, ffn_ids, out_cotangent, left_cotangent, query_weight, keyval_weight, project_weight, chooser, selector, gain_one, bias_one, gain_two, bias_two, halt_weight, expert_in, expert_out):
    resident = states.reshape(-1, D).astype(jnp.float32)
    left_flat = remaining.reshape(-1)
    head_ids = moa_ids.reshape(-1, MOA_TOP).astype(jnp.int32)
    route_ids = ffn_ids.reshape(-1, FFN_TOP).astype(jnp.int32)
    weights = tuple((item.astype(jnp.float32) for item in (query_weight, keyval_weight, project_weight, chooser, selector, gain_one, bias_one, gain_two, bias_two, halt_weight, expert_in, expert_out)))

    def run_layer(resident_in, left_in, *params):
        return forward(resident_in, left_in, *params, head_ids, route_ids)
    (outputs, left_next), pullback = jax.vjp(run_layer, resident, left_flat, *weights)
    grads = pullback((out_cotangent.reshape(-1, D).astype(jnp.float32), left_cotangent.reshape(-1).astype(jnp.float32)))
    return (outputs.astype(jnp.bfloat16).reshape(SEQS, LENGTH, D), left_next.reshape(SEQS, LENGTH), grads[0].reshape(SEQS, LENGTH, D), grads[1].reshape(SEQS, LENGTH), grads[2], grads[3], grads[4], grads[5], grads[6], grads[7], grads[8], grads[9], grads[10], grads[11], grads[12], grads[13])
```

```python
from functools import partial

import jax
import jax.numpy as jnp
from jax import lax
from jax.experimental import pallas as pl
from jax.experimental.pallas import tpu as pltpu
from jax.sharding import PartitionSpec as P

D = 512
HS = 64
MOA_EXPERTS = 24
MOA_TOP = 4
EXP_DEV = 2
FFN_TOP = 2
FF = 2048


EPS = 1e-05
HIGH = lax.Precision.HIGHEST


def shifted(x, axis, by):
    length = lax.axis_size(axis)
    return lax.ppermute(x, axis, [(i, (i + by) % length) for i in range(length)])


def layer_norm(values, gain, bias):
    centred = values - jnp.mean(values, -1, keepdims=True)
    inverse = lax.rsqrt(jnp.mean(centred * centred, -1, keepdims=True) + EPS)
    normal = centred * inverse
    return (normal * gain + bias, normal, inverse)


def norm_back(incoming, normal, inverse, gain):
    scaled = incoming * gain
    inner_term = (
        scaled
        - jnp.mean(scaled, -1, keepdims=True)
        - normal * jnp.mean(scaled * normal, -1, keepdims=True)
    )
    return (inverse * inner_term, jnp.sum(incoming * normal, 0), jnp.sum(incoming, 0))


def one_hot(index, count):
    return (index[..., None] == jnp.arange(count, dtype=jnp.int32)).astype(jnp.float32)


def choose_back(gates, upstream):
    return gates * (upstream - jnp.sum(gates * upstream, -1, keepdims=True))


def block_rows(row_count):
    if row_count > 512 and row_count % 512 == 0:
        return 512
    return row_count


def expert_slots(route_ids, experts):
    flat_ids = route_ids.reshape(-1)
    table = (flat_ids[:, None] == jnp.arange(experts, dtype=jnp.int32)[None, :]).astype(jnp.float32)
    place = jnp.arange(flat_ids.shape[0], dtype=jnp.int32)
    before = (place[None, :] < place[:, None]).astype(jnp.bfloat16)
    earlier = jnp.dot(before, table.astype(jnp.bfloat16), preferred_element_type=jnp.float32)
    return jnp.sum(earlier * table, 1).astype(jnp.int32).reshape(route_ids.shape)


def general_body(
    states,
    remaining,
    moa_ids,
    ffn_ids,
    out_cotangent,
    left_cotangent,
    query_weight,
    keyval_weight,
    project_weight,
    chooser,
    selector,
    gain_one,
    bias_one,
    gain_two,
    bias_two,
    halt_weight,
    expert_in,
    expert_out,
):
    tokens = states.shape[1]
    devices = lax.axis_size("ctx")
    experts = EXP_DEV * devices
    capacity = max(2, (4 * tokens + experts - 1) // experts)
    rows_total = tokens * MOA_TOP
    scaling = HS ** (-0.5)
    f32 = jnp.float32
    bf16 = jnp.bfloat16
    (
        query_full,
        keyval_full,
        project_full,
        chooser_full,
        selector_full,
        gainone_full,
        biasone_full,
        gaintwo_full,
        biastwo_full,
        halt_full,
    ) = (
        lax.all_gather(query_weight, ("seq", "wsh"), axis=0, tiled=True),
        lax.all_gather(keyval_weight, ("seq", "wsh"), axis=0, tiled=True),
        lax.all_gather(project_weight, ("seq", "wsh"), axis=0, tiled=True),
        lax.all_gather(chooser, ("seq", "wsh"), axis=0, tiled=True),
        lax.all_gather(selector, ("seq", "wsh"), axis=0, tiled=True),
        lax.all_gather(gain_one, ("seq", "wsh"), axis=0, tiled=True),
        lax.all_gather(bias_one, ("seq", "wsh"), axis=0, tiled=True),
        lax.all_gather(gain_two, ("seq", "wsh"), axis=0, tiled=True),
        lax.all_gather(bias_two, ("seq", "wsh"), axis=0, tiled=True),
        lax.all_gather(halt_weight, ("seq", "wsh"), axis=0, tiled=True),
    )
    inner_full, outer_full = (
        lax.all_gather(expert_in, ("seq", "wsh"), axis=1, tiled=True),
        lax.all_gather(expert_out, ("seq", "wsh"), axis=1, tiled=True),
    )
    gain_first = gainone_full.astype(f32)
    gain_second = gaintwo_full.astype(f32)
    halt_vector = halt_full.astype(f32)
    resident = states[0].astype(f32)
    normed_one, normal_one, inverse_one = layer_norm(resident, gain_first, biasone_full.astype(f32))
    acted = normed_one.astype(bf16)
    query_all = (
        jnp.dot(acted, query_full, preferred_element_type=f32)
        .astype(bf16)
        .reshape(tokens, MOA_EXPERTS, HS)
    )
    head_ids = moa_ids[0]
    query_sel = jnp.take_along_axis(query_all, head_ids[:, :, None], axis=1).reshape(rows_total, HS)
    keyval = jnp.dot(acted, keyval_full, preferred_element_type=f32).astype(bf16)
    chosen = one_hot(head_ids, MOA_EXPERTS)
    head_logits = jnp.sum(
        chosen * jnp.dot(acted, chooser_full, preferred_element_type=f32)[:, None, :], -1
    )
    head_gates = jax.nn.softmax(head_logits, -1)
    start_state = (
        jnp.full((rows_total,), -1e30, f32),
        jnp.zeros((rows_total,), f32),
        jnp.zeros((rows_total, HS), f32),
    )
    running = start_state
    shard_rows = lax.all_gather(keyval, "ctx", axis=0, tiled=True)
    block_size = block_rows(shard_rows.shape[0])
    grouped = shard_rows.reshape(shard_rows.shape[0] // block_size, block_size, 2 * HS)

    def absorb(carried, key_block):
        row_peak, row_total, gathered = carried
        scores = jnp.dot(query_sel, key_block[:, :HS].T, preferred_element_type=f32) * scaling
        new_peak = jnp.maximum(row_peak, jnp.max(scores, -1))
        fading = jnp.exp(row_peak - new_peak)
        weights = jnp.exp(scores - new_peak[:, None])
        row_total = row_total * fading + jnp.sum(weights, -1)
        gathered = gathered * fading[:, None] + jnp.dot(
            weights.astype(bf16), key_block[:, HS:], preferred_element_type=f32
        )
        return ((new_peak, row_total, gathered), None)

    running, unused = lax.scan(absorb, running, grouped)
    row_peak, row_total, gathered = running
    heads_out = gathered / row_total[:, None]
    log_total = row_peak + jnp.log(row_total)
    heads_view = heads_out.reshape(tokens, MOA_TOP, HS)
    mixed_sel = (head_gates[:, :, None] * heads_view).astype(bf16)
    chosen_low = chosen.astype(bf16)
    mixture = jnp.sum(chosen_low[:, :, :, None] * mixed_sel[:, :, None, :], 1).reshape(
        tokens, MOA_EXPERTS * HS
    )
    middle = resident + jnp.dot(mixture, project_full, preferred_element_type=f32)
    normed_two, normal_two, inverse_two = layer_norm(middle, gain_second, biastwo_full.astype(f32))
    entering = normed_two.astype(bf16)
    route_ids = ffn_ids[0]
    picked = one_hot(route_ids, experts)
    expert_logits = jnp.sum(
        picked * jnp.dot(entering, selector_full, preferred_element_type=f32)[:, None, :], -1
    )
    expert_gates = jax.nn.softmax(expert_logits, -1)
    slots = expert_slots(route_ids, experts)
    target = (route_ids * capacity + slots).reshape(-1)
    copies = jnp.broadcast_to(entering[:, None, :], (tokens, FFN_TOP, D)).reshape(-1, D)
    outgoing = (
        jnp.zeros((experts * capacity, D), bf16)
        .at[target]
        .set(copies)
        .reshape(devices, EXP_DEV, capacity, D)
    )
    arrived_rows = lax.all_to_all(outgoing, "ctx", split_axis=0, concat_axis=0, tiled=True)
    before = jnp.einsum("nekd,edf->nekf", arrived_rows, inner_full, preferred_element_type=f32)
    activated = jax.nn.gelu(before, approximate=False).astype(bf16)
    result_rows = jnp.einsum(
        "nekf,efd->nekd", activated, outer_full, preferred_element_type=f32
    ).astype(bf16)
    returned = lax.all_to_all(result_rows, "ctx", split_axis=0, concat_axis=0, tiled=True).reshape(
        experts * capacity, D
    )
    expert_rows = returned[target].reshape(tokens, FFN_TOP, D).astype(f32)
    final = middle + jnp.sum(expert_gates[:, :, None] * expert_rows, 1)
    halting = jax.nn.sigmoid(jnp.dot(final, halt_vector, precision=HIGH))
    left_mass = remaining[0]
    stopped = left_mass * halting
    new_states = (stopped[:, None] * resident + (1.0 - stopped)[:, None] * final).astype(bf16)
    remaining_next = left_mass * (1.0 - halting)
    out_grad = out_cotangent[0]
    left_grad = left_cotangent[0]
    stop_grad = jnp.sum(out_grad * (resident - final), -1)
    grad_remaining = stop_grad * halting + left_grad * (1.0 - halting)
    halt_logit_grad = (stop_grad - left_grad) * left_mass * halting * (1.0 - halting)
    grad_halt = jnp.sum(halt_logit_grad[:, None] * final, 0)
    grad_final = (1.0 - stopped)[:, None] * out_grad + halt_logit_grad[:, None] * halt_vector
    gate_grad = jnp.sum(grad_final[:, None, :] * expert_rows, -1)
    selector_logit_grad = jnp.sum(choose_back(expert_gates, gate_grad)[:, :, None] * picked, 1)
    entering_wide = entering.astype(f32)
    grad_selector = jnp.dot(entering_wide.T, selector_logit_grad, precision=HIGH)
    rows_grad = (expert_gates[:, :, None] * grad_final[:, None, :]).astype(bf16).reshape(-1, D)
    grad_outgoing = (
        jnp.zeros((experts * capacity, D), bf16)
        .at[target]
        .set(rows_grad)
        .reshape(devices, EXP_DEV, capacity, D)
    )
    grad_arrived = lax.all_to_all(grad_outgoing, "ctx", split_axis=0, concat_axis=0, tiled=True)
    grad_activated = jnp.einsum(
        "nekd,efd->nekf", grad_arrived, outer_full, preferred_element_type=f32
    )
    activated_again, gelu_back = jax.vjp(partial(jax.nn.gelu, approximate=False), before)
    before_grad = gelu_back(grad_activated)[0].astype(bf16)
    outer_grad = jnp.einsum(
        "nekf,nekd->efd", activated_again.astype(bf16), grad_arrived, preferred_element_type=f32
    )
    inner_grad = jnp.einsum("nekd,nekf->edf", arrived_rows, before_grad, preferred_element_type=f32)
    grad_sent = jnp.einsum(
        "nekf,edf->nekd", before_grad, inner_full, preferred_element_type=f32
    ).astype(bf16)
    grad_back = lax.all_to_all(grad_sent, "ctx", split_axis=0, concat_axis=0, tiled=True).reshape(
        experts * capacity, D
    )
    entering_grad = jnp.sum(grad_back[target].reshape(tokens, FFN_TOP, D).astype(f32), 1)
    entering_grad = entering_grad + jnp.dot(
        selector_logit_grad, selector_full.astype(f32).T, precision=HIGH
    )
    middle_extra, grad_gain_two, grad_bias_two = norm_back(
        entering_grad, normal_two, inverse_two, gain_second
    )
    middle_grad = grad_final + middle_extra
    attn_grad = middle_grad.astype(bf16)
    grad_project = jnp.dot(mixture.T, attn_grad, preferred_element_type=f32)
    mix_grad = jnp.dot(attn_grad, project_full.T, preferred_element_type=f32).reshape(
        tokens, MOA_EXPERTS, HS
    )
    mix_sel_grad = jnp.take_along_axis(mix_grad, head_ids[:, :, None], axis=1)
    head_gate_grad = jnp.sum(mix_sel_grad * heads_view, -1)
    chooser_logit_grad = jnp.sum(choose_back(head_gates, head_gate_grad)[:, :, None] * chosen, 1)
    acted_wide = acted.astype(f32)
    grad_chooser = jnp.dot(acted_wide.T, chooser_logit_grad, precision=HIGH)
    acted_grad = jnp.dot(chooser_logit_grad, chooser_full.astype(f32).T, precision=HIGH)
    heads_grad = (head_gates[:, :, None] * mix_sel_grad).astype(bf16).reshape(rows_total, HS)
    row_delta = jnp.sum(heads_grad.astype(f32) * heads_out, -1)

    def cycle_turn(turn_index, carried):
        visiting, grads_visiting, query_grad = carried
        block_size = block_rows(tokens)

        def per_block(query_acc, key_block):
            scores = jnp.dot(query_sel, key_block[:, :HS].T, preferred_element_type=f32) * scaling
            probability = jnp.exp(scores - log_total[:, None])
            prob_grad = jnp.dot(heads_grad, key_block[:, HS:].T, preferred_element_type=f32)
            score_grad = (probability * (prob_grad - row_delta[:, None])).astype(bf16)
            query_acc = (
                query_acc
                + jnp.dot(score_grad, key_block[:, :HS], preferred_element_type=f32) * scaling
            )
            keys_grad = jnp.dot(score_grad.T, query_sel, preferred_element_type=f32) * scaling
            values_grad = jnp.dot(
                probability.astype(bf16).T, heads_grad, preferred_element_type=f32
            )
            return (query_acc, jnp.concatenate([keys_grad, values_grad], -1))

        query_grad, block_grads = lax.scan(
            per_block, query_grad, visiting.reshape(tokens // block_size, block_size, 2 * HS)
        )
        grads_visiting = grads_visiting + block_grads.reshape(tokens, 2 * HS)
        visiting = shifted(visiting, "ctx", 1)
        grads_visiting = shifted(grads_visiting.astype(jnp.bfloat16), "ctx", 1).astype(
            grads_visiting.dtype
        )
        return (visiting, grads_visiting, query_grad)

    cycle_state = (keyval, jnp.zeros((tokens, 2 * HS), f32), jnp.zeros((rows_total, HS), f32))
    unused_keys, keyval_grad, query_grad = lax.fori_loop(0, devices, cycle_turn, cycle_state)
    query_sel_grad = query_grad.astype(bf16).reshape(tokens, MOA_TOP, HS)
    query_all_grad = jnp.sum(chosen_low[:, :, :, None] * query_sel_grad[:, :, None, :], 1).reshape(
        tokens, MOA_EXPERTS * HS
    )
    keyval_low = keyval_grad.astype(bf16)
    grad_query = jnp.dot(acted.T, query_all_grad, preferred_element_type=f32)
    grad_keyval = jnp.dot(acted.T, keyval_low, preferred_element_type=f32)
    acted_grad = acted_grad + jnp.dot(query_all_grad, query_full.T, preferred_element_type=f32)
    acted_grad = acted_grad + jnp.dot(keyval_low, keyval_full.T, preferred_element_type=f32)
    resident_grad, grad_gain_one, grad_bias_one = norm_back(
        acted_grad, normal_one, inverse_one, gain_first
    )
    grad_states = middle_grad + resident_grad + stopped[:, None] * out_grad
    dense_grads = (
        grad_query,
        grad_keyval,
        grad_project,
        grad_chooser,
        grad_selector,
        grad_gain_one,
        grad_bias_one,
        grad_gain_two,
        grad_bias_two,
        grad_halt,
    )
    totals = (
        lax.psum(dense_grads[0].astype(jnp.bfloat16), "ctx").astype(jnp.float32),
        lax.psum(dense_grads[1].astype(jnp.bfloat16), "ctx").astype(jnp.float32),
        lax.psum(dense_grads[2].astype(jnp.bfloat16), "ctx").astype(jnp.float32),
        lax.psum(dense_grads[3].astype(jnp.bfloat16), "ctx").astype(jnp.float32),
        lax.psum(dense_grads[4].astype(jnp.bfloat16), "ctx").astype(jnp.float32),
        lax.psum(dense_grads[5].astype(jnp.bfloat16), "ctx").astype(jnp.float32),
        lax.psum(dense_grads[6].astype(jnp.bfloat16), "ctx").astype(jnp.float32),
        lax.psum(dense_grads[7].astype(jnp.bfloat16), "ctx").astype(jnp.float32),
        lax.psum(dense_grads[8].astype(jnp.bfloat16), "ctx").astype(jnp.float32),
        lax.psum(dense_grads[9].astype(jnp.bfloat16), "ctx").astype(jnp.float32),
    )
    shards = (
        lax.psum_scatter(
            totals[0].astype(jnp.bfloat16), ("seq", "wsh"), scatter_dimension=0, tiled=True
        ).astype(jnp.float32),
        lax.psum_scatter(
            totals[1].astype(jnp.bfloat16), ("seq", "wsh"), scatter_dimension=0, tiled=True
        ).astype(jnp.float32),
        lax.psum_scatter(
            totals[2].astype(jnp.bfloat16), ("seq", "wsh"), scatter_dimension=0, tiled=True
        ).astype(jnp.float32),
        lax.psum_scatter(
            totals[3].astype(jnp.bfloat16), ("seq", "wsh"), scatter_dimension=0, tiled=True
        ).astype(jnp.float32),
        lax.psum_scatter(
            totals[4].astype(jnp.bfloat16), ("seq", "wsh"), scatter_dimension=0, tiled=True
        ).astype(jnp.float32),
        lax.psum_scatter(
            totals[5].astype(jnp.bfloat16), ("seq", "wsh"), scatter_dimension=0, tiled=True
        ).astype(jnp.float32),
        lax.psum_scatter(
            totals[6].astype(jnp.bfloat16), ("seq", "wsh"), scatter_dimension=0, tiled=True
        ).astype(jnp.float32),
        lax.psum_scatter(
            totals[7].astype(jnp.bfloat16), ("seq", "wsh"), scatter_dimension=0, tiled=True
        ).astype(jnp.float32),
        lax.psum_scatter(
            totals[8].astype(jnp.bfloat16), ("seq", "wsh"), scatter_dimension=0, tiled=True
        ).astype(jnp.float32),
        lax.psum_scatter(
            totals[9].astype(jnp.bfloat16), ("seq", "wsh"), scatter_dimension=0, tiled=True
        ).astype(jnp.float32),
    )
    inner_shard, outer_shard = (
        lax.psum_scatter(
            inner_grad.astype(jnp.bfloat16), ("seq", "wsh"), scatter_dimension=1, tiled=True
        ).astype(jnp.float32),
        lax.psum_scatter(
            outer_grad.astype(jnp.bfloat16), ("seq", "wsh"), scatter_dimension=1, tiled=True
        ).astype(jnp.float32),
    )
    return (
        new_states[None],
        remaining_next[None],
        grad_states[None],
        grad_remaining[None],
        shards[0],
        shards[1],
        shards[2],
        shards[3],
        shards[4],
        shards[5],
        shards[6],
        shards[7],
        shards[8],
        shards[9],
        inner_shard,
        outer_shard,
    )


MESH = pl.DeviceIdType.MESH
CAP = 192
KEEP = 0.7071067811865476
SPREAD = 0.3989422804014327
ERF_P = 0.3275911
ERF_A = (0.254829592, -0.284496736, 1.421413741, -1.453152027, 1.061405429)


def remote(source, target, send_sem, recv_sem, device):
    return pltpu.make_async_remote_copy(
        src_ref=source,
        dst_ref=target,
        send_sem=send_sem,
        recv_sem=recv_sem,
        device_id=device,
        device_id_type=MESH,
    )


def places():
    ctx, seq, wsh = (lax.axis_index(name) for name in ("ctx", "seq", "wsh"))
    chip, core = seq // 2, seq % 2
    over = (1 - chip) * 2 + core
    twin = (ctx, chip * 2 + 1 - core, wsh)
    beside = (ctx, over, wsh)
    above = (ctx, seq, 1 - wsh)
    across = (ctx, over, 1 - wsh)
    return (ctx, seq, wsh), twin, beside, above, across


def shard_of(place):
    return place[1] * 2 + place[2]


def moved(place, offset, length):
    return ((place[0] + offset) % length, place[1], place[2])


class PlaneGather:
    def __init__(self, shard, full, halves, send, recv, local):
        self.shard, self.full, self.halves = shard, full, halves
        self.send, self.recv, self.local = send, recv, local
        self.me, self.twin, self.beside, self.above, self.across = places()

    def pair(self, view, slot, device):
        return remote(view, view, self.send.at[slot], self.recv.at[slot], device)

    def own(self, slot, device):
        target = self.full(shard_of(self.me))
        return remote(self.shard, target, self.send.at[slot], self.recv.at[slot], device)

    def keep(self):
        return pltpu.make_async_copy(self.shard, self.full(shard_of(self.me)), self.local)

    def start(self):
        self.own(0, self.twin).start()
        self.own(1, self.beside).start()
        self.own(2, self.above).start()
        if self.halves is None:
            self.own(3, self.across).start()
        self.keep().start()

    def arrive(self, slot, place):
        self.pair(self.full(shard_of(place)), slot, self.twin).wait_recv()

    def relay(self):
        if self.halves is None:
            for slot, place in ((1, self.beside), (2, self.above), (3, self.across)):
                self.arrive(slot, place)
                self.pair(self.full(shard_of(place)), slot + 3, self.twin).start()
            return
        self.arrive(1, self.beside)
        self.pair(self.halves(shard_of(self.beside), 1), 7, self.above).start()
        self.pair(self.full(shard_of(self.beside)), 4, self.twin).start()
        self.arrive(2, self.above)
        self.pair(self.halves(shard_of(self.above), 0), 3, self.beside).start()
        self.pair(self.full(shard_of(self.above)), 5, self.twin).start()

    def relay_rest(self):
        shard = shard_of(self.across)
        for slot, half in ((3, 0), (7, 1)):
            view = self.halves(shard, half)
            self.pair(view, slot, self.twin).wait_recv()
            self.pair(view, 6 if half == 0 else 8, self.twin).start()

    def finish(self):
        self.keep().wait()
        ctx, seq, wsh = self.twin
        over = (1 - seq // 2) * 2 + seq % 2
        self.arrive(0, self.twin)
        self.arrive(4, (ctx, over, wsh))
        self.arrive(5, (ctx, seq, 1 - wsh))
        rest = shard_of((ctx, over, 1 - wsh))
        if self.halves is None:
            self.pair(self.full(rest), 6, self.twin).wait_recv()
        else:
            self.pair(self.halves(rest, 0), 6, self.twin).wait_recv()
            self.pair(self.halves(rest, 1), 8, self.twin).wait_recv()

    def drain(self):
        self.own(0, self.twin).wait_send()
        self.own(1, self.beside).wait_send()
        self.own(2, self.above).wait_send()
        beside, above, across = (shard_of(p) for p in (self.beside, self.above, self.across))
        self.pair(self.full(beside), 4, self.twin).wait_send()
        self.pair(self.full(above), 5, self.twin).wait_send()
        if self.halves is None:
            self.own(3, self.across).wait_send()
            self.pair(self.full(across), 6, self.twin).wait_send()
        else:
            self.pair(self.halves(above, 0), 3, self.beside).wait_send()
            self.pair(self.halves(beside, 1), 7, self.above).wait_send()
            self.pair(self.halves(across, 0), 6, self.twin).wait_send()
            self.pair(self.halves(across, 1), 8, self.twin).wait_send()


class LineGather:
    def __init__(self, length, blocks, send, recv):
        self.length, self.blocks, self.send, self.recv = length, blocks, send, recv
        self.me = places()[0]

    def hop(self, block, way, step, device):
        view = self.blocks(block)
        return remote(view, view, self.send.at[way, step], self.recv.at[way, step], device)

    def ways(self, step):
        ctx = self.me[0]
        left = (ctx - 1, self.me[1], self.me[2])
        right = (ctx + 1, self.me[1], self.me[2])
        return (
            (0, ctx - step, ctx - step >= 0, right, ctx + 1 < self.length),
            (1, ctx + step, ctx + step < self.length, left, ctx - 1 >= 0),
        )

    def start(self):
        for way, block, unused, device, there in self.ways(0):
            pl.when(there)(lambda b=block, w=way, d=device: self.hop(b, w, 0, d).start())

    def relay(self, step):
        for way, block, come, device, there in self.ways(step):

            def pass_on(way=way, block=block, device=device, there=there):
                self.hop(block, way, step - 1, device).wait_recv()
                if step < self.length - 1:
                    pl.when(there)(lambda: self.hop(block, way, step, device).start())

            pl.when(come)(pass_on)

    def drain(self):
        for step in range(self.length - 1):
            for way, block, come, device, there in self.ways(step):
                pl.when(jnp.logical_and(come, there))(
                    lambda b=block, w=way, d=device, s=step: self.hop(b, w, s, d).wait_send()
                )


def direct_send(view, send, recv, length):
    me = places()[0]
    return [
        remote(view, view, send.at[step - 1], recv.at[step - 1], moved(me, step, length))
        for step in range(1, length)
    ]


def direct_wait(view_of, send, recv, length):
    me = places()[0]
    for step in range(1, length):
        source = moved(me, length - step, length)
        view = view_of(source[0])
        remote(view, view, send.at[step - 1], recv.at[step - 1], source).wait_recv()


def lanes_of(shape):
    return lax.broadcasted_iota(jnp.int32, shape, 1)


def rows_of(shape):
    return lax.broadcasted_iota(jnp.int32, shape, 0)


def product(left, right, dims=((1,), (0,))):
    return lax.dot_general(left, right, (dims, ((), ())), preferred_element_type=jnp.float32)


def gelu_parts(values):
    near = jnp.abs(values) * KEEP
    turn = 1.0 / (1.0 + ERF_P * near)
    bell = jnp.exp(-near * near)
    series = ERF_A[4]
    for term in ERF_A[3::-1]:
        series = series * turn + term
    tail = 0.5 * series * turn * bell
    share = jnp.where(values >= 0, 1.0 - tail, tail)
    return values * share, share + values * bell * SPREAD


def forward_kernel(
    length,
    states,
    cotangent,
    head_ids,
    route_ids,
    pack,
    query_part,
    project_part,
    inner_part,
    outer_part,
    slot_rows,
    active,
    slope,
    result,
    slot_cot,
    inner,
    outer,
    query,
    project,
    packed,
    acted,
    mixture,
    queries,
    heads,
    keyval,
    head_gates,
    middle,
    entering,
    cots,
    routes,
    scores_back,
    small,
    normal,
    score_sent,
    plane_send,
    plane_recv,
    plane_local,
    line_send,
    line_recv,
    direct_sems,
    direct_recvs,
):
    f32, bf16 = jnp.float32, jnp.bfloat16
    tokens = states.shape[0]
    me, twin, beside, above, across = places()
    ctx = me[0]
    experts = EXP_DEV * length
    peers = [twin, beside, above, across] + [moved(me, k, length) for k in range(1, length)]
    barrier = pltpu.get_barrier_semaphore()
    for peer in peers:
        pl.semaphore_signal(barrier, inc=1, device_id=peer, device_id_type=MESH)

    def gather(index, shard, full, halves=None):
        return PlaneGather(
            shard, full, halves, plane_send.at[index], plane_recv.at[index], plane_local.at[index]
        )

    def rows_view(ref, rows):
        return lambda shard: ref.at[pl.ds(shard * rows, rows), :]

    pack_gather = gather(0, pack, rows_view(packed, 64))
    query_gather = gather(1, query_part, rows_view(query, 64))
    project_gather = gather(2, project_part, rows_view(project, 192))
    inner_gather = gather(
        3,
        inner_part,
        lambda shard: inner.at[:, pl.ds(shard * 64, 64), :],
        lambda shard, half: inner.at[half, pl.ds(shard * 64, 64), :],
    )
    outer_gather = gather(
        4,
        outer_part,
        lambda shard: outer.at[:, pl.ds(shard * 256, 256), :],
        lambda shard, half: outer.at[half, pl.ds(shard * 256, 256), :],
    )
    cot_gather = LineGather(length, lambda b: cots.at[b], line_send.at[0], line_recv.at[0])
    entering_gather = LineGather(length, lambda b: entering.at[b], line_send.at[1], line_recv.at[1])

    def keyval_view(block):
        return keyval.at[pl.ds(block * tokens, tokens), :]

    cots[ctx] = cotangent[...].astype(bf16)
    pl.semaphore_wait(barrier, len(peers))
    pack_gather.start()
    query_gather.start()
    cot_gather.start()

    values = states[...].astype(f32)
    centred = values - jnp.mean(values, -1, keepdims=True)
    inverse = lax.rsqrt(jnp.mean(centred * centred, -1, keepdims=True) + EPS)
    normal[...] = centred * inverse

    lane = lanes_of((tokens, 128))
    ids = route_ids[...].astype(f32)
    both = jnp.where(lane == 0, ids[:, 0:1], ids[:, 1:2])
    turned = jnp.transpose(both)[0:8]
    expert_row = rows_of((8, tokens)).astype(f32)
    picked = jnp.logical_or(expert_row == turned[0:1], expert_row == turned[1:2])
    marks = jnp.concatenate([picked.astype(f32), jnp.zeros((8, tokens), f32)], 0).astype(bf16)
    earlier = (rows_of((tokens, tokens)) < lanes_of((tokens, tokens))).astype(f32).astype(bf16)
    ranks = product(marks, earlier)[0:8]
    routes[ctx, 0:8, :] = jnp.where(picked, ranks, -1.0)

    pack_gather.relay()
    pack_gather.finish()
    small[...] = jnp.transpose(packed[:, 128:256].astype(f32))
    shaped = (normal[...] * small[32:33, :] + small[33:34, :]).astype(bf16)
    acted[...] = shaped
    sides = product(shaped, packed[...])
    keyval_view(ctx)[...] = sides[:, 0:128].astype(bf16)
    keyval_sends = direct_send(keyval_view(ctx), direct_sems.at[0], direct_recvs.at[0], length)
    for copy in keyval_sends:
        copy.start()

    id_lanes = [head_ids[:, j : j + 1] for j in range(MOA_TOP)]
    logits = [
        jnp.sum(jnp.where(lane == id_lanes[j], sides[:, 128:256], 0.0), -1, keepdims=True)
        for j in range(MOA_TOP)
    ]
    peak = jnp.maximum(jnp.maximum(logits[0], logits[1]), jnp.maximum(logits[2], logits[3]))
    powers = [jnp.exp(item - peak) for item in logits]
    total = powers[0] + powers[1] + powers[2] + powers[3]
    gates = [item / total for item in powers]
    head_gates[...] = jnp.where(
        lane == 0,
        gates[0],
        jnp.where(lane == 1, gates[1], jnp.where(lane == 2, gates[2], gates[3])),
    )

    query_gather.relay()
    project_gather.start()
    inner_gather.start()
    query_gather.finish()
    for part in range(6):
        columns = slice(part * 256, part * 256 + 256)
        mixture[:, columns] = product(acted[...], query[:, columns]).astype(bf16)
    cot_gather.relay(1)

    low_half = lane < HS
    side = lane // HS
    for j in range(MOA_TOP):
        wanted = id_lanes[j] - side
        chosen = jnp.zeros((tokens, 128), f32)
        for pair in range(MOA_EXPERTS // 2):
            block = mixture[:, pair * 128 : pair * 128 + 128].astype(f32)
            chosen = chosen + jnp.where(wanted == 2 * pair, block, 0.0)
        folded = chosen + pltpu.roll(chosen, HS, 1)
        queries[j * tokens : (j + 1) * tokens, :] = (
            jnp.where(low_half, folded, 0.0) * HS ** (-0.5)
        ).astype(bf16)

    direct_wait(keyval_view, direct_sems.at[0], direct_recvs.at[0], length)
    chunk = 256

    def attend(turn, carried):
        rows = pl.ds(pl.multiple_of(turn * chunk, chunk), chunk)
        scores = product(queries[rows, :], keyval[...], ((1,), (1,)))
        top = jnp.max(scores, -1, keepdims=True)
        weights = jnp.exp(scores - top)
        mass = jnp.sum(weights, -1, keepdims=True)
        seen = product(weights.astype(bf16), keyval[...]) / mass
        heads[rows, :] = jnp.where(lanes_of((chunk, 128)) < HS, top + jnp.log(mass), seen)
        return carried

    lax.fori_loop(0, MOA_TOP * tokens // chunk, attend, 0)
    project_gather.relay()

    spread = []
    for j in range(MOA_TOP):
        head = heads[j * tokens : (j + 1) * tokens, :]
        both = jnp.where(low_half, pltpu.roll(head, HS, 1), head)
        spread.append(both * head_gates[:, j : j + 1])
    for pair in range(MOA_EXPERTS // 2):
        block = jnp.zeros((tokens, 128), f32)
        for j in range(MOA_TOP):
            block = jnp.where(id_lanes[j] - side == 2 * pair, spread[j], block)
        mixture[:, pair * 128 : pair * 128 + 128] = block.astype(bf16)

    project_gather.finish()
    between = states[...].astype(f32) + product(mixture[...], project[...])
    middle[...] = between
    centred = between - jnp.mean(between, -1, keepdims=True)
    inverse = lax.rsqrt(jnp.mean(centred * centred, -1, keepdims=True) + EPS)
    entry = (centred * inverse * small[34:35, :] + small[35:36, :]).astype(bf16)
    entering[ctx] = entry
    entering_gather.start()
    logits = product(small[16:32, :].astype(bf16), entry, ((1,), (1,)))[8:16]
    peak = jnp.max(jnp.where(picked, logits, -1e30), 0, keepdims=True)
    powers = jnp.where(picked, jnp.exp(jnp.where(picked, logits - peak, 0.0)), 0.0)
    routes[ctx, 8:16, :] = powers / jnp.sum(powers, 0, keepdims=True)
    route_sends = direct_send(routes.at[ctx], direct_sems.at[1], direct_recvs.at[1], length)
    for copy in route_sends:
        copy.start()

    def selection(source, expert):
        row = routes[source, pl.ds(EXP_DEV * ctx + expert, 1), :]
        return rows_of((CAP, tokens)).astype(f32) == row

    def slots(source):
        return pl.ds(pl.multiple_of(source * CAP, CAP), CAP)

    def first_half(source):
        def one(expert, carried):
            chosen = selection(source, expert).astype(f32).astype(bf16)
            rows = product(chosen, entering[source]).astype(bf16)
            slot_rows[expert, slots(source), :] = rows

            def part(index, kept):
                columns = pl.ds(pl.multiple_of(index * 512, 512), 512)
                before = product(rows, inner[expert, :, columns])
                value, gradient = gelu_parts(before)
                active[expert, slots(source), columns] = value.astype(bf16)
                slope[expert, slots(source), columns] = gradient.astype(bf16)
                return kept

            return lax.fori_loop(0, 4, part, carried)

        lax.fori_loop(0, EXP_DEV, one, 0)

    inner_gather.relay()
    outer_gather.start()
    direct_wait(lambda b: routes.at[b], direct_sems.at[1], direct_recvs.at[1], length)
    entering_gather.relay(1)
    inner_gather.relay_rest()
    inner_gather.finish()

    def step_of(step, carried):
        for ahead in range(2, length):

            @pl.when(step == ahead - 1)
            def _():
                entering_gather.relay(ahead)
                if ahead < length - 1:
                    pass

        @pl.when(step == length - 2)
        def _():
            cot_gather.relay(2)

        @pl.when(step == length - 1)
        def _():
            outer_gather.relay()

        before_me = ctx - step >= 0
        after_me = jnp.logical_and(ctx + step < length, step > 0)
        count = before_me.astype(jnp.int32) + after_me.astype(jnp.int32)

        def visit(turn, kept):
            source = jnp.where(jnp.logical_and(turn == 0, before_me), ctx - step, ctx + step)
            first_half(source)
            return kept

        lax.fori_loop(0, count, visit, 0)
        return carried

    lax.fori_loop(0, length, step_of, 0)
    outer_gather.relay_rest()
    cot_gather.relay(length - 1)
    outer_gather.finish()

    def second_half(turn, carried):
        expert, part = turn // 2, turn % 2
        rows = pl.ds(pl.multiple_of(part * 384, 384), 384)
        result[expert, rows, :] = product(active[expert, rows, :], outer[expert]).astype(bf16)
        return carried

    lax.fori_loop(0, 2 * EXP_DEV, second_half, 0)

    def score(source, carried):
        lines = []
        for expert in range(EXP_DEV):
            chosen = selection(source, expert).astype(f32)
            cot_rows = product(chosen.astype(bf16), cots[source]).astype(bf16)
            slot_cot[expert, slots(source), :] = cot_rows
            rows = result[expert, slots(source), :].astype(f32)
            toward = jnp.sum(rows * small[36:37, :], -1, keepdims=True)
            against = jnp.sum(rows * cot_rows.astype(f32), -1, keepdims=True)
            lines.append(jnp.sum(chosen * toward, 0, keepdims=True))
            lines.append(jnp.sum(chosen * against, 0, keepdims=True))
        lines.append(jnp.zeros((8 - 2 * EXP_DEV, tokens), f32))
        sheet = jnp.concatenate(lines, 0)

        @pl.when(source == ctx)
        def _():
            scores_back[ctx] = sheet

        @pl.when(source != ctx)
        def _():
            score_sent[source] = sheet
            offset = (source - ctx + length) % length
            remote(
                score_sent.at[source],
                scores_back.at[ctx],
                direct_sems.at[2, offset - 1],
                direct_recvs.at[2, offset - 1],
                (source, me[1], me[2]),
            ).start()

        return carried

    lax.fori_loop(0, length, score, 0)
    direct_wait(lambda b: scores_back.at[b], direct_sems.at[2], direct_recvs.at[2], length)
    for step in range(1, length):
        target = moved(me, step, length)
        remote(
            score_sent.at[target[0]],
            scores_back.at[ctx],
            direct_sems.at[2, step - 1],
            direct_recvs.at[2, step - 1],
            target,
        ).wait_send()
    for copy in keyval_sends + route_sends:
        copy.wait_send()
    for item in (pack_gather, query_gather, project_gather, inner_gather, outer_gather):
        item.drain()
    cot_gather.drain()
    entering_gather.drain()


def fast_forward(length, states, cotangent, head_ids, route_ids, pack, query, project, inner, outer):
    f32, bf16 = jnp.float32, jnp.bfloat16
    tokens = states.shape[0]
    rows = length * CAP
    shape = jax.ShapeDtypeStruct
    in_vmem = pl.BlockSpec(memory_space=pltpu.VMEM)
    in_place = pl.BlockSpec(memory_space=pl.ANY)
    outs = (
        shape((EXP_DEV, rows, D), bf16),
        shape((EXP_DEV, rows, FF), bf16),
        shape((EXP_DEV, rows, FF), bf16),
        shape((EXP_DEV, rows, D), bf16),
        shape((EXP_DEV, rows, D), bf16),
        shape((EXP_DEV, D, FF), bf16),
        shape((EXP_DEV, FF, D), bf16),
        shape((D, MOA_EXPERTS * HS), bf16),
        shape((MOA_EXPERTS * HS, D), bf16),
        shape((D, 256), bf16),
        shape((tokens, D), bf16),
        shape((tokens, MOA_EXPERTS * HS), bf16),
        shape((MOA_TOP * tokens, 128), bf16),
        shape((MOA_TOP * tokens, 128), f32),
        shape((length * tokens, 128), bf16),
        shape((tokens, 128), f32),
        shape((tokens, D), f32),
        shape((length, tokens, D), bf16),
        shape((length, tokens, D), bf16),
        shape((length, 16, tokens), f32),
        shape((length, 8, tokens), f32),
        shape((128, D), f32),
    )
    dma = pltpu.SemaphoreType.DMA
    return pl.pallas_call(
        partial(forward_kernel, length),
        out_shape=outs,
        in_specs=[in_vmem] * 5 + [in_place] * 4,
        out_specs=[in_vmem] * len(outs),
        scratch_shapes=[
            pltpu.VMEM((tokens, D), f32),
            pltpu.VMEM((length, 8, tokens), f32),
            dma((5, 9)),
            dma((5, 9)),
            dma((5,)),
            dma((2, 2, length)),
            dma((2, 2, length)),
            dma((3, length)),
            dma((3, length)),
        ],
        compiler_params=pltpu.CompilerParams(
            collective_id=0, has_side_effects=True, vmem_limit_bytes=60 * 2**20
        ),
        name="forward",
    )(states, cotangent, head_ids, route_ids, pack, query, project, inner, outer)


def fast_body(
    states,
    remaining,
    moa_ids,
    ffn_ids,
    out_cotangent,
    left_cotangent,
    query_weight,
    keyval_weight,
    project_weight,
    chooser,
    selector,
    gain_one,
    bias_one,
    gain_two,
    bias_two,
    halt_weight,
    expert_in,
    expert_out,
):
    tokens = states.shape[1]
    devices = lax.axis_size("ctx")
    experts = EXP_DEV * devices
    capacity = max(2, (4 * tokens + experts - 1) // experts)
    rows_total = tokens * MOA_TOP
    scaling = HS ** (-0.5)
    f32 = jnp.float32
    bf16 = jnp.bfloat16
    flat = jnp.stack([gain_one, bias_one, gain_two, bias_two, halt_weight], 1)
    pack = jnp.concatenate(
        [keyval_weight, chooser, selector, flat, jnp.zeros((flat.shape[0], 91), bf16)], 1
    )
    (
        arrived_flat,
        activated_flat,
        slope_flat,
        result_flat,
        unused_cot,
        inner_full,
        outer_full,
        query_full,
        project_full,
        packed,
        acted,
        mixture,
        queries_flat,
        heads_flat,
        shard_rows,
        gate_lanes,
        middle,
        entering_all,
        unused_cots,
        routes,
        unused_scores,
        small,
    ) = fast_forward(
        devices, states[0], out_cotangent[0], moa_ids[0], ffn_ids[0],
        pack, query_weight, project_weight, expert_in, expert_out,
    )
    spot = lax.axis_index("ctx")
    keyval_full = packed[:, :128]
    chooser_full = packed[:, 128:152]
    selector_full = packed[:, 152:160]
    gainone_full, biasone_full, gaintwo_full, biastwo_full, halt_full = (small[32 + i] for i in range(5))
    gain_first = gainone_full.astype(f32)
    gain_second = gaintwo_full.astype(f32)
    halt_vector = halt_full.astype(f32)
    resident = states[0].astype(f32)
    normed_one, normal_one, inverse_one = layer_norm(resident, gain_first, biasone_full.astype(f32))
    head_ids = moa_ids[0]
    query_sel = (
        (queries_flat[:, :HS] * 8.0).reshape(MOA_TOP, tokens, HS).swapaxes(0, 1).reshape(rows_total, HS)
    )
    keyval = lax.dynamic_slice_in_dim(shard_rows, spot * tokens, tokens, 0)
    chosen = one_hot(head_ids, MOA_EXPERTS)
    head_gates = gate_lanes[:, :MOA_TOP]
    heads_view = heads_flat[:, HS:].reshape(MOA_TOP, tokens, HS).swapaxes(0, 1)
    heads_out = heads_view.reshape(rows_total, HS)
    log_total = heads_flat[:, 0].reshape(MOA_TOP, tokens).T.reshape(rows_total)
    chosen_low = chosen.astype(bf16)
    normed_two, normal_two, inverse_two = layer_norm(middle, gain_second, biastwo_full.astype(f32))
    entering = lax.dynamic_index_in_dim(entering_all, spot, 0, False)
    own = lax.dynamic_index_in_dim(routes, spot, 0, False)
    route_ids = ffn_ids[0]
    picked = one_hot(route_ids, experts)
    expert_gates = jnp.sum(picked * own[8:16].T[:, None, :], -1)
    slots = jnp.sum(picked * own[0:8].T[:, None, :], -1).astype(jnp.int32)
    target = (route_ids * capacity + slots).reshape(-1)

    def by_source(flat):
        return flat.reshape(EXP_DEV, devices, capacity, flat.shape[-1]).swapaxes(0, 1)

    arrived_rows = by_source(arrived_flat)
    activated = by_source(activated_flat)
    slope = by_source(slope_flat)
    result_rows = by_source(result_flat)
    returned = lax.all_to_all(result_rows, "ctx", split_axis=0, concat_axis=0, tiled=True).reshape(
        experts * capacity, D
    )
    expert_rows = returned[target].reshape(tokens, FFN_TOP, D).astype(f32)
    final = middle + jnp.sum(expert_gates[:, :, None] * expert_rows, 1)
    halting = jax.nn.sigmoid(jnp.dot(final, halt_vector, precision=HIGH))
    left_mass = remaining[0]
    stopped = left_mass * halting
    new_states = (stopped[:, None] * resident + (1.0 - stopped)[:, None] * final).astype(bf16)
    remaining_next = left_mass * (1.0 - halting)
    out_grad = out_cotangent[0]
    left_grad = left_cotangent[0]
    stop_grad = jnp.sum(out_grad * (resident - final), -1)
    grad_remaining = stop_grad * halting + left_grad * (1.0 - halting)
    halt_logit_grad = (stop_grad - left_grad) * left_mass * halting * (1.0 - halting)
    grad_halt = jnp.sum(halt_logit_grad[:, None] * final, 0)
    grad_final = (1.0 - stopped)[:, None] * out_grad + halt_logit_grad[:, None] * halt_vector
    gate_grad = jnp.sum(grad_final[:, None, :] * expert_rows, -1)
    selector_logit_grad = jnp.sum(choose_back(expert_gates, gate_grad)[:, :, None] * picked, 1)
    entering_wide = entering.astype(f32)
    grad_selector = jnp.dot(entering_wide.T, selector_logit_grad, precision=HIGH)
    rows_grad = (expert_gates[:, :, None] * grad_final[:, None, :]).astype(bf16).reshape(-1, D)
    grad_outgoing = (
        jnp.zeros((experts * capacity, D), bf16)
        .at[target]
        .set(rows_grad)
        .reshape(devices, EXP_DEV, capacity, D)
    )
    grad_arrived = lax.all_to_all(grad_outgoing, "ctx", split_axis=0, concat_axis=0, tiled=True)
    grad_activated = jnp.einsum(
        "nekd,efd->nekf", grad_arrived, outer_full, preferred_element_type=f32
    )
    before_grad = (grad_activated * slope.astype(f32)).astype(bf16)
    outer_grad = jnp.einsum(
        "nekf,nekd->efd", activated, grad_arrived, preferred_element_type=f32
    )
    inner_grad = jnp.einsum("nekd,nekf->edf", arrived_rows, before_grad, preferred_element_type=f32)
    grad_sent = jnp.einsum(
        "nekf,edf->nekd", before_grad, inner_full, preferred_element_type=f32
    ).astype(bf16)
    grad_back = lax.all_to_all(grad_sent, "ctx", split_axis=0, concat_axis=0, tiled=True).reshape(
        experts * capacity, D
    )
    entering_grad = jnp.sum(grad_back[target].reshape(tokens, FFN_TOP, D).astype(f32), 1)
    entering_grad = entering_grad + jnp.dot(
        selector_logit_grad, selector_full.astype(f32).T, precision=HIGH
    )
    middle_extra, grad_gain_two, grad_bias_two = norm_back(
        entering_grad, normal_two, inverse_two, gain_second
    )
    middle_grad = grad_final + middle_extra
    attn_grad = middle_grad.astype(bf16)
    grad_project = jnp.dot(mixture.T, attn_grad, preferred_element_type=f32)
    mix_grad = jnp.dot(attn_grad, project_full.T, preferred_element_type=f32).reshape(
        tokens, MOA_EXPERTS, HS
    )
    mix_sel_grad = jnp.take_along_axis(mix_grad, head_ids[:, :, None], axis=1)
    head_gate_grad = jnp.sum(mix_sel_grad * heads_view, -1)
    chooser_logit_grad = jnp.sum(choose_back(head_gates, head_gate_grad)[:, :, None] * chosen, 1)
    acted_wide = acted.astype(f32)
    grad_chooser = jnp.dot(acted_wide.T, chooser_logit_grad, precision=HIGH)
    acted_grad = jnp.dot(chooser_logit_grad, chooser_full.astype(f32).T, precision=HIGH)
    heads_grad = (head_gates[:, :, None] * mix_sel_grad).astype(bf16).reshape(rows_total, HS)
    row_delta = jnp.sum(heads_grad.astype(f32) * heads_out, -1)

    def cycle_turn(turn_index, carried):
        visiting, grads_visiting, query_grad = carried
        block_size = block_rows(tokens)

        def per_block(query_acc, key_block):
            scores = jnp.dot(query_sel, key_block[:, :HS].T, preferred_element_type=f32) * scaling
            probability = jnp.exp(scores - log_total[:, None])
            prob_grad = jnp.dot(heads_grad, key_block[:, HS:].T, preferred_element_type=f32)
            score_grad = (probability * (prob_grad - row_delta[:, None])).astype(bf16)
            query_acc = (
                query_acc
                + jnp.dot(score_grad, key_block[:, :HS], preferred_element_type=f32) * scaling
            )
            keys_grad = jnp.dot(score_grad.T, query_sel, preferred_element_type=f32) * scaling
            values_grad = jnp.dot(
                probability.astype(bf16).T, heads_grad, preferred_element_type=f32
            )
            return (query_acc, jnp.concatenate([keys_grad, values_grad], -1))

        query_grad, block_grads = lax.scan(
            per_block, query_grad, visiting.reshape(tokens // block_size, block_size, 2 * HS)
        )
        grads_visiting = grads_visiting + block_grads.reshape(tokens, 2 * HS)
        visiting = shifted(visiting, "ctx", 1)
        grads_visiting = shifted(grads_visiting.astype(jnp.bfloat16), "ctx", 1).astype(
            grads_visiting.dtype
        )
        return (visiting, grads_visiting, query_grad)

    cycle_state = (keyval, jnp.zeros((tokens, 2 * HS), f32), jnp.zeros((rows_total, HS), f32))
    unused_keys, keyval_grad, query_grad = lax.fori_loop(0, devices, cycle_turn, cycle_state)
    query_sel_grad = query_grad.astype(bf16).reshape(tokens, MOA_TOP, HS)
    query_all_grad = jnp.sum(chosen_low[:, :, :, None] * query_sel_grad[:, :, None, :], 1).reshape(
        tokens, MOA_EXPERTS * HS
    )
    keyval_low = keyval_grad.astype(bf16)
    grad_query = jnp.dot(acted.T, query_all_grad, preferred_element_type=f32)
    grad_keyval = jnp.dot(acted.T, keyval_low, preferred_element_type=f32)
    acted_grad = acted_grad + jnp.dot(query_all_grad, query_full.T, preferred_element_type=f32)
    acted_grad = acted_grad + jnp.dot(keyval_low, keyval_full.T, preferred_element_type=f32)
    resident_grad, grad_gain_one, grad_bias_one = norm_back(
        acted_grad, normal_one, inverse_one, gain_first
    )
    grad_states = middle_grad + resident_grad + stopped[:, None] * out_grad
    dense_grads = (
        grad_query,
        grad_keyval,
        grad_project,
        grad_chooser,
        grad_selector,
        grad_gain_one,
        grad_bias_one,
        grad_gain_two,
        grad_bias_two,
        grad_halt,
    )
    totals = (
        lax.psum(dense_grads[0].astype(jnp.bfloat16), "ctx").astype(jnp.float32),
        lax.psum(dense_grads[1].astype(jnp.bfloat16), "ctx").astype(jnp.float32),
        lax.psum(dense_grads[2].astype(jnp.bfloat16), "ctx").astype(jnp.float32),
        lax.psum(dense_grads[3].astype(jnp.bfloat16), "ctx").astype(jnp.float32),
        lax.psum(dense_grads[4].astype(jnp.bfloat16), "ctx").astype(jnp.float32),
        lax.psum(dense_grads[5].astype(jnp.bfloat16), "ctx").astype(jnp.float32),
        lax.psum(dense_grads[6].astype(jnp.bfloat16), "ctx").astype(jnp.float32),
        lax.psum(dense_grads[7].astype(jnp.bfloat16), "ctx").astype(jnp.float32),
        lax.psum(dense_grads[8].astype(jnp.bfloat16), "ctx").astype(jnp.float32),
        lax.psum(dense_grads[9].astype(jnp.bfloat16), "ctx").astype(jnp.float32),
    )
    shards = (
        lax.psum_scatter(
            totals[0].astype(jnp.bfloat16), ("seq", "wsh"), scatter_dimension=0, tiled=True
        ).astype(jnp.float32),
        lax.psum_scatter(
            totals[1].astype(jnp.bfloat16), ("seq", "wsh"), scatter_dimension=0, tiled=True
        ).astype(jnp.float32),
        lax.psum_scatter(
            totals[2].astype(jnp.bfloat16), ("seq", "wsh"), scatter_dimension=0, tiled=True
        ).astype(jnp.float32),
        lax.psum_scatter(
            totals[3].astype(jnp.bfloat16), ("seq", "wsh"), scatter_dimension=0, tiled=True
        ).astype(jnp.float32),
        lax.psum_scatter(
            totals[4].astype(jnp.bfloat16), ("seq", "wsh"), scatter_dimension=0, tiled=True
        ).astype(jnp.float32),
        lax.psum_scatter(
            totals[5].astype(jnp.bfloat16), ("seq", "wsh"), scatter_dimension=0, tiled=True
        ).astype(jnp.float32),
        lax.psum_scatter(
            totals[6].astype(jnp.bfloat16), ("seq", "wsh"), scatter_dimension=0, tiled=True
        ).astype(jnp.float32),
        lax.psum_scatter(
            totals[7].astype(jnp.bfloat16), ("seq", "wsh"), scatter_dimension=0, tiled=True
        ).astype(jnp.float32),
        lax.psum_scatter(
            totals[8].astype(jnp.bfloat16), ("seq", "wsh"), scatter_dimension=0, tiled=True
        ).astype(jnp.float32),
        lax.psum_scatter(
            totals[9].astype(jnp.bfloat16), ("seq", "wsh"), scatter_dimension=0, tiled=True
        ).astype(jnp.float32),
    )
    inner_shard, outer_shard = (
        lax.psum_scatter(
            inner_grad.astype(jnp.bfloat16), ("seq", "wsh"), scatter_dimension=1, tiled=True
        ).astype(jnp.float32),
        lax.psum_scatter(
            outer_grad.astype(jnp.bfloat16), ("seq", "wsh"), scatter_dimension=1, tiled=True
        ).astype(jnp.float32),
    )
    return (
        new_states[None],
        remaining_next[None],
        grad_states[None],
        grad_remaining[None],
        shards[0],
        shards[1],
        shards[2],
        shards[3],
        shards[4],
        shards[5],
        shards[6],
        shards[7],
        shards[8],
        shards[9],
        inner_shard,
        outer_shard,
    )


def solution(mesh):
    in_specs = (
        P(("seq", "wsh"), "ctx", None),
        P(("seq", "wsh"), "ctx"),
        P(("seq", "wsh"), "ctx", None),
        P(("seq", "wsh"), "ctx", None),
        P(("seq", "wsh"), "ctx", None),
        P(("seq", "wsh"), "ctx"),
        P(("seq", "wsh"), None),
        P(("seq", "wsh"), None),
        P(("seq", "wsh"), None),
        P(("seq", "wsh"), None),
        P(("seq", "wsh"), None),
        P(("seq", "wsh")),
        P(("seq", "wsh")),
        P(("seq", "wsh")),
        P(("seq", "wsh")),
        P(("seq", "wsh")),
        P("ctx", ("seq", "wsh"), None),
        P("ctx", ("seq", "wsh"), None),
    )
    out_specs = (
        P(("seq", "wsh"), "ctx", None),
        P(("seq", "wsh"), "ctx"),
        P(("seq", "wsh"), "ctx", None),
        P(("seq", "wsh"), "ctx"),
        P(("seq", "wsh"), None),
        P(("seq", "wsh"), None),
        P(("seq", "wsh"), None),
        P(("seq", "wsh"), None),
        P(("seq", "wsh"), None),
        P(("seq", "wsh")),
        P(("seq", "wsh")),
        P(("seq", "wsh")),
        P(("seq", "wsh")),
        P(("seq", "wsh")),
        P("ctx", ("seq", "wsh"), None),
        P("ctx", ("seq", "wsh"), None),
    )
    body = fast_body if mesh.shape["ctx"] == 4 else general_body
    return jax.shard_map(body, mesh=mesh, in_specs=in_specs, out_specs=out_specs, check_vma=False)
```

```python
from functools import partial
from types import SimpleNamespace

import jax
import jax.numpy as jnp
from jax import lax
from jax.experimental import pallas as pl
from jax.experimental.pallas import tpu as pltpu
from jax.sharding import PartitionSpec as P

D = 512
HS = 64
MOA_EXPERTS = 24
MOA_TOP = 4
EXP_DEV = 2
FFN_TOP = 2
FF = 2048


EPS = 1e-05
HIGH = lax.Precision.HIGHEST


def shifted(x, axis, by):
    length = lax.axis_size(axis)
    return lax.ppermute(x, axis, [(i, (i + by) % length) for i in range(length)])


def layer_norm(values, gain, bias):
    centred = values - jnp.mean(values, -1, keepdims=True)
    inverse = lax.rsqrt(jnp.mean(centred * centred, -1, keepdims=True) + EPS)
    normal = centred * inverse
    return (normal * gain + bias, normal, inverse)


def norm_back(incoming, normal, inverse, gain):
    scaled = incoming * gain
    inner_term = (
        scaled
        - jnp.mean(scaled, -1, keepdims=True)
        - normal * jnp.mean(scaled * normal, -1, keepdims=True)
    )
    return (inverse * inner_term, jnp.sum(incoming * normal, 0), jnp.sum(incoming, 0))


def one_hot(index, count):
    return (index[..., None] == jnp.arange(count, dtype=jnp.int32)).astype(jnp.float32)


def choose_back(gates, upstream):
    return gates * (upstream - jnp.sum(gates * upstream, -1, keepdims=True))


def block_rows(row_count):
    if row_count > 512 and row_count % 512 == 0:
        return 512
    return row_count


def expert_slots(route_ids, experts):
    flat_ids = route_ids.reshape(-1)
    table = (flat_ids[:, None] == jnp.arange(experts, dtype=jnp.int32)[None, :]).astype(jnp.float32)
    place = jnp.arange(flat_ids.shape[0], dtype=jnp.int32)
    before = (place[None, :] < place[:, None]).astype(jnp.bfloat16)
    earlier = jnp.dot(before, table.astype(jnp.bfloat16), preferred_element_type=jnp.float32)
    return jnp.sum(earlier * table, 1).astype(jnp.int32).reshape(route_ids.shape)


def general_body(
    states,
    remaining,
    moa_ids,
    ffn_ids,
    out_cotangent,
    left_cotangent,
    query_weight,
    keyval_weight,
    project_weight,
    chooser,
    selector,
    gain_one,
    bias_one,
    gain_two,
    bias_two,
    halt_weight,
    expert_in,
    expert_out,
):
    tokens = states.shape[1]
    devices = lax.axis_size("ctx")
    experts = EXP_DEV * devices
    capacity = max(2, (4 * tokens + experts - 1) // experts)
    rows_total = tokens * MOA_TOP
    scaling = HS ** (-0.5)
    f32 = jnp.float32
    bf16 = jnp.bfloat16
    (
        query_full,
        keyval_full,
        project_full,
        chooser_full,
        selector_full,
        gainone_full,
        biasone_full,
        gaintwo_full,
        biastwo_full,
        halt_full,
    ) = (
        lax.all_gather(query_weight, ("seq", "wsh"), axis=0, tiled=True),
        lax.all_gather(keyval_weight, ("seq", "wsh"), axis=0, tiled=True),
        lax.all_gather(project_weight, ("seq", "wsh"), axis=0, tiled=True),
        lax.all_gather(chooser, ("seq", "wsh"), axis=0, tiled=True),
        lax.all_gather(selector, ("seq", "wsh"), axis=0, tiled=True),
        lax.all_gather(gain_one, ("seq", "wsh"), axis=0, tiled=True),
        lax.all_gather(bias_one, ("seq", "wsh"), axis=0, tiled=True),
        lax.all_gather(gain_two, ("seq", "wsh"), axis=0, tiled=True),
        lax.all_gather(bias_two, ("seq", "wsh"), axis=0, tiled=True),
        lax.all_gather(halt_weight, ("seq", "wsh"), axis=0, tiled=True),
    )
    inner_full, outer_full = (
        lax.all_gather(expert_in, ("seq", "wsh"), axis=1, tiled=True),
        lax.all_gather(expert_out, ("seq", "wsh"), axis=1, tiled=True),
    )
    gain_first = gainone_full.astype(f32)
    gain_second = gaintwo_full.astype(f32)
    halt_vector = halt_full.astype(f32)
    resident = states[0].astype(f32)
    normed_one, normal_one, inverse_one = layer_norm(resident, gain_first, biasone_full.astype(f32))
    acted = normed_one.astype(bf16)
    query_all = (
        jnp.dot(acted, query_full, preferred_element_type=f32)
        .astype(bf16)
        .reshape(tokens, MOA_EXPERTS, HS)
    )
    head_ids = moa_ids[0]
    query_sel = jnp.take_along_axis(query_all, head_ids[:, :, None], axis=1).reshape(rows_total, HS)
    keyval = jnp.dot(acted, keyval_full, preferred_element_type=f32).astype(bf16)
    chosen = one_hot(head_ids, MOA_EXPERTS)
    head_logits = jnp.sum(
        chosen * jnp.dot(acted, chooser_full, preferred_element_type=f32)[:, None, :], -1
    )
    head_gates = jax.nn.softmax(head_logits, -1)
    start_state = (
        jnp.full((rows_total,), -1e30, f32),
        jnp.zeros((rows_total,), f32),
        jnp.zeros((rows_total, HS), f32),
    )
    running = start_state
    shard_rows = lax.all_gather(keyval, "ctx", axis=0, tiled=True)
    block_size = block_rows(shard_rows.shape[0])
    grouped = shard_rows.reshape(shard_rows.shape[0] // block_size, block_size, 2 * HS)

    def absorb(carried, key_block):
        row_peak, row_total, gathered = carried
        scores = jnp.dot(query_sel, key_block[:, :HS].T, preferred_element_type=f32) * scaling
        new_peak = jnp.maximum(row_peak, jnp.max(scores, -1))
        fading = jnp.exp(row_peak - new_peak)
        weights = jnp.exp(scores - new_peak[:, None])
        row_total = row_total * fading + jnp.sum(weights, -1)
        gathered = gathered * fading[:, None] + jnp.dot(
            weights.astype(bf16), key_block[:, HS:], preferred_element_type=f32
        )
        return ((new_peak, row_total, gathered), None)

    running, unused = lax.scan(absorb, running, grouped)
    row_peak, row_total, gathered = running
    heads_out = gathered / row_total[:, None]
    log_total = row_peak + jnp.log(row_total)
    heads_view = heads_out.reshape(tokens, MOA_TOP, HS)
    mixed_sel = (head_gates[:, :, None] * heads_view).astype(bf16)
    chosen_low = chosen.astype(bf16)
    mixture = jnp.sum(chosen_low[:, :, :, None] * mixed_sel[:, :, None, :], 1).reshape(
        tokens, MOA_EXPERTS * HS
    )
    middle = resident + jnp.dot(mixture, project_full, preferred_element_type=f32)
    normed_two, normal_two, inverse_two = layer_norm(middle, gain_second, biastwo_full.astype(f32))
    entering = normed_two.astype(bf16)
    route_ids = ffn_ids[0]
    picked = one_hot(route_ids, experts)
    expert_logits = jnp.sum(
        picked * jnp.dot(entering, selector_full, preferred_element_type=f32)[:, None, :], -1
    )
    expert_gates = jax.nn.softmax(expert_logits, -1)
    slots = expert_slots(route_ids, experts)
    target = (route_ids * capacity + slots).reshape(-1)
    copies = jnp.broadcast_to(entering[:, None, :], (tokens, FFN_TOP, D)).reshape(-1, D)
    outgoing = (
        jnp.zeros((experts * capacity, D), bf16)
        .at[target]
        .set(copies)
        .reshape(devices, EXP_DEV, capacity, D)
    )
    arrived_rows = lax.all_to_all(outgoing, "ctx", split_axis=0, concat_axis=0, tiled=True)
    before = jnp.einsum("nekd,edf->nekf", arrived_rows, inner_full, preferred_element_type=f32)
    activated = jax.nn.gelu(before, approximate=False).astype(bf16)
    result_rows = jnp.einsum(
        "nekf,efd->nekd", activated, outer_full, preferred_element_type=f32
    ).astype(bf16)
    returned = lax.all_to_all(result_rows, "ctx", split_axis=0, concat_axis=0, tiled=True).reshape(
        experts * capacity, D
    )
    expert_rows = returned[target].reshape(tokens, FFN_TOP, D).astype(f32)
    final = middle + jnp.sum(expert_gates[:, :, None] * expert_rows, 1)
    halting = jax.nn.sigmoid(jnp.dot(final, halt_vector, precision=HIGH))
    left_mass = remaining[0]
    stopped = left_mass * halting
    new_states = (stopped[:, None] * resident + (1.0 - stopped)[:, None] * final).astype(bf16)
    remaining_next = left_mass * (1.0 - halting)
    out_grad = out_cotangent[0]
    left_grad = left_cotangent[0]
    stop_grad = jnp.sum(out_grad * (resident - final), -1)
    grad_remaining = stop_grad * halting + left_grad * (1.0 - halting)
    halt_logit_grad = (stop_grad - left_grad) * left_mass * halting * (1.0 - halting)
    grad_halt = jnp.sum(halt_logit_grad[:, None] * final, 0)
    grad_final = (1.0 - stopped)[:, None] * out_grad + halt_logit_grad[:, None] * halt_vector
    gate_grad = jnp.sum(grad_final[:, None, :] * expert_rows, -1)
    selector_logit_grad = jnp.sum(choose_back(expert_gates, gate_grad)[:, :, None] * picked, 1)
    entering_wide = entering.astype(f32)
    grad_selector = jnp.dot(entering_wide.T, selector_logit_grad, precision=HIGH)
    rows_grad = (expert_gates[:, :, None] * grad_final[:, None, :]).astype(bf16).reshape(-1, D)
    grad_outgoing = (
        jnp.zeros((experts * capacity, D), bf16)
        .at[target]
        .set(rows_grad)
        .reshape(devices, EXP_DEV, capacity, D)
    )
    grad_arrived = lax.all_to_all(grad_outgoing, "ctx", split_axis=0, concat_axis=0, tiled=True)
    grad_activated = jnp.einsum(
        "nekd,efd->nekf", grad_arrived, outer_full, preferred_element_type=f32
    )
    activated_again, gelu_back = jax.vjp(partial(jax.nn.gelu, approximate=False), before)
    before_grad = gelu_back(grad_activated)[0].astype(bf16)
    outer_grad = jnp.einsum(
        "nekf,nekd->efd", activated_again.astype(bf16), grad_arrived, preferred_element_type=f32
    )
    inner_grad = jnp.einsum("nekd,nekf->edf", arrived_rows, before_grad, preferred_element_type=f32)
    grad_sent = jnp.einsum(
        "nekf,edf->nekd", before_grad, inner_full, preferred_element_type=f32
    ).astype(bf16)
    grad_back = lax.all_to_all(grad_sent, "ctx", split_axis=0, concat_axis=0, tiled=True).reshape(
        experts * capacity, D
    )
    entering_grad = jnp.sum(grad_back[target].reshape(tokens, FFN_TOP, D).astype(f32), 1)
    entering_grad = entering_grad + jnp.dot(
        selector_logit_grad, selector_full.astype(f32).T, precision=HIGH
    )
    middle_extra, grad_gain_two, grad_bias_two = norm_back(
        entering_grad, normal_two, inverse_two, gain_second
    )
    middle_grad = grad_final + middle_extra
    attn_grad = middle_grad.astype(bf16)
    grad_project = jnp.dot(mixture.T, attn_grad, preferred_element_type=f32)
    mix_grad = jnp.dot(attn_grad, project_full.T, preferred_element_type=f32).reshape(
        tokens, MOA_EXPERTS, HS
    )
    mix_sel_grad = jnp.take_along_axis(mix_grad, head_ids[:, :, None], axis=1)
    head_gate_grad = jnp.sum(mix_sel_grad * heads_view, -1)
    chooser_logit_grad = jnp.sum(choose_back(head_gates, head_gate_grad)[:, :, None] * chosen, 1)
    acted_wide = acted.astype(f32)
    grad_chooser = jnp.dot(acted_wide.T, chooser_logit_grad, precision=HIGH)
    acted_grad = jnp.dot(chooser_logit_grad, chooser_full.astype(f32).T, precision=HIGH)
    heads_grad = (head_gates[:, :, None] * mix_sel_grad).astype(bf16).reshape(rows_total, HS)
    row_delta = jnp.sum(heads_grad.astype(f32) * heads_out, -1)

    def cycle_turn(turn_index, carried):
        visiting, grads_visiting, query_grad = carried
        block_size = block_rows(tokens)

        def per_block(query_acc, key_block):
            scores = jnp.dot(query_sel, key_block[:, :HS].T, preferred_element_type=f32) * scaling
            probability = jnp.exp(scores - log_total[:, None])
            prob_grad = jnp.dot(heads_grad, key_block[:, HS:].T, preferred_element_type=f32)
            score_grad = (probability * (prob_grad - row_delta[:, None])).astype(bf16)
            query_acc = (
                query_acc
                + jnp.dot(score_grad, key_block[:, :HS], preferred_element_type=f32) * scaling
            )
            keys_grad = jnp.dot(score_grad.T, query_sel, preferred_element_type=f32) * scaling
            values_grad = jnp.dot(
                probability.astype(bf16).T, heads_grad, preferred_element_type=f32
            )
            return (query_acc, jnp.concatenate([keys_grad, values_grad], -1))

        query_grad, block_grads = lax.scan(
            per_block, query_grad, visiting.reshape(tokens // block_size, block_size, 2 * HS)
        )
        grads_visiting = grads_visiting + block_grads.reshape(tokens, 2 * HS)
        visiting = shifted(visiting, "ctx", 1)
        grads_visiting = shifted(grads_visiting.astype(jnp.bfloat16), "ctx", 1).astype(
            grads_visiting.dtype
        )
        return (visiting, grads_visiting, query_grad)

    cycle_state = (keyval, jnp.zeros((tokens, 2 * HS), f32), jnp.zeros((rows_total, HS), f32))
    unused_keys, keyval_grad, query_grad = lax.fori_loop(0, devices, cycle_turn, cycle_state)
    query_sel_grad = query_grad.astype(bf16).reshape(tokens, MOA_TOP, HS)
    query_all_grad = jnp.sum(chosen_low[:, :, :, None] * query_sel_grad[:, :, None, :], 1).reshape(
        tokens, MOA_EXPERTS * HS
    )
    keyval_low = keyval_grad.astype(bf16)
    grad_query = jnp.dot(acted.T, query_all_grad, preferred_element_type=f32)
    grad_keyval = jnp.dot(acted.T, keyval_low, preferred_element_type=f32)
    acted_grad = acted_grad + jnp.dot(query_all_grad, query_full.T, preferred_element_type=f32)
    acted_grad = acted_grad + jnp.dot(keyval_low, keyval_full.T, preferred_element_type=f32)
    resident_grad, grad_gain_one, grad_bias_one = norm_back(
        acted_grad, normal_one, inverse_one, gain_first
    )
    grad_states = middle_grad + resident_grad + stopped[:, None] * out_grad
    dense_grads = (
        grad_query,
        grad_keyval,
        grad_project,
        grad_chooser,
        grad_selector,
        grad_gain_one,
        grad_bias_one,
        grad_gain_two,
        grad_bias_two,
        grad_halt,
    )
    totals = (
        lax.psum(dense_grads[0].astype(jnp.bfloat16), "ctx").astype(jnp.float32),
        lax.psum(dense_grads[1].astype(jnp.bfloat16), "ctx").astype(jnp.float32),
        lax.psum(dense_grads[2].astype(jnp.bfloat16), "ctx").astype(jnp.float32),
        lax.psum(dense_grads[3].astype(jnp.bfloat16), "ctx").astype(jnp.float32),
        lax.psum(dense_grads[4].astype(jnp.bfloat16), "ctx").astype(jnp.float32),
        lax.psum(dense_grads[5].astype(jnp.bfloat16), "ctx").astype(jnp.float32),
        lax.psum(dense_grads[6].astype(jnp.bfloat16), "ctx").astype(jnp.float32),
        lax.psum(dense_grads[7].astype(jnp.bfloat16), "ctx").astype(jnp.float32),
        lax.psum(dense_grads[8].astype(jnp.bfloat16), "ctx").astype(jnp.float32),
        lax.psum(dense_grads[9].astype(jnp.bfloat16), "ctx").astype(jnp.float32),
    )
    shards = (
        lax.psum_scatter(
            totals[0].astype(jnp.bfloat16), ("seq", "wsh"), scatter_dimension=0, tiled=True
        ).astype(jnp.float32),
        lax.psum_scatter(
            totals[1].astype(jnp.bfloat16), ("seq", "wsh"), scatter_dimension=0, tiled=True
        ).astype(jnp.float32),
        lax.psum_scatter(
            totals[2].astype(jnp.bfloat16), ("seq", "wsh"), scatter_dimension=0, tiled=True
        ).astype(jnp.float32),
        lax.psum_scatter(
            totals[3].astype(jnp.bfloat16), ("seq", "wsh"), scatter_dimension=0, tiled=True
        ).astype(jnp.float32),
        lax.psum_scatter(
            totals[4].astype(jnp.bfloat16), ("seq", "wsh"), scatter_dimension=0, tiled=True
        ).astype(jnp.float32),
        lax.psum_scatter(
            totals[5].astype(jnp.bfloat16), ("seq", "wsh"), scatter_dimension=0, tiled=True
        ).astype(jnp.float32),
        lax.psum_scatter(
            totals[6].astype(jnp.bfloat16), ("seq", "wsh"), scatter_dimension=0, tiled=True
        ).astype(jnp.float32),
        lax.psum_scatter(
            totals[7].astype(jnp.bfloat16), ("seq", "wsh"), scatter_dimension=0, tiled=True
        ).astype(jnp.float32),
        lax.psum_scatter(
            totals[8].astype(jnp.bfloat16), ("seq", "wsh"), scatter_dimension=0, tiled=True
        ).astype(jnp.float32),
        lax.psum_scatter(
            totals[9].astype(jnp.bfloat16), ("seq", "wsh"), scatter_dimension=0, tiled=True
        ).astype(jnp.float32),
    )
    inner_shard, outer_shard = (
        lax.psum_scatter(
            inner_grad.astype(jnp.bfloat16), ("seq", "wsh"), scatter_dimension=1, tiled=True
        ).astype(jnp.float32),
        lax.psum_scatter(
            outer_grad.astype(jnp.bfloat16), ("seq", "wsh"), scatter_dimension=1, tiled=True
        ).astype(jnp.float32),
    )
    return (
        new_states[None],
        remaining_next[None],
        grad_states[None],
        grad_remaining[None],
        shards[0],
        shards[1],
        shards[2],
        shards[3],
        shards[4],
        shards[5],
        shards[6],
        shards[7],
        shards[8],
        shards[9],
        inner_shard,
        outer_shard,
    )


MESH = pl.DeviceIdType.MESH
CAP = 192
LIMIT_MIB = 63
KEEP = 0.7071067811865476
SPREAD = 0.3989422804014327
ERF_P = 0.3275911
ERF_A = (0.254829592, -0.284496736, 1.421413741, -1.453152027, 1.061405429)


def remote(source, target, send_sem, recv_sem, device):
    return pltpu.make_async_remote_copy(
        src_ref=source,
        dst_ref=target,
        send_sem=send_sem,
        recv_sem=recv_sem,
        device_id=device,
        device_id_type=MESH,
    )


def places():
    ctx, seq, wsh = (lax.axis_index(name) for name in ("ctx", "seq", "wsh"))
    chip, core = seq // 2, seq % 2
    over = (1 - chip) * 2 + core
    twin = (ctx, chip * 2 + 1 - core, wsh)
    beside = (ctx, over, wsh)
    above = (ctx, seq, 1 - wsh)
    across = (ctx, over, 1 - wsh)
    return (ctx, seq, wsh), twin, beside, above, across


def shard_of(place):
    return place[1] * 2 + place[2]


def moved(place, offset, length):
    return ((place[0] + offset) % length, place[1], place[2])


class PlaneGather:
    def __init__(self, shard, full, halves, send, recv, local):
        self.shard, self.full, self.halves = shard, full, halves
        self.send, self.recv, self.local = send, recv, local
        self.me, self.twin, self.beside, self.above, self.across = places()

    def pair(self, view, slot, device):
        return remote(view, view, self.send.at[slot], self.recv.at[slot], device)

    def own(self, slot, device):
        target = self.full(shard_of(self.me))
        return remote(self.shard, target, self.send.at[slot], self.recv.at[slot], device)

    def keep(self):
        return pltpu.make_async_copy(self.shard, self.full(shard_of(self.me)), self.local)

    def start(self):
        self.own(0, self.twin).start()
        self.own(1, self.beside).start()
        self.own(2, self.above).start()
        if self.halves is None:
            self.own(3, self.across).start()
        self.keep().start()

    def arrive(self, slot, place):
        self.pair(self.full(shard_of(place)), slot, self.twin).wait_recv()

    def relay(self):
        if self.halves is None:
            for slot, place in ((1, self.beside), (2, self.above), (3, self.across)):
                self.arrive(slot, place)
                self.pair(self.full(shard_of(place)), slot + 3, self.twin).start()
            return
        self.arrive(1, self.beside)
        self.pair(self.halves(shard_of(self.beside), 1), 7, self.above).start()
        self.pair(self.full(shard_of(self.beside)), 4, self.twin).start()
        self.arrive(2, self.above)
        self.pair(self.halves(shard_of(self.above), 0), 3, self.beside).start()
        self.pair(self.full(shard_of(self.above)), 5, self.twin).start()

    def relay_rest(self):
        shard = shard_of(self.across)
        for slot, half in ((3, 0), (7, 1)):
            view = self.halves(shard, half)
            self.pair(view, slot, self.twin).wait_recv()
            self.pair(view, 6 if half == 0 else 8, self.twin).start()

    def finish(self):
        self.keep().wait()
        ctx, seq, wsh = self.twin
        over = (1 - seq // 2) * 2 + seq % 2
        self.arrive(0, self.twin)
        self.arrive(4, (ctx, over, wsh))
        self.arrive(5, (ctx, seq, 1 - wsh))
        rest = shard_of((ctx, over, 1 - wsh))
        if self.halves is None:
            self.pair(self.full(rest), 6, self.twin).wait_recv()
        else:
            self.pair(self.halves(rest, 0), 6, self.twin).wait_recv()
            self.pair(self.halves(rest, 1), 8, self.twin).wait_recv()

    def drain(self):
        self.own(0, self.twin).wait_send()
        self.own(1, self.beside).wait_send()
        self.own(2, self.above).wait_send()
        beside, above, across = (shard_of(p) for p in (self.beside, self.above, self.across))
        self.pair(self.full(beside), 4, self.twin).wait_send()
        self.pair(self.full(above), 5, self.twin).wait_send()
        if self.halves is None:
            self.own(3, self.across).wait_send()
            self.pair(self.full(across), 6, self.twin).wait_send()
        else:
            self.pair(self.halves(above, 0), 3, self.beside).wait_send()
            self.pair(self.halves(beside, 1), 7, self.above).wait_send()
            self.pair(self.halves(across, 0), 6, self.twin).wait_send()
            self.pair(self.halves(across, 1), 8, self.twin).wait_send()


class LineGather:
    def __init__(self, length, blocks, send, recv):
        self.length, self.blocks, self.send, self.recv = length, blocks, send, recv
        self.me = places()[0]

    def hop(self, block, way, step, device):
        view = self.blocks(block)
        return remote(view, view, self.send.at[way, step], self.recv.at[way, step], device)

    def ways(self, step):
        ctx = self.me[0]
        left = (ctx - 1, self.me[1], self.me[2])
        right = (ctx + 1, self.me[1], self.me[2])
        return (
            (0, ctx - step, ctx - step >= 0, right, ctx + 1 < self.length),
            (1, ctx + step, ctx + step < self.length, left, ctx - 1 >= 0),
        )

    def start(self):
        for way, block, unused, device, there in self.ways(0):
            pl.when(there)(lambda b=block, w=way, d=device: self.hop(b, w, 0, d).start())

    def relay(self, step):
        for way, block, come, device, there in self.ways(step):

            def pass_on(way=way, block=block, device=device, there=there):
                self.hop(block, way, step - 1, device).wait_recv()
                if step < self.length - 1:
                    pl.when(there)(lambda: self.hop(block, way, step, device).start())

            pl.when(come)(pass_on)

    def drain(self):
        for step in range(self.length - 1):
            for way, block, come, device, there in self.ways(step):
                pl.when(jnp.logical_and(come, there))(
                    lambda b=block, w=way, d=device, s=step: self.hop(b, w, s, d).wait_send()
                )


def direct_send(view, send, recv, length):
    me = places()[0]
    return [
        remote(view, view, send.at[step - 1], recv.at[step - 1], moved(me, step, length))
        for step in range(1, length)
    ]


def direct_wait(view_of, send, recv, length):
    me = places()[0]
    for step in range(1, length):
        source = moved(me, length - step, length)
        view = view_of(source[0])
        remote(view, view, send.at[step - 1], recv.at[step - 1], source).wait_recv()


def lanes_of(shape):
    return lax.broadcasted_iota(jnp.int32, shape, 1)


def rows_of(shape):
    return lax.broadcasted_iota(jnp.int32, shape, 0)


def product(left, right, dims=((1,), (0,))):
    return lax.dot_general(left, right, (dims, ((), ())), preferred_element_type=jnp.float32)


def gelu_parts(values):
    near = jnp.abs(values) * KEEP
    turn = 1.0 / (1.0 + ERF_P * near)
    bell = jnp.exp(-near * near)
    series = ERF_A[4]
    for term in ERF_A[3::-1]:
        series = series * turn + term
    tail = 0.5 * series * turn * bell
    share = jnp.where(values >= 0, 1.0 - tail, tail)
    return values * share, share + values * bell * SPREAD


def forward_part(length, r):
    f32, bf16 = jnp.float32, jnp.bfloat16
    tokens = r.states.shape[0]
    me, twin, beside, above, across = places()
    ctx = me[0]
    experts = EXP_DEV * length
    peers = [twin, beside, above, across] + [moved(me, k, length) for k in range(1, length)]
    barrier = pltpu.get_barrier_semaphore()
    for peer in peers:
        pl.semaphore_signal(barrier, inc=1, device_id=peer, device_id_type=MESH)

    def gather(index, shard, full, halves=None):
        return PlaneGather(
            shard, full, halves, r.plane_send.at[index], r.plane_recv.at[index], r.plane_local.at[index]
        )

    def rows_view(ref, rows):
        return lambda shard: ref.at[pl.ds(shard * rows, rows), :]

    pack_gather = gather(0, r.pack, rows_view(r.packed, 64))
    query_gather = gather(1, r.query_part, rows_view(r.query, 64))
    project_gather = gather(2, r.project_part, rows_view(r.project, 192))
    inner_gather = gather(
        3,
        r.inner_part,
        lambda shard: r.inner.at[:, pl.ds(shard * 64, 64), :],
        lambda shard, half: r.inner.at[half, pl.ds(shard * 64, 64), :],
    )
    outer_gather = gather(
        4,
        r.outer_part,
        lambda shard: r.outer.at[:, pl.ds(shard * 256, 256), :],
        lambda shard, half: r.outer.at[half, pl.ds(shard * 256, 256), :],
    )
    cot_gather = LineGather(length, lambda b: r.cots.at[b], r.line_send.at[0], r.line_recv.at[0])
    entering_gather = LineGather(length, lambda b: r.entering.at[b], r.line_send.at[1], r.line_recv.at[1])

    def keyval_view(block):
        return r.keyval.at[pl.ds(block * tokens, tokens), :]

    r.cots[ctx] = r.cotangent[...].astype(bf16)
    pl.semaphore_wait(barrier, len(peers))
    pack_gather.start()
    query_gather.start()
    cot_gather.start()

    values = r.states[...].astype(f32)
    centred = values - jnp.mean(values, -1, keepdims=True)
    inverse = lax.rsqrt(jnp.mean(centred * centred, -1, keepdims=True) + EPS)
    r.flow[...] = centred * inverse

    lane = lanes_of((tokens, 128))
    ids = r.route_ids[...].astype(f32)
    both = jnp.where(lane == 0, ids[:, 0:1], ids[:, 1:2])
    turned = jnp.transpose(both)[0:8]
    expert_row = rows_of((8, tokens)).astype(f32)
    picked = jnp.logical_or(expert_row == turned[0:1], expert_row == turned[1:2])
    marks = jnp.concatenate([picked.astype(f32), jnp.zeros((8, tokens), f32)], 0).astype(bf16)
    earlier = (rows_of((tokens, tokens)) < lanes_of((tokens, tokens))).astype(f32).astype(bf16)
    ranks = product(marks, earlier)[0:8]
    r.routes[ctx, 0:8, :] = jnp.where(picked, ranks, -1.0)

    pack_gather.relay()
    pack_gather.finish()
    r.small[...] = jnp.transpose(r.packed[:, 128:256].astype(f32))
    shaped = (r.flow[...] * r.small[32:33, :] + r.small[33:34, :]).astype(bf16)
    r.acted[...] = shaped
    sides = product(shaped, r.packed[...])
    keyval_view(ctx)[...] = sides[:, 0:128].astype(bf16)
    keyval_sends = direct_send(keyval_view(ctx), r.direct_sems.at[0], r.direct_recvs.at[0], length)
    for copy in keyval_sends:
        copy.start()

    id_lanes = [r.head_ids[:, j : j + 1] for j in range(MOA_TOP)]
    logits = [
        jnp.sum(jnp.where(lane == id_lanes[j], sides[:, 128:256], 0.0), -1, keepdims=True)
        for j in range(MOA_TOP)
    ]
    peak = jnp.maximum(jnp.maximum(logits[0], logits[1]), jnp.maximum(logits[2], logits[3]))
    powers = [jnp.exp(item - peak) for item in logits]
    total = powers[0] + powers[1] + powers[2] + powers[3]
    gates = [item / total for item in powers]
    r.head_gates[...] = jnp.where(
        lane == 0,
        gates[0],
        jnp.where(lane == 1, gates[1], jnp.where(lane == 2, gates[2], gates[3])),
    )

    query_gather.relay()
    project_gather.start()
    inner_gather.start()
    query_gather.finish()
    for part in range(6):
        columns = slice(part * 256, part * 256 + 256)
        r.mixture[:, columns] = product(r.acted[...], r.query[:, columns]).astype(bf16)
    cot_gather.relay(1)

    low_half = lane < HS
    side = lane // HS
    for j in range(MOA_TOP):
        wanted = id_lanes[j] - side
        chosen = jnp.zeros((tokens, 128), f32)
        for pair in range(MOA_EXPERTS // 2):
            block = r.mixture[:, pair * 128 : pair * 128 + 128].astype(f32)
            chosen = chosen + jnp.where(wanted == 2 * pair, block, 0.0)
        folded = chosen + pltpu.roll(chosen, HS, 1)
        r.queries[j * tokens : (j + 1) * tokens, :] = (
            jnp.where(low_half, folded, 0.0) * HS ** (-0.5)
        ).astype(bf16)

    direct_wait(keyval_view, r.direct_sems.at[0], r.direct_recvs.at[0], length)
    chunk = 256

    def attend(turn, carried):
        rows = pl.ds(pl.multiple_of(turn * chunk, chunk), chunk)
        scores = product(r.queries[rows, :], r.keyval[...], ((1,), (1,)))
        top = jnp.max(scores, -1, keepdims=True)
        weights = jnp.exp(scores - top)
        mass = jnp.sum(weights, -1, keepdims=True)
        seen = product(weights.astype(bf16), r.keyval[...]) / mass
        r.heads[rows, :] = jnp.where(lanes_of((chunk, 128)) < HS, top + jnp.log(mass), seen)
        return carried

    lax.fori_loop(0, MOA_TOP * tokens // chunk, attend, 0)
    project_gather.relay()

    spread = []
    for j in range(MOA_TOP):
        head = r.heads[j * tokens : (j + 1) * tokens, :]
        both = jnp.where(low_half, pltpu.roll(head, HS, 1), head)
        spread.append(both * r.head_gates[:, j : j + 1])
    for pair in range(MOA_EXPERTS // 2):
        block = jnp.zeros((tokens, 128), f32)
        for j in range(MOA_TOP):
            block = jnp.where(id_lanes[j] - side == 2 * pair, spread[j], block)
        r.mixture[:, pair * 128 : pair * 128 + 128] = block.astype(bf16)

    project_gather.finish()
    between = r.states[...].astype(f32) + product(r.mixture[...], r.project[...])
    r.middle[...] = between
    centred = between - jnp.mean(between, -1, keepdims=True)
    inverse = lax.rsqrt(jnp.mean(centred * centred, -1, keepdims=True) + EPS)
    entry = (centred * inverse * r.small[34:35, :] + r.small[35:36, :]).astype(bf16)
    r.entering[ctx] = entry
    entering_gather.start()
    logits = product(r.small[16:32, :].astype(bf16), entry, ((1,), (1,)))[8:16]
    peak = jnp.max(jnp.where(picked, logits, -1e30), 0, keepdims=True)
    powers = jnp.where(picked, jnp.exp(jnp.where(picked, logits - peak, 0.0)), 0.0)
    r.routes[ctx, 8:16, :] = powers / jnp.sum(powers, 0, keepdims=True)
    route_sends = direct_send(r.routes.at[ctx], r.direct_sems.at[1], r.direct_recvs.at[1], length)
    for copy in route_sends:
        copy.start()

    def selection(source, expert):
        row = r.routes[source, pl.ds(EXP_DEV * ctx + expert, 1), :]
        return rows_of((CAP, tokens)).astype(f32) == row

    def slots(source):
        return pl.ds(pl.multiple_of(source * CAP, CAP), CAP)

    def first_half(source):
        def one(expert, carried):
            chosen = selection(source, expert).astype(f32).astype(bf16)
            rows = product(chosen, r.entering[source]).astype(bf16)
            r.slot_rows[expert, slots(source), :] = rows

            def part(index, kept):
                columns = pl.ds(pl.multiple_of(index * 512, 512), 512)
                before = product(rows, r.inner[expert, :, columns])
                value, gradient = gelu_parts(before)
                r.active[expert, slots(source), columns] = value.astype(bf16)
                r.slope[expert, slots(source), columns] = gradient.astype(bf16)
                return kept

            return lax.fori_loop(0, 4, part, carried)

        lax.fori_loop(0, EXP_DEV, one, 0)

    inner_gather.relay()
    outer_gather.start()
    direct_wait(lambda b: r.routes.at[b], r.direct_sems.at[1], r.direct_recvs.at[1], length)
    entering_gather.relay(1)
    inner_gather.relay_rest()
    inner_gather.finish()

    def step_of(step, carried):
        for ahead in range(2, length):

            @pl.when(step == ahead - 1)
            def _():
                entering_gather.relay(ahead)
                if ahead < length - 1:
                    pass

        @pl.when(step == length - 2)
        def _():
            cot_gather.relay(2)

        @pl.when(step == length - 1)
        def _():
            outer_gather.relay()

        before_me = ctx - step >= 0
        after_me = jnp.logical_and(ctx + step < length, step > 0)
        count = before_me.astype(jnp.int32) + after_me.astype(jnp.int32)

        def visit(turn, kept):
            source = jnp.where(jnp.logical_and(turn == 0, before_me), ctx - step, ctx + step)
            first_half(source)
            return kept

        lax.fori_loop(0, count, visit, 0)
        return carried

    lax.fori_loop(0, length, step_of, 0)
    outer_gather.relay_rest()
    cot_gather.relay(length - 1)
    outer_gather.finish()

    def second_half(turn, carried):
        expert, part = turn // 2, turn % 2
        rows = pl.ds(pl.multiple_of(part * 384, 384), 384)
        r.result[expert, rows, :] = product(r.active[expert, rows, :], r.outer[expert]).astype(bf16)
        return carried

    lax.fori_loop(0, 2 * EXP_DEV, second_half, 0)

    def score(source, carried):
        lines = []
        for expert in range(EXP_DEV):
            chosen = selection(source, expert).astype(f32)
            cot_rows = product(chosen.astype(bf16), r.cots[source]).astype(bf16)
            r.slot_cot[expert, slots(source), :] = cot_rows
            rows = r.result[expert, slots(source), :].astype(f32)
            toward = jnp.sum(rows * r.small[36:37, :], -1, keepdims=True)
            against = jnp.sum(rows * cot_rows.astype(f32), -1, keepdims=True)
            lines.append(jnp.sum(chosen * toward, 0, keepdims=True))
            lines.append(jnp.sum(chosen * against, 0, keepdims=True))
        lines.append(jnp.zeros((8 - 2 * EXP_DEV, tokens), f32))
        sheet = jnp.concatenate(lines, 0)

        @pl.when(source == ctx)
        def _():
            r.scores_back[ctx] = sheet

        @pl.when(source != ctx)
        def _():
            r.score_sent[source] = sheet
            offset = (source - ctx + length) % length
            remote(
                r.score_sent.at[source],
                r.scores_back.at[ctx],
                r.direct_sems.at[2, offset - 1],
                r.direct_recvs.at[2, offset - 1],
                (source, me[1], me[2]),
            ).start()

        return carried

    lax.fori_loop(0, length, score, 0)
    direct_wait(lambda b: r.scores_back.at[b], r.direct_sems.at[2], r.direct_recvs.at[2], length)
    for step in range(1, length):
        target = moved(me, step, length)
        remote(
            r.score_sent.at[target[0]],
            r.scores_back.at[ctx],
            r.direct_sems.at[2, step - 1],
            r.direct_recvs.at[2, step - 1],
            target,
        ).wait_send()
    for copy in keyval_sends + route_sends:
        copy.wait_send()
    for item in (pack_gather, query_gather, project_gather, inner_gather, outer_gather):
        item.drain()
    cot_gather.drain()
    entering_gather.drain()


class PlaneReduce:
    def __init__(self, piece, rows, halves, arrived, send, recv):
        self.piece, self.rows, self.halves, self.arrived = piece, rows, halves, arrived
        self.send, self.recv = send, recv
        self.me, self.twin, self.beside, self.above, self.across = places()
        self.chip, self.core, self.line = self.me[1] // 2, self.me[1] % 2, self.me[2]

    def half(self, chip, core):
        view, half = self.piece(chip, core), self.halves.at[chip]
        return remote(view, half, self.send.at[chip], self.recv.at[chip], self.twin)

    def shard(self, chip, line):
        return self.piece(chip, self.core).at[pl.ds(line * self.rows, self.rows), :]

    def start(self):
        for chip in range(2):
            self.half(chip, 1 - self.core).start()

    def spread(self, slot, chip, line, device):
        return remote(
            self.shard(chip, line),
            self.arrived.at[slot],
            self.send.at[2 + slot],
            self.recv.at[2 + slot],
            device,
        )

    def sends(self):
        return (
            self.spread(0, 1 - self.chip, self.line, self.beside),
            self.spread(1, self.chip, 1 - self.line, self.above),
            self.spread(2, 1 - self.chip, 1 - self.line, self.across),
        )

    def add_halves(self):
        for chip in range(2):
            self.half(chip, self.core).wait_recv()
            view = self.piece(chip, self.core)
            both = view[...].astype(jnp.float32) + self.halves[chip].astype(jnp.float32)
            view[...] = both.astype(jnp.bfloat16)
        for copy in self.sends():
            copy.start()

    def total(self):
        for copy in self.sends():
            copy.wait_recv()
        value = self.shard(self.chip, self.line)[...].astype(jnp.float32)
        for slot in range(3):
            value = value + self.arrived[slot].astype(jnp.float32)
        return value

    def drain(self):
        for chip in range(2):
            self.half(chip, 1 - self.core).wait_send()
        for copy in self.sends():
            copy.wait_send()


class LineSum:
    def __init__(self, length, value, parts, summed, reduce_sems, gather_sems):
        self.length, self.value, self.parts, self.summed = length, value, parts, summed
        self.reduce_sems, self.gather_sems = reduce_sems, gather_sems
        self.me = places()[0]
        self.share = value.shape[0] // length

    def rows(self, block):
        return pl.ds(pl.multiple_of(block * self.share, self.share), self.share)

    def part(self, step):
        target = moved(self.me, step, self.length)
        send, recv = self.reduce_sems
        return remote(
            self.value.at[self.rows(target[0]), :],
            self.parts.at[step - 1],
            send.at[step - 1],
            recv.at[step - 1],
            target,
        )

    def start(self, value):
        self.value[...] = value.astype(jnp.bfloat16)
        for step in range(1, self.length):
            self.part(step).start()

    def view(self, block):
        return self.summed.at[self.rows(block), :]

    def share_out(self):
        for step in range(1, self.length):
            self.part(step).wait_recv()
        value = self.value[self.rows(self.me[0]), :].astype(jnp.float32)
        for step in range(1, self.length):
            value = value + self.parts[step - 1].astype(jnp.float32)
        self.view(self.me[0])[...] = value.astype(jnp.bfloat16)
        for copy in direct_send(self.view(self.me[0]), *self.gather_sems, self.length):
            copy.start()

    def finish(self):
        direct_wait(self.view, *self.gather_sems, self.length)
        return self.summed[...]

    def drain(self):
        for step in range(1, self.length):
            self.part(step).wait_send()
        for copy in direct_send(self.view(self.me[0]), *self.gather_sems, self.length):
            copy.wait_send()


class ExpertReduce:
    def __init__(self, inner, outer, half_in, half_out, side_in, side_out, last_in, last_out, send, recv):
        self.arrays = (inner, outer)
        self.halves = (half_in, half_out)
        self.sides = (side_in, side_out)
        self.lasts = (last_in, last_out)
        self.counts = (64, 256)
        self.send, self.recv = send, recv
        self.me, self.twin, self.beside, self.above, unused = places()
        self.chip, self.core, self.line = self.me[1] // 2, self.me[1] % 2, self.me[2]

    def rows(self, which, chip, core, line, count):
        size = self.counts[which]
        start = pl.multiple_of(((chip * 2 + core) * 2 + line) * size, size)
        return self.arrays[which].at[:, pl.ds(start, count * size), :]

    def copy(self, source, target, slot, device):
        return remote(source, target, self.send.at[slot], self.recv.at[slot], device)

    def half(self, which, chip, core):
        return self.copy(
            self.rows(which, chip, core, 0, 2), self.halves[which].at[chip], 2 * which + chip, self.twin
        )

    def start(self, which):
        for chip in range(2):
            self.half(which, chip, 1 - self.core).start()

    def side(self, which):
        if which == 0:
            source = self.rows(0, 1 - self.chip, self.core, 0, 2)
            return [self.copy(source, self.sides[0], 4, self.beside)]
        return [
            self.copy(
                self.rows(1, chip, self.core, 1 - self.line, 1), self.sides[1].at[chip], 5 + chip, self.above
            )
            for chip in range(2)
        ]

    def add(self, view, other):
        for expert in range(EXP_DEV):
            both = view[expert].astype(jnp.float32) + other[expert].astype(jnp.float32)
            view[expert] = both.astype(jnp.bfloat16)

    def add_halves(self, which):
        def one(chip, carried):
            self.half(which, chip, self.core).wait_recv()
            self.add(self.rows(which, chip, self.core, 0, 2), self.halves[which].at[chip])
            return carried

        lax.fori_loop(0, 2, one, 0)
        for copy in self.side(which):
            copy.start()

    def last(self, which):
        if which == 0:
            source = self.rows(0, self.chip, self.core, 1 - self.line, 1)
            return self.copy(source, self.lasts[0], 7, self.above)
        source = self.rows(1, 1 - self.chip, self.core, self.line, 1)
        return self.copy(source, self.lasts[1], 8, self.beside)

    def add_sides(self, which):
        for copy in self.side(which):
            copy.wait_recv()
        if which == 0:
            self.add(self.rows(0, self.chip, self.core, 0, 2), self.sides[0])
        else:
            for chip in range(2):
                self.add(self.rows(1, chip, self.core, self.line, 1), self.sides[1].at[chip])
        self.last(which).start()

    def total(self, which, result):
        self.last(which).wait_recv()
        view = self.rows(which, self.chip, self.core, self.line, 1)
        for expert in range(EXP_DEV):
            both = view[expert].astype(jnp.float32) + self.lasts[which][expert].astype(jnp.float32)
            result[expert] = both.astype(jnp.bfloat16)

    def drain(self):
        for which in range(2):
            for chip in range(2):
                self.half(which, chip, 1 - self.core).wait_send()
            for copy in self.side(which):
                copy.wait_send()
            self.last(which).wait_send()


def backward_part(length, r):
    f32, bf16 = jnp.float32, jnp.bfloat16
    tokens = r.states.shape[0]
    me = places()[0]
    ctx = me[0]
    lane = lanes_of((tokens, 128))
    low_half = lane < HS
    side = lane // HS
    id_lanes = [r.head_ids[:, j : j + 1] for j in range(MOA_TOP)]

    def sems(row):
        return r.direct_sems.at[row], r.direct_recvs.at[row]

    def slots(source):
        return pl.ds(pl.multiple_of(source * CAP, CAP), CAP)

    def to_owner(view, target_ref, row, block):
        slot = (block - ctx + length) % length - 1
        send, recv = sems(row)
        return remote(view, target_ref.at[slot], send.at[slot], recv.at[slot], (block, me[1], me[2]))

    def from_all(target_ref, row):
        send, recv = sems(row)
        for step in range(1, length):
            view = target_ref.at[step - 1]
            source = moved(me, length - step, length)
            remote(view, view, send.at[step - 1], recv.at[step - 1], source).wait_recv()

    def sent_all(view_of, target_ref, row):
        for step in range(1, length):
            block = moved(me, step, length)[0]
            to_owner(view_of(block), target_ref, row, block).wait_send()

    r.gsmall[...] = jnp.zeros_like(r.gsmall)
    mid = r.middle[...]
    cot = r.cotangent[...]
    halt_row = r.small[36:37, :]
    reach = jnp.sum(mid * halt_row, -1, keepdims=True)
    gap = jnp.sum(cot * (r.states[...].astype(f32) - mid), -1, keepdims=True)
    turned = jnp.transpose(jnp.where(lane == 0, reach, gap))[0:8]
    gates = r.routes[ctx, 8:16, :]
    toward = jnp.concatenate(
        [r.scores_back[d, 2 * e : 2 * e + 1, :] for d in range(length) for e in range(EXP_DEV)], 0
    )
    against = jnp.concatenate(
        [r.scores_back[d, 2 * e + 1 : 2 * e + 2, :] for d in range(length) for e in range(EXP_DEV)], 0
    )
    halting = jax.nn.sigmoid(turned[0:1] + jnp.sum(gates * toward, 0, keepdims=True))
    stop_grad = turned[1:2] - jnp.sum(gates * against, 0, keepdims=True)
    mass, left = r.remaining[...], r.left_cot[...]
    stopped = mass * halting
    halt_grad = (stop_grad - left) * mass * halting * (1.0 - halting)
    r.rows_out[0:1, :] = mass * (1.0 - halting)
    r.rows_out[1:2, :] = stop_grad * halting + left * (1.0 - halting)
    sheet = jnp.concatenate([1.0 - stopped, halt_grad, stopped, jnp.zeros((5, tokens), f32)], 0)
    r.factors[ctx] = sheet
    factor_sends = direct_send(r.factors.at[ctx], *sems(3), length)
    for copy in factor_sends:
        copy.start()
    r.columns[...] = jnp.transpose(jnp.concatenate([sheet, jnp.zeros((120, tokens), f32)], 0))
    gate_grad = (1.0 - stopped) * against + halt_grad * toward
    pick_grad = gates * (gate_grad - jnp.sum(gates * gate_grad, 0, keepdims=True))
    coarse = pick_grad.astype(bf16).astype(f32)
    r.pick_grads[...] = jnp.concatenate([coarse, pick_grad - coarse], 0).astype(bf16)
    sums = product(r.pick_grads[...], r.entering[ctx])
    r.gsmall[24:32, :] = sums[0:8] + sums[8:16]
    keep_col, halt_col = r.columns[:, 0:1], r.columns[:, 1:2]
    r.flow[...] = keep_col * cot + halt_col * halt_row
    r.gsmall[36:37, :] = jnp.sum(halt_col * mid, 0, keepdims=True)

    def picks(block, expert):
        row = r.routes[block, pl.ds(EXP_DEV * ctx + expert, 1), :]
        return (rows_of((CAP, tokens)).astype(f32) == row).astype(f32)

    def block_back(turn, carried):
        offset = jnp.where(turn == 0, 0, jnp.where(turn == length - 1, 1, turn + 1))
        block = (ctx + offset) % length

        @pl.when(turn > 0)
        def _():
            slot = (ctx - block + length) % length - 1
            view = r.factors.at[block]
            send, recv = sems(3)
            remote(view, view, send.at[slot], recv.at[slot], (block, me[1], me[2])).wait_recv()

        def one(expert, kept):
            chosen = picks(block, expert)
            keep = jnp.sum(chosen * r.factors[block, 0:1, :], -1, keepdims=True)
            halt = jnp.sum(chosen * r.factors[block, 1:2, :], -1, keepdims=True)
            gate = jnp.sum(
                chosen * r.routes[block, pl.ds(8 + EXP_DEV * ctx + expert, 1), :], -1, keepdims=True
            )
            rows = r.result[expert, slots(block), :].astype(f32) * gate
            r.gsmall[36:37, :] += jnp.sum(halt * rows, 0, keepdims=True)
            r.result[expert, slots(block), :] = rows.astype(bf16)
            incoming = r.slot_cot[expert, slots(block), :].astype(f32)
            rows_grad = (gate * (keep * incoming + halt * halt_row)).astype(bf16)
            r.slot_cot[expert, slots(block), :] = rows_grad

            def part(index, inside):
                columns = pl.ds(pl.multiple_of(index * 512, 512), 512)
                back = product(rows_grad, r.outer[expert, columns, :], ((1,), (1,)))
                slope = r.slope[expert, slots(block), columns].astype(f32)
                r.slope[expert, slots(block), columns] = (back * slope).astype(bf16)
                return inside

            lax.fori_loop(0, 4, part, 0)
            sent = product(r.slope[expert, slots(block), :], r.inner[expert], ((1,), (1,)))
            r.slot_back[expert] = sent.astype(bf16)
            return kept

        lax.fori_loop(0, EXP_DEV, one, 0)
        spread = product(picks(block, 0).astype(bf16), r.slot_back[0], ((0,), (0,)))
        spread = spread + product(picks(block, 1).astype(bf16), r.slot_back[1], ((0,), (0,)))
        r.entering[block] = spread.astype(bf16)

        @pl.when(turn > 0)
        def _():
            to_owner(r.entering.at[block], r.back_in, 4, block).start()

        return carried

    lax.fori_loop(0, length, block_back, 0)

    def block_forward(turn, carried):
        offset = jnp.where(turn == 0, 0, jnp.where(turn == length - 1, 1, turn + 1))
        block = (ctx + offset) % length
        spread = product(picks(block, 0).astype(bf16), r.result[0, slots(block), :], ((0,), (0,)))
        spread = spread + product(
            picks(block, 1).astype(bf16), r.result[1, slots(block), :], ((0,), (0,))
        )
        r.cots[block] = spread.astype(bf16)

        @pl.when(turn > 0)
        def _():
            to_owner(r.cots.at[block], r.mix_in, 5, block).start()

        return carried

    lax.fori_loop(0, length, block_forward, 0)

    experts = ExpertReduce(
        r.inner, r.outer, r.half_in, r.half_out, r.side_in, r.side_out, r.last_in, r.last_out,
        r.expert_send, r.expert_recv,
    )

    def outer_grad(turn, carried):
        expert, part = turn // 4, turn % 4
        columns = pl.ds(pl.multiple_of(part * 512, 512), 512)
        value = product(r.active[expert, :, columns], r.slot_cot[expert], ((0,), (0,)))
        r.outer[expert, columns, :] = value.astype(bf16)
        return carried

    lax.fori_loop(0, 4 * EXP_DEV, outer_grad, 0)
    experts.start(1)

    def inner_grad(turn, carried):
        expert, part = turn // 4, turn % 4
        columns = pl.ds(pl.multiple_of(part * 512, 512), 512)
        value = product(r.slot_rows[expert], r.slope[expert, :, columns], ((0,), (0,)))
        r.inner[expert, :, columns] = value.astype(bf16)
        return carried

    lax.fori_loop(0, 4 * EXP_DEV, inner_grad, 0)
    experts.start(0)
    experts.add_halves(1)
    experts.add_halves(0)

    from_all(r.back_in, 4)
    mid = r.middle[...]
    selector = r.small[24:32, :]
    double = jnp.concatenate([selector, selector], 0).astype(bf16)
    back = product(r.pick_grads[...], double, ((0,), (0,))) + r.entering[ctx].astype(f32)
    for step in range(length - 1):
        back = back + r.back_in[step].astype(f32)
    centred = mid - jnp.mean(mid, -1, keepdims=True)
    inverse = lax.rsqrt(jnp.mean(centred * centred, -1, keepdims=True) + EPS)
    plain = centred * inverse
    r.gsmall[34:35, :] = jnp.sum(back * plain, 0, keepdims=True)
    r.gsmall[35:36, :] = jnp.sum(back, 0, keepdims=True)
    scaled = back * r.small[34:35, :]
    level = jnp.mean(scaled, -1, keepdims=True)
    tilt = jnp.mean(scaled * plain, -1, keepdims=True)
    flow = r.flow[...] + inverse * (scaled - level - plain * tilt)
    r.flow[...] = flow
    attn_grad = flow.astype(bf16)

    def project_piece(chip, core):
        column = pl.multiple_of((chip * 2 + core) * 512, 512)
        return r.active.at[1, pl.ds(0, 384), pl.ds(column, 512)]

    for part in range(4):
        value = product(r.mixture[:, part * 384 : part * 384 + 384], attn_grad, ((0,), (0,)))
        r.active[1, 0:384, part * 512 : part * 512 + 512] = value.astype(bf16)

    def reducer(index, piece, rows, halves, arrived):
        return PlaneReduce(piece, rows, halves, arrived, r.dense_send.at[index], r.dense_recv.at[index])

    project_reduce = reducer(0, project_piece, 192, r.project_half, r.project_in)
    project_reduce.start()

    chosen = [jnp.zeros((tokens, 128), f32) for unused in range(MOA_TOP)]
    for part in range(6):
        value = product(attn_grad, r.project[part * 256 : part * 256 + 256, :], ((1,), (1,)))
        for pair in range(2):
            block = value[:, pair * 128 : pair * 128 + 128]
            for j in range(MOA_TOP):
                wanted = id_lanes[j] - side == 2 * (2 * part + pair)
                chosen[j] = chosen[j] + jnp.where(wanted, block, 0.0)
    gate_lanes = [r.head_gates[:, j : j + 1] for j in range(MOA_TOP)]
    gate_grads = []
    for j in range(MOA_TOP):
        rows = slice(j * tokens, (j + 1) * tokens)
        head = r.heads[rows, :]
        folded = jnp.where(low_half, 0.0, chosen[j] + pltpu.roll(chosen[j], HS, 1))
        gate_grads.append(jnp.sum(folded * head, -1, keepdims=True))
        grads = (gate_lanes[j] * folded).astype(bf16)
        r.heads_grad[rows, :] = grads
        delta = jnp.sum(grads.astype(f32) * head, -1, keepdims=True)
        pair = jnp.transpose(jnp.where(lane == 0, head[:, 0:1], delta))
        r.stats[:, rows] = pair[0:8]
    common = sum(g * v for g, v in zip(gate_lanes, gate_grads))
    logit = jnp.zeros((tokens, 128), f32)
    for j in range(MOA_TOP):
        logit = jnp.where(lane == id_lanes[j], gate_lanes[j] * (gate_grads[j] - common), logit)
    coarse = logit.astype(bf16)
    fine = (logit - coarse.astype(f32)).astype(bf16)
    sums = product(coarse, r.acted[...], ((0,), (0,))) + product(fine, r.acted[...], ((0,), (0,)))
    r.gsmall[0:24, :] = sums[0:24]
    chooser = r.small[...].astype(bf16)
    r.acted_grad[...] = product(coarse, chooser) + product(fine, chooser)
    project_reduce.add_halves()
    experts.add_sides(1)
    experts.add_sides(0)

    r.kv_grad[...] = jnp.zeros_like(r.kv_grad)
    chunk = 256

    def attend_back(turn, carried):
        rows = pl.ds(pl.multiple_of(turn * chunk, chunk), chunk)
        query, grads, keyval = r.queries[rows, :], r.heads_grad[rows, :], r.keyval[...]
        scores = product(keyval, query, ((1,), (1,)))
        weights = jnp.exp(scores - r.stats[0:1, rows])
        upward = product(keyval, grads, ((1,), (1,)))
        score_grad = (weights * (upward - r.stats[1:2, rows])).astype(bf16)
        r.kv_grad[...] += product(score_grad, query) + product(weights.astype(bf16), grads)
        r.heads[rows, :] = product(score_grad, keyval, ((0,), (0,))) * HS ** (-0.5)
        return carried

    lax.fori_loop(0, MOA_TOP * tokens // chunk, attend_back, 0)

    def send_keyval(turn, carried):
        block = (ctx + turn) % length
        rows = pl.ds(pl.multiple_of(block * tokens, tokens), tokens)

        @pl.when(turn > 0)
        def _():
            r.heads_grad[rows, :] = r.kv_grad[rows, :].astype(bf16)
            to_owner(r.heads_grad.at[rows, :], r.kv_in, 6, block).start()

        return carried

    lax.fori_loop(0, length, send_keyval, 0)
    spread = []
    for j in range(MOA_TOP):
        piece = r.heads[j * tokens : (j + 1) * tokens, :]
        spread.append(jnp.where(low_half, piece, pltpu.roll(piece, HS, 1)))
    for pair in range(MOA_EXPERTS // 2):
        block = jnp.zeros((tokens, 128), f32)
        for j in range(MOA_TOP):
            block = jnp.where(id_lanes[j] - side == 2 * pair, spread[j], block)
        r.mixture[:, pair * 128 : pair * 128 + 128] = block.astype(bf16)
    for part in range(4):
        columns = slice(part * 384, part * 384 + 384)
        value = product(r.acted[...], r.mixture[:, columns], ((0,), (0,)))
        r.active[0, 0:512, columns] = value.astype(bf16)

    def wide_piece(first, width):
        def piece(chip, core):
            start = pl.multiple_of((chip * 2 + core) * 128, 128)
            return r.active.at[0, pl.ds(start, 128), pl.ds(first, width)]

        return piece

    query_reduce = reducer(1, wide_piece(0, 1536), 64, r.query_half, r.query_in)
    query_reduce.start()
    r.acted_grad[...] += product(r.mixture[...], r.query[...], ((1,), (1,)))
    project_line = LineSum(length, r.project_value, r.project_parts, r.project_sum, sems(7), sems(8))
    project_line.start(project_reduce.total())
    query_reduce.add_halves()

    own_rows = pl.ds(pl.multiple_of(ctx * tokens, tokens), tokens)
    from_all(r.kv_in, 6)
    keyval_grad = r.kv_grad[own_rows, :]
    for step in range(length - 1):
        keyval_grad = keyval_grad + r.kv_in[step].astype(f32)
    keyval_grad = keyval_grad.astype(bf16)
    back = r.acted_grad[...] + product(keyval_grad, r.packed[:, 0:128], ((1,), (1,)))
    values = r.states[...].astype(f32)
    centred = values - jnp.mean(values, -1, keepdims=True)
    inverse = lax.rsqrt(jnp.mean(centred * centred, -1, keepdims=True) + EPS)
    plain = centred * inverse
    r.gsmall[32:33, :] = jnp.sum(back * plain, 0, keepdims=True)
    r.gsmall[33:34, :] = jnp.sum(back, 0, keepdims=True)
    r.active[0, 0:512, 1536:1664] = product(r.acted[...], keyval_grad, ((0,), (0,))).astype(bf16)
    r.active[0, 0:512, 1664:1792] = jnp.transpose(r.gsmall[...]).astype(bf16)
    small_reduce = reducer(2, wide_piece(1536, 256), 64, r.small_half, r.small_in)
    small_reduce.start()
    scaled = back * r.small[32:33, :]
    level = jnp.mean(scaled, -1, keepdims=True)
    tilt = jnp.mean(scaled * plain, -1, keepdims=True)
    r.grad_states[...] = (
        r.flow[...] + inverse * (scaled - level - plain * tilt) + r.columns[:, 2:3] * r.cotangent[...]
    )
    small_reduce.add_halves()
    project_line.share_out()
    query_line = LineSum(length, r.query_value, r.query_parts, r.query_sum, sems(9), sems(10))
    query_line.start(query_reduce.total())
    small_line = LineSum(length, r.small_value, r.small_parts, r.small_sum, sems(11), sems(12))
    small_line.start(small_reduce.total())

    experts.total(1, r.grad_outer)
    experts.total(0, r.grad_inner)
    from_all(r.mix_in, 5)
    final = r.middle[...] + r.cots[ctx].astype(f32)
    for step in range(length - 1):
        final = final + r.mix_in[step].astype(f32)
    r.new_states[...] = (
        r.columns[:, 2:3] * r.states[...].astype(f32) + r.columns[:, 0:1] * final
    ).astype(bf16)
    query_line.share_out()
    small_line.share_out()
    r.grad_project[...] = project_line.finish()
    r.grad_query[...] = query_line.finish()
    r.grad_small[...] = small_line.finish()

    for copy in factor_sends:
        copy.wait_send()
    sent_all(lambda b: r.entering.at[b], r.back_in, 4)
    sent_all(lambda b: r.cots.at[b], r.mix_in, 5)
    sent_all(
        lambda b: r.heads_grad.at[pl.ds(pl.multiple_of(b * tokens, tokens), tokens), :], r.kv_in, 6
    )
    for item in (project_reduce, query_reduce, small_reduce, experts):
        item.drain()
    for item in (project_line, query_line, small_line):
        item.drain()


def whole_kernel(length, names, *refs):
    r = SimpleNamespace(**dict(zip(names, refs)))
    forward_part(length, r)
    backward_part(length, r)


def fast_body(
    states,
    remaining,
    moa_ids,
    ffn_ids,
    out_cotangent,
    left_cotangent,
    query_weight,
    keyval_weight,
    project_weight,
    chooser,
    selector,
    gain_one,
    bias_one,
    gain_two,
    bias_two,
    halt_weight,
    expert_in,
    expert_out,
):
    f32, bf16 = jnp.float32, jnp.bfloat16
    length = lax.axis_size("ctx")
    tokens = states.shape[1]
    rows = length * CAP
    wide = MOA_EXPERTS * HS
    flat = jnp.stack([gain_one, bias_one, gain_two, bias_two, halt_weight], 1)
    pack = jnp.concatenate(
        [keyval_weight, chooser, selector, flat, jnp.zeros((flat.shape[0], 91), bf16)], 1
    )
    inputs = dict(
        states=states[0],
        cotangent=out_cotangent[0],
        head_ids=moa_ids[0],
        route_ids=ffn_ids[0],
        remaining=remaining,
        left_cot=left_cotangent,
        pack=pack,
        query_part=query_weight,
        project_part=project_weight,
        inner_part=expert_in,
        outer_part=expert_out,
    )
    in_place = ("query_part", "project_part", "inner_part", "outer_part")
    shape = jax.ShapeDtypeStruct
    outputs = dict(
        new_states=shape((tokens, D), bf16),
        rows_out=shape((8, tokens), f32),
        grad_states=shape((tokens, D), f32),
        grad_query=shape((64, wide), bf16),
        grad_project=shape((192, D), bf16),
        grad_small=shape((64, 256), bf16),
        grad_inner=shape((EXP_DEV, 64, FF), bf16),
        grad_outer=shape((EXP_DEV, 256, D), bf16),
    )
    vmem, dma = pltpu.VMEM, pltpu.SemaphoreType.DMA
    scratch = dict(
        slot_rows=vmem((EXP_DEV, rows, D), bf16),
        active=vmem((EXP_DEV, rows, FF), bf16),
        slope=vmem((EXP_DEV, rows, FF), bf16),
        result=vmem((EXP_DEV, rows, D), bf16),
        slot_cot=vmem((EXP_DEV, rows, D), bf16),
        inner=vmem((EXP_DEV, D, FF), bf16),
        outer=vmem((EXP_DEV, FF, D), bf16),
        query=vmem((D, wide), bf16),
        project=vmem((wide, D), bf16),
        packed=vmem((D, 256), bf16),
        acted=vmem((tokens, D), bf16),
        mixture=vmem((tokens, wide), bf16),
        queries=vmem((MOA_TOP * tokens, 128), bf16),
        heads=vmem((MOA_TOP * tokens, 128), f32),
        keyval=vmem((length * tokens, 128), bf16),
        head_gates=vmem((tokens, 128), f32),
        middle=vmem((tokens, D), f32),
        entering=vmem((length, tokens, D), bf16),
        cots=vmem((length, tokens, D), bf16),
        routes=vmem((length, 16, tokens), f32),
        scores_back=vmem((length, 8, tokens), f32),
        small=vmem((128, D), f32),
        score_sent=vmem((length, 8, tokens), f32),
        factors=vmem((length, 8, tokens), f32),
        columns=vmem((tokens, 128), f32),
        pick_grads=vmem((16, tokens), bf16),
        gsmall=vmem((128, D), f32),
        flow=vmem((tokens, D), f32),
        slot_back=vmem((EXP_DEV, CAP, D), bf16),
        back_in=vmem((length - 1, tokens, D), bf16),
        mix_in=vmem((length - 1, tokens, D), bf16),
        half_in=vmem((2, EXP_DEV, 128, FF), bf16),
        half_out=vmem((2, EXP_DEV, 512, D), bf16),
        side_in=vmem((EXP_DEV, 128, FF), bf16),
        side_out=vmem((2, EXP_DEV, 256, D), bf16),
        last_in=vmem((EXP_DEV, 64, FF), bf16),
        last_out=vmem((EXP_DEV, 256, D), bf16),
        heads_grad=vmem((MOA_TOP * tokens, 128), bf16),
        stats=vmem((8, MOA_TOP * tokens), f32),
        acted_grad=vmem((tokens, D), f32),
        kv_grad=vmem((length * tokens, 128), f32),
        kv_in=vmem((length - 1, tokens, 128), bf16),
        project_half=vmem((2, 384, D), bf16),
        project_in=vmem((3, 192, D), bf16),
        query_half=vmem((2, 128, wide), bf16),
        query_in=vmem((3, 64, wide), bf16),
        small_half=vmem((2, 128, 256), bf16),
        small_in=vmem((3, 64, 256), bf16),
        project_value=vmem((192, D), bf16),
        project_parts=vmem((length - 1, 192 // length, D), bf16),
        project_sum=vmem((192, D), bf16),
        query_value=vmem((64, wide), bf16),
        query_parts=vmem((length - 1, 64 // length, wide), bf16),
        query_sum=vmem((64, wide), bf16),
        small_value=vmem((64, 256), bf16),
        small_parts=vmem((length - 1, 64 // length, 256), bf16),
        small_sum=vmem((64, 256), bf16),
        plane_send=dma((5, 9)),
        plane_recv=dma((5, 9)),
        plane_local=dma((5,)),
        line_send=dma((2, 2, length)),
        line_recv=dma((2, 2, length)),
        direct_sems=dma((13, length)),
        direct_recvs=dma((13, length)),
        expert_send=dma((9,)),
        expert_recv=dma((9,)),
        dense_send=dma((3, 5)),
        dense_recv=dma((3, 5)),
    )
    in_vmem = pl.BlockSpec(memory_space=pltpu.VMEM)
    anywhere = pl.BlockSpec(memory_space=pl.ANY)
    names = (*inputs, *outputs, *scratch)
    results = pl.pallas_call(
        partial(whole_kernel, length, names),
        out_shape=tuple(outputs.values()),
        in_specs=[anywhere if name in in_place else in_vmem for name in inputs],
        out_specs=[in_vmem] * len(outputs),
        scratch_shapes=list(scratch.values()),
        compiler_params=pltpu.CompilerParams(
            collective_id=0, has_side_effects=True, vmem_limit_bytes=LIMIT_MIB * 2**20
        ),
        name="layer_step",
    )(*inputs.values())
    o = SimpleNamespace(**dict(zip(outputs, results)))
    small = o.grad_small.astype(f32)
    return (
        o.new_states[None],
        o.rows_out[0:1],
        o.grad_states[None],
        o.rows_out[1:2],
        o.grad_query.astype(f32),
        small[:, 0:128],
        o.grad_project.astype(f32),
        small[:, 128:152],
        small[:, 152:160],
        small[:, 160],
        small[:, 161],
        small[:, 162],
        small[:, 163],
        small[:, 164],
        o.grad_inner.astype(f32),
        o.grad_outer.astype(f32),
    )


def solution(mesh):
    in_specs = (
        P(("seq", "wsh"), "ctx", None),
        P(("seq", "wsh"), "ctx"),
        P(("seq", "wsh"), "ctx", None),
        P(("seq", "wsh"), "ctx", None),
        P(("seq", "wsh"), "ctx", None),
        P(("seq", "wsh"), "ctx"),
        P(("seq", "wsh"), None),
        P(("seq", "wsh"), None),
        P(("seq", "wsh"), None),
        P(("seq", "wsh"), None),
        P(("seq", "wsh"), None),
        P(("seq", "wsh")),
        P(("seq", "wsh")),
        P(("seq", "wsh")),
        P(("seq", "wsh")),
        P(("seq", "wsh")),
        P("ctx", ("seq", "wsh"), None),
        P("ctx", ("seq", "wsh"), None),
    )
    out_specs = (
        P(("seq", "wsh"), "ctx", None),
        P(("seq", "wsh"), "ctx"),
        P(("seq", "wsh"), "ctx", None),
        P(("seq", "wsh"), "ctx"),
        P(("seq", "wsh"), None),
        P(("seq", "wsh"), None),
        P(("seq", "wsh"), None),
        P(("seq", "wsh"), None),
        P(("seq", "wsh"), None),
        P(("seq", "wsh")),
        P(("seq", "wsh")),
        P(("seq", "wsh")),
        P(("seq", "wsh")),
        P(("seq", "wsh")),
        P("ctx", ("seq", "wsh"), None),
        P("ctx", ("seq", "wsh"), None),
    )
    body = fast_body if mesh.shape["ctx"] == 4 else general_body
    return jax.shard_map(body, mesh=mesh, in_specs=in_specs, out_specs=out_specs, check_vma=False)
```

```python
from functools import partial
from types import SimpleNamespace

import jax
import jax.numpy as jnp
from jax import lax
from jax.experimental import pallas as pl
from jax.experimental.pallas import tpu as pltpu
from jax.sharding import PartitionSpec as P

D = 512
HS = 64
MOA_EXPERTS = 24
MOA_TOP = 4
EXP_DEV = 2
FFN_TOP = 2
FF = 2048


EPS = 1e-05
HIGH = lax.Precision.HIGHEST


def shifted(x, axis, by):
    length = lax.axis_size(axis)
    return lax.ppermute(x, axis, [(i, (i + by) % length) for i in range(length)])


def layer_norm(values, gain, bias):
    centred = values - jnp.mean(values, -1, keepdims=True)
    inverse = lax.rsqrt(jnp.mean(centred * centred, -1, keepdims=True) + EPS)
    normal = centred * inverse
    return (normal * gain + bias, normal, inverse)


def norm_back(incoming, normal, inverse, gain):
    scaled = incoming * gain
    inner_term = (
        scaled
        - jnp.mean(scaled, -1, keepdims=True)
        - normal * jnp.mean(scaled * normal, -1, keepdims=True)
    )
    return (inverse * inner_term, jnp.sum(incoming * normal, 0), jnp.sum(incoming, 0))


def one_hot(index, count):
    return (index[..., None] == jnp.arange(count, dtype=jnp.int32)).astype(jnp.float32)


def choose_back(gates, upstream):
    return gates * (upstream - jnp.sum(gates * upstream, -1, keepdims=True))


def block_rows(row_count):
    if row_count > 512 and row_count % 512 == 0:
        return 512
    return row_count


def expert_slots(route_ids, experts):
    flat_ids = route_ids.reshape(-1)
    table = (flat_ids[:, None] == jnp.arange(experts, dtype=jnp.int32)[None, :]).astype(jnp.float32)
    place = jnp.arange(flat_ids.shape[0], dtype=jnp.int32)
    before = (place[None, :] < place[:, None]).astype(jnp.bfloat16)
    earlier = jnp.dot(before, table.astype(jnp.bfloat16), preferred_element_type=jnp.float32)
    return jnp.sum(earlier * table, 1).astype(jnp.int32).reshape(route_ids.shape)


def general_body(
    states,
    remaining,
    moa_ids,
    ffn_ids,
    out_cotangent,
    left_cotangent,
    query_weight,
    keyval_weight,
    project_weight,
    chooser,
    selector,
    gain_one,
    bias_one,
    gain_two,
    bias_two,
    halt_weight,
    expert_in,
    expert_out,
):
    tokens = states.shape[1]
    devices = lax.axis_size("ctx")
    experts = EXP_DEV * devices
    capacity = max(2, (4 * tokens + experts - 1) // experts)
    rows_total = tokens * MOA_TOP
    scaling = HS ** (-0.5)
    f32 = jnp.float32
    bf16 = jnp.bfloat16
    (
        query_full,
        keyval_full,
        project_full,
        chooser_full,
        selector_full,
        gainone_full,
        biasone_full,
        gaintwo_full,
        biastwo_full,
        halt_full,
    ) = (
        lax.all_gather(query_weight, ("seq", "wsh"), axis=0, tiled=True),
        lax.all_gather(keyval_weight, ("seq", "wsh"), axis=0, tiled=True),
        lax.all_gather(project_weight, ("seq", "wsh"), axis=0, tiled=True),
        lax.all_gather(chooser, ("seq", "wsh"), axis=0, tiled=True),
        lax.all_gather(selector, ("seq", "wsh"), axis=0, tiled=True),
        lax.all_gather(gain_one, ("seq", "wsh"), axis=0, tiled=True),
        lax.all_gather(bias_one, ("seq", "wsh"), axis=0, tiled=True),
        lax.all_gather(gain_two, ("seq", "wsh"), axis=0, tiled=True),
        lax.all_gather(bias_two, ("seq", "wsh"), axis=0, tiled=True),
        lax.all_gather(halt_weight, ("seq", "wsh"), axis=0, tiled=True),
    )
    inner_full, outer_full = (
        lax.all_gather(expert_in, ("seq", "wsh"), axis=1, tiled=True),
        lax.all_gather(expert_out, ("seq", "wsh"), axis=1, tiled=True),
    )
    gain_first = gainone_full.astype(f32)
    gain_second = gaintwo_full.astype(f32)
    halt_vector = halt_full.astype(f32)
    resident = states[0].astype(f32)
    normed_one, normal_one, inverse_one = layer_norm(resident, gain_first, biasone_full.astype(f32))
    acted = normed_one.astype(bf16)
    query_all = (
        jnp.dot(acted, query_full, preferred_element_type=f32)
        .astype(bf16)
        .reshape(tokens, MOA_EXPERTS, HS)
    )
    head_ids = moa_ids[0]
    query_sel = jnp.take_along_axis(query_all, head_ids[:, :, None], axis=1).reshape(rows_total, HS)
    keyval = jnp.dot(acted, keyval_full, preferred_element_type=f32).astype(bf16)
    chosen = one_hot(head_ids, MOA_EXPERTS)
    head_logits = jnp.sum(
        chosen * jnp.dot(acted, chooser_full, preferred_element_type=f32)[:, None, :], -1
    )
    head_gates = jax.nn.softmax(head_logits, -1)
    start_state = (
        jnp.full((rows_total,), -1e30, f32),
        jnp.zeros((rows_total,), f32),
        jnp.zeros((rows_total, HS), f32),
    )
    running = start_state
    shard_rows = lax.all_gather(keyval, "ctx", axis=0, tiled=True)
    block_size = block_rows(shard_rows.shape[0])
    grouped = shard_rows.reshape(shard_rows.shape[0] // block_size, block_size, 2 * HS)

    def absorb(carried, key_block):
        row_peak, row_total, gathered = carried
        scores = jnp.dot(query_sel, key_block[:, :HS].T, preferred_element_type=f32) * scaling
        new_peak = jnp.maximum(row_peak, jnp.max(scores, -1))
        fading = jnp.exp(row_peak - new_peak)
        weights = jnp.exp(scores - new_peak[:, None])
        row_total = row_total * fading + jnp.sum(weights, -1)
        gathered = gathered * fading[:, None] + jnp.dot(
            weights.astype(bf16), key_block[:, HS:], preferred_element_type=f32
        )
        return ((new_peak, row_total, gathered), None)

    running, unused = lax.scan(absorb, running, grouped)
    row_peak, row_total, gathered = running
    heads_out = gathered / row_total[:, None]
    log_total = row_peak + jnp.log(row_total)
    heads_view = heads_out.reshape(tokens, MOA_TOP, HS)
    mixed_sel = (head_gates[:, :, None] * heads_view).astype(bf16)
    chosen_low = chosen.astype(bf16)
    mixture = jnp.sum(chosen_low[:, :, :, None] * mixed_sel[:, :, None, :], 1).reshape(
        tokens, MOA_EXPERTS * HS
    )
    middle = resident + jnp.dot(mixture, project_full, preferred_element_type=f32)
    normed_two, normal_two, inverse_two = layer_norm(middle, gain_second, biastwo_full.astype(f32))
    entering = normed_two.astype(bf16)
    route_ids = ffn_ids[0]
    picked = one_hot(route_ids, experts)
    expert_logits = jnp.sum(
        picked * jnp.dot(entering, selector_full, preferred_element_type=f32)[:, None, :], -1
    )
    expert_gates = jax.nn.softmax(expert_logits, -1)
    slots = expert_slots(route_ids, experts)
    target = (route_ids * capacity + slots).reshape(-1)
    copies = jnp.broadcast_to(entering[:, None, :], (tokens, FFN_TOP, D)).reshape(-1, D)
    outgoing = (
        jnp.zeros((experts * capacity, D), bf16)
        .at[target]
        .set(copies)
        .reshape(devices, EXP_DEV, capacity, D)
    )
    arrived_rows = lax.all_to_all(outgoing, "ctx", split_axis=0, concat_axis=0, tiled=True)
    before = jnp.einsum("nekd,edf->nekf", arrived_rows, inner_full, preferred_element_type=f32)
    activated = jax.nn.gelu(before, approximate=False).astype(bf16)
    result_rows = jnp.einsum(
        "nekf,efd->nekd", activated, outer_full, preferred_element_type=f32
    ).astype(bf16)
    returned = lax.all_to_all(result_rows, "ctx", split_axis=0, concat_axis=0, tiled=True).reshape(
        experts * capacity, D
    )
    expert_rows = returned[target].reshape(tokens, FFN_TOP, D).astype(f32)
    final = middle + jnp.sum(expert_gates[:, :, None] * expert_rows, 1)
    halting = jax.nn.sigmoid(jnp.dot(final, halt_vector, precision=HIGH))
    left_mass = remaining[0]
    stopped = left_mass * halting
    new_states = (stopped[:, None] * resident + (1.0 - stopped)[:, None] * final).astype(bf16)
    remaining_next = left_mass * (1.0 - halting)
    out_grad = out_cotangent[0]
    left_grad = left_cotangent[0]
    stop_grad = jnp.sum(out_grad * (resident - final), -1)
    grad_remaining = stop_grad * halting + left_grad * (1.0 - halting)
    halt_logit_grad = (stop_grad - left_grad) * left_mass * halting * (1.0 - halting)
    grad_halt = jnp.sum(halt_logit_grad[:, None] * final, 0)
    grad_final = (1.0 - stopped)[:, None] * out_grad + halt_logit_grad[:, None] * halt_vector
    gate_grad = jnp.sum(grad_final[:, None, :] * expert_rows, -1)
    selector_logit_grad = jnp.sum(choose_back(expert_gates, gate_grad)[:, :, None] * picked, 1)
    entering_wide = entering.astype(f32)
    grad_selector = jnp.dot(entering_wide.T, selector_logit_grad, precision=HIGH)
    rows_grad = (expert_gates[:, :, None] * grad_final[:, None, :]).astype(bf16).reshape(-1, D)
    grad_outgoing = (
        jnp.zeros((experts * capacity, D), bf16)
        .at[target]
        .set(rows_grad)
        .reshape(devices, EXP_DEV, capacity, D)
    )
    grad_arrived = lax.all_to_all(grad_outgoing, "ctx", split_axis=0, concat_axis=0, tiled=True)
    grad_activated = jnp.einsum(
        "nekd,efd->nekf", grad_arrived, outer_full, preferred_element_type=f32
    )
    activated_again, gelu_back = jax.vjp(partial(jax.nn.gelu, approximate=False), before)
    before_grad = gelu_back(grad_activated)[0].astype(bf16)
    outer_grad = jnp.einsum(
        "nekf,nekd->efd", activated_again.astype(bf16), grad_arrived, preferred_element_type=f32
    )
    inner_grad = jnp.einsum("nekd,nekf->edf", arrived_rows, before_grad, preferred_element_type=f32)
    grad_sent = jnp.einsum(
        "nekf,edf->nekd", before_grad, inner_full, preferred_element_type=f32
    ).astype(bf16)
    grad_back = lax.all_to_all(grad_sent, "ctx", split_axis=0, concat_axis=0, tiled=True).reshape(
        experts * capacity, D
    )
    entering_grad = jnp.sum(grad_back[target].reshape(tokens, FFN_TOP, D).astype(f32), 1)
    entering_grad = entering_grad + jnp.dot(
        selector_logit_grad, selector_full.astype(f32).T, precision=HIGH
    )
    middle_extra, grad_gain_two, grad_bias_two = norm_back(
        entering_grad, normal_two, inverse_two, gain_second
    )
    middle_grad = grad_final + middle_extra
    attn_grad = middle_grad.astype(bf16)
    grad_project = jnp.dot(mixture.T, attn_grad, preferred_element_type=f32)
    mix_grad = jnp.dot(attn_grad, project_full.T, preferred_element_type=f32).reshape(
        tokens, MOA_EXPERTS, HS
    )
    mix_sel_grad = jnp.take_along_axis(mix_grad, head_ids[:, :, None], axis=1)
    head_gate_grad = jnp.sum(mix_sel_grad * heads_view, -1)
    chooser_logit_grad = jnp.sum(choose_back(head_gates, head_gate_grad)[:, :, None] * chosen, 1)
    acted_wide = acted.astype(f32)
    grad_chooser = jnp.dot(acted_wide.T, chooser_logit_grad, precision=HIGH)
    acted_grad = jnp.dot(chooser_logit_grad, chooser_full.astype(f32).T, precision=HIGH)
    heads_grad = (head_gates[:, :, None] * mix_sel_grad).astype(bf16).reshape(rows_total, HS)
    row_delta = jnp.sum(heads_grad.astype(f32) * heads_out, -1)

    def cycle_turn(turn_index, carried):
        visiting, grads_visiting, query_grad = carried
        block_size = block_rows(tokens)

        def per_block(query_acc, key_block):
            scores = jnp.dot(query_sel, key_block[:, :HS].T, preferred_element_type=f32) * scaling
            probability = jnp.exp(scores - log_total[:, None])
            prob_grad = jnp.dot(heads_grad, key_block[:, HS:].T, preferred_element_type=f32)
            score_grad = (probability * (prob_grad - row_delta[:, None])).astype(bf16)
            query_acc = (
                query_acc
                + jnp.dot(score_grad, key_block[:, :HS], preferred_element_type=f32) * scaling
            )
            keys_grad = jnp.dot(score_grad.T, query_sel, preferred_element_type=f32) * scaling
            values_grad = jnp.dot(
                probability.astype(bf16).T, heads_grad, preferred_element_type=f32
            )
            return (query_acc, jnp.concatenate([keys_grad, values_grad], -1))

        query_grad, block_grads = lax.scan(
            per_block, query_grad, visiting.reshape(tokens // block_size, block_size, 2 * HS)
        )
        grads_visiting = grads_visiting + block_grads.reshape(tokens, 2 * HS)
        visiting = shifted(visiting, "ctx", 1)
        grads_visiting = shifted(grads_visiting.astype(jnp.bfloat16), "ctx", 1).astype(
            grads_visiting.dtype
        )
        return (visiting, grads_visiting, query_grad)

    cycle_state = (keyval, jnp.zeros((tokens, 2 * HS), f32), jnp.zeros((rows_total, HS), f32))
    unused_keys, keyval_grad, query_grad = lax.fori_loop(0, devices, cycle_turn, cycle_state)
    query_sel_grad = query_grad.astype(bf16).reshape(tokens, MOA_TOP, HS)
    query_all_grad = jnp.sum(chosen_low[:, :, :, None] * query_sel_grad[:, :, None, :], 1).reshape(
        tokens, MOA_EXPERTS * HS
    )
    keyval_low = keyval_grad.astype(bf16)
    grad_query = jnp.dot(acted.T, query_all_grad, preferred_element_type=f32)
    grad_keyval = jnp.dot(acted.T, keyval_low, preferred_element_type=f32)
    acted_grad = acted_grad + jnp.dot(query_all_grad, query_full.T, preferred_element_type=f32)
    acted_grad = acted_grad + jnp.dot(keyval_low, keyval_full.T, preferred_element_type=f32)
    resident_grad, grad_gain_one, grad_bias_one = norm_back(
        acted_grad, normal_one, inverse_one, gain_first
    )
    grad_states = middle_grad + resident_grad + stopped[:, None] * out_grad
    dense_grads = (
        grad_query,
        grad_keyval,
        grad_project,
        grad_chooser,
        grad_selector,
        grad_gain_one,
        grad_bias_one,
        grad_gain_two,
        grad_bias_two,
        grad_halt,
    )
    totals = (
        lax.psum(dense_grads[0].astype(jnp.bfloat16), "ctx").astype(jnp.float32),
        lax.psum(dense_grads[1].astype(jnp.bfloat16), "ctx").astype(jnp.float32),
        lax.psum(dense_grads[2].astype(jnp.bfloat16), "ctx").astype(jnp.float32),
        lax.psum(dense_grads[3].astype(jnp.bfloat16), "ctx").astype(jnp.float32),
        lax.psum(dense_grads[4].astype(jnp.bfloat16), "ctx").astype(jnp.float32),
        lax.psum(dense_grads[5].astype(jnp.bfloat16), "ctx").astype(jnp.float32),
        lax.psum(dense_grads[6].astype(jnp.bfloat16), "ctx").astype(jnp.float32),
        lax.psum(dense_grads[7].astype(jnp.bfloat16), "ctx").astype(jnp.float32),
        lax.psum(dense_grads[8].astype(jnp.bfloat16), "ctx").astype(jnp.float32),
        lax.psum(dense_grads[9].astype(jnp.bfloat16), "ctx").astype(jnp.float32),
    )
    shards = (
        lax.psum_scatter(
            totals[0].astype(jnp.bfloat16), ("seq", "wsh"), scatter_dimension=0, tiled=True
        ).astype(jnp.float32),
        lax.psum_scatter(
            totals[1].astype(jnp.bfloat16), ("seq", "wsh"), scatter_dimension=0, tiled=True
        ).astype(jnp.float32),
        lax.psum_scatter(
            totals[2].astype(jnp.bfloat16), ("seq", "wsh"), scatter_dimension=0, tiled=True
        ).astype(jnp.float32),
        lax.psum_scatter(
            totals[3].astype(jnp.bfloat16), ("seq", "wsh"), scatter_dimension=0, tiled=True
        ).astype(jnp.float32),
        lax.psum_scatter(
            totals[4].astype(jnp.bfloat16), ("seq", "wsh"), scatter_dimension=0, tiled=True
        ).astype(jnp.float32),
        lax.psum_scatter(
            totals[5].astype(jnp.bfloat16), ("seq", "wsh"), scatter_dimension=0, tiled=True
        ).astype(jnp.float32),
        lax.psum_scatter(
            totals[6].astype(jnp.bfloat16), ("seq", "wsh"), scatter_dimension=0, tiled=True
        ).astype(jnp.float32),
        lax.psum_scatter(
            totals[7].astype(jnp.bfloat16), ("seq", "wsh"), scatter_dimension=0, tiled=True
        ).astype(jnp.float32),
        lax.psum_scatter(
            totals[8].astype(jnp.bfloat16), ("seq", "wsh"), scatter_dimension=0, tiled=True
        ).astype(jnp.float32),
        lax.psum_scatter(
            totals[9].astype(jnp.bfloat16), ("seq", "wsh"), scatter_dimension=0, tiled=True
        ).astype(jnp.float32),
    )
    inner_shard, outer_shard = (
        lax.psum_scatter(
            inner_grad.astype(jnp.bfloat16), ("seq", "wsh"), scatter_dimension=1, tiled=True
        ).astype(jnp.float32),
        lax.psum_scatter(
            outer_grad.astype(jnp.bfloat16), ("seq", "wsh"), scatter_dimension=1, tiled=True
        ).astype(jnp.float32),
    )
    return (
        new_states[None],
        remaining_next[None],
        grad_states[None],
        grad_remaining[None],
        shards[0],
        shards[1],
        shards[2],
        shards[3],
        shards[4],
        shards[5],
        shards[6],
        shards[7],
        shards[8],
        shards[9],
        inner_shard,
        outer_shard,
    )


MESH = pl.DeviceIdType.MESH
CAP = 192
LIMIT_MIB = 63
KEEP = 0.7071067811865476
SPREAD = 0.3989422804014327
ERF_P = 0.3275911
ERF_A = (0.254829592, -0.284496736, 1.421413741, -1.453152027, 1.061405429)


def remote(source, target, send_sem, recv_sem, device):
    return pltpu.make_async_remote_copy(
        src_ref=source,
        dst_ref=target,
        send_sem=send_sem,
        recv_sem=recv_sem,
        device_id=device,
        device_id_type=MESH,
    )


def places():
    ctx, seq, wsh = (lax.axis_index(name) for name in ("ctx", "seq", "wsh"))
    chip, core = seq // 2, seq % 2
    over = (1 - chip) * 2 + core
    twin = (ctx, chip * 2 + 1 - core, wsh)
    beside = (ctx, over, wsh)
    above = (ctx, seq, 1 - wsh)
    across = (ctx, over, 1 - wsh)
    return (ctx, seq, wsh), twin, beside, above, across


def shard_of(place):
    return place[1] * 2 + place[2]


def moved(place, offset, length):
    return ((place[0] + offset) % length, place[1], place[2])


def plane_peer(place, step):
    shard = (shard_of(place) + step) % 8
    return (place[0], shard // 2, shard % 2)


class PlaneGather:
    def __init__(self, shard, full, halves, send, recv, local):
        self.shard, self.full, self.halves = shard, full, halves
        self.send, self.recv, self.local = send, recv, local
        self.me, self.twin, self.beside, self.above, self.across = places()

    def pair(self, view, slot, device):
        return remote(view, view, self.send.at[slot], self.recv.at[slot], device)

    def own(self, slot, device):
        target = self.full(shard_of(self.me))
        return remote(self.shard, target, self.send.at[slot], self.recv.at[slot], device)

    def keep(self):
        return pltpu.make_async_copy(self.shard, self.full(shard_of(self.me)), self.local)

    def start(self):
        self.own(0, self.twin).start()
        self.own(1, self.beside).start()
        self.own(2, self.above).start()
        if self.halves is None:
            self.own(3, self.across).start()
        self.keep().start()

    def arrive(self, slot, place):
        self.pair(self.full(shard_of(place)), slot, self.twin).wait_recv()

    def relay(self):
        if self.halves is None:
            for slot, place in ((1, self.beside), (2, self.above), (3, self.across)):
                self.arrive(slot, place)
                self.pair(self.full(shard_of(place)), slot + 3, self.twin).start()
            return
        self.arrive(1, self.beside)
        self.pair(self.halves(shard_of(self.beside), 1), 7, self.above).start()
        self.pair(self.full(shard_of(self.beside)), 4, self.twin).start()
        self.arrive(2, self.above)
        self.pair(self.halves(shard_of(self.above), 0), 3, self.beside).start()
        self.pair(self.full(shard_of(self.above)), 5, self.twin).start()

    def relay_rest(self):
        shard = shard_of(self.across)
        for slot, half in ((3, 0), (7, 1)):
            view = self.halves(shard, half)
            self.pair(view, slot, self.twin).wait_recv()
            self.pair(view, 6 if half == 0 else 8, self.twin).start()

    def finish(self):
        self.keep().wait()
        ctx, seq, wsh = self.twin
        over = (1 - seq // 2) * 2 + seq % 2
        self.arrive(0, self.twin)
        self.arrive(4, (ctx, over, wsh))
        self.arrive(5, (ctx, seq, 1 - wsh))
        rest = shard_of((ctx, over, 1 - wsh))
        if self.halves is None:
            self.pair(self.full(rest), 6, self.twin).wait_recv()
        else:
            self.pair(self.halves(rest, 0), 6, self.twin).wait_recv()
            self.pair(self.halves(rest, 1), 8, self.twin).wait_recv()

    def drain(self):
        self.own(0, self.twin).wait_send()
        self.own(1, self.beside).wait_send()
        self.own(2, self.above).wait_send()
        beside, above, across = (shard_of(p) for p in (self.beside, self.above, self.across))
        self.pair(self.full(beside), 4, self.twin).wait_send()
        self.pair(self.full(above), 5, self.twin).wait_send()
        if self.halves is None:
            self.own(3, self.across).wait_send()
            self.pair(self.full(across), 6, self.twin).wait_send()
        else:
            self.pair(self.halves(above, 0), 3, self.beside).wait_send()
            self.pair(self.halves(beside, 1), 7, self.above).wait_send()
            self.pair(self.halves(across, 0), 6, self.twin).wait_send()
            self.pair(self.halves(across, 1), 8, self.twin).wait_send()


class PlaneShare:
    def __init__(self, blocks, send, recv):
        self.blocks, self.send, self.recv = blocks, send, recv
        self.me = places()[0]
        self.shard = shard_of(self.me)

    def copy(self, shard, step, device):
        view = self.blocks.at[shard]
        return remote(view, view, self.send.at[step - 1], self.recv.at[step - 1], device)

    def sends(self):
        return [self.copy(self.shard, step, plane_peer(self.me, step)) for step in range(1, 8)]

    def wait(self):
        for step in range(1, 8):
            source = plane_peer(self.me, 8 - step)
            self.copy(shard_of(source), step, source).wait_recv()


class LineGather:
    def __init__(self, length, blocks, send, recv):
        self.length, self.blocks, self.send, self.recv = length, blocks, send, recv
        self.me = places()[0]

    def hop(self, block, way, step, device):
        view = self.blocks(block)
        return remote(view, view, self.send.at[way, step], self.recv.at[way, step], device)

    def ways(self, step):
        ctx = self.me[0]
        left = (ctx - 1, self.me[1], self.me[2])
        right = (ctx + 1, self.me[1], self.me[2])
        return (
            (0, ctx - step, ctx - step >= 0, right, ctx + 1 < self.length),
            (1, ctx + step, ctx + step < self.length, left, ctx - 1 >= 0),
        )

    def start(self):
        for way, block, unused, device, there in self.ways(0):
            pl.when(there)(lambda b=block, w=way, d=device: self.hop(b, w, 0, d).start())

    def relay(self, step):
        for way, block, come, device, there in self.ways(step):

            def pass_on(way=way, block=block, device=device, there=there):
                self.hop(block, way, step - 1, device).wait_recv()
                if step < self.length - 1:
                    pl.when(there)(lambda: self.hop(block, way, step, device).start())

            pl.when(come)(pass_on)

    def drain(self):
        for step in range(self.length - 1):
            for way, block, come, device, there in self.ways(step):
                pl.when(jnp.logical_and(come, there))(
                    lambda b=block, w=way, d=device, s=step: self.hop(b, w, s, d).wait_send()
                )


def direct_send(view, send, recv, length):
    me = places()[0]
    return [
        remote(view, view, send.at[step - 1], recv.at[step - 1], moved(me, step, length))
        for step in range(1, length)
    ]


def direct_wait(view_of, send, recv, length):
    me = places()[0]
    for step in range(1, length):
        source = moved(me, length - step, length)
        view = view_of(source[0])
        remote(view, view, send.at[step - 1], recv.at[step - 1], source).wait_recv()


def lanes_of(shape):
    return lax.broadcasted_iota(jnp.int32, shape, 1)


def rows_of(shape):
    return lax.broadcasted_iota(jnp.int32, shape, 0)


def product(left, right, dims=((1,), (0,))):
    return lax.dot_general(left, right, (dims, ((), ())), preferred_element_type=jnp.float32)


def gelu_parts(values):
    near = jnp.abs(values) * KEEP
    turn = 1.0 / (1.0 + ERF_P * near)
    bell = jnp.exp(-near * near)
    series = ERF_A[4]
    for term in ERF_A[3::-1]:
        series = series * turn + term
    tail = 0.5 * series * turn * bell
    share = jnp.where(values >= 0, 1.0 - tail, tail)
    return values * share, share + values * bell * SPREAD


def picks(r, block, expert):
    tokens = r.states.shape[0]
    row = r.routes[block, pl.ds(EXP_DEV * lax.axis_index("ctx") + expert, 1), :]
    return (rows_of((CAP, tokens)).astype(jnp.float32) == row).astype(jnp.float32)


def slots(block):
    return pl.ds(pl.multiple_of(block * CAP, CAP), CAP)


def to_owner(length, r, view, target, row, block):
    me = places()[0]
    slot = (block - me[0] + length) % length - 1
    send, recv = r.direct_sems.at[row, slot], r.direct_recvs.at[row, slot]
    return remote(view, target.at[slot], send, recv, (block, me[1], me[2]))


def give_back(length, r, block):
    total = 0.0
    for expert in range(EXP_DEV):
        chosen = picks(r, block, expert).astype(jnp.bfloat16)
        total = total + product(chosen, r.result[expert, slots(block), :], ((0,), (0,)))
    r.cots[block] = total.astype(jnp.bfloat16)


def returns(length, r):
    return (
        LineReturn(length, r.cots, r.mix_in, r.return_send.at[0], r.return_recv.at[0]),
        LineReturn(length, r.entering, r.back_in, r.return_send.at[1], r.return_recv.at[1]),
    )


def forward_part(length, r):
    f32, bf16 = jnp.float32, jnp.bfloat16
    tokens = r.states.shape[0]
    me, twin, beside, above, across = places()
    ctx = me[0]
    peers = [plane_peer(me, k) for k in range(1, 8)] + [moved(me, k, length) for k in range(1, length)]
    barrier = pltpu.get_barrier_semaphore()
    for peer in peers:
        pl.semaphore_signal(barrier, inc=1, device_id=peer, device_id_type=MESH)

    def gather(index, shard, full, halves=None):
        return PlaneGather(
            shard, full, halves, r.plane_send.at[index], r.plane_recv.at[index], r.plane_local.at[index]
        )

    def rows_view(ref, rows):
        return lambda shard: ref.at[pl.ds(shard * rows, rows), :]

    def half_view(ref, rows):
        return lambda shard, half: ref.at[pl.ds(shard * rows + half * (rows // 2), rows // 2), :]

    pack_share = PlaneShare(r.packs, r.pack_send, r.pack_recv)
    query_gather = gather(0, r.query_part, rows_view(r.query, 64), half_view(r.query, 64))
    project_gather = gather(1, r.project_part, rows_view(r.project, 192), half_view(r.project, 192))
    inner_gather = gather(
        2,
        r.inner_part,
        lambda shard: r.inner.at[:, pl.ds(shard * 64, 64), :],
        lambda shard, half: r.inner.at[half, pl.ds(shard * 64, 64), :],
    )
    outer_gathers = [
        gather(
            3 + k, r.outer_part.at[k], rows_view(r.outer.at[k], 256), half_view(r.outer.at[k], 256)
        )
        for k in range(EXP_DEV)
    ]
    cot_gather = LineGather(length, lambda b: r.cots.at[b], r.line_send.at[0], r.line_recv.at[0])
    entering_gather = LineGather(length, lambda b: r.entering.at[b], r.line_send.at[1], r.line_recv.at[1])

    def keyval_view(block):
        return r.keyval.at[pl.ds(block * tokens, tokens), :]

    fetch = pltpu.make_async_copy(r.cotangent_part, r.cotangent, r.plane_local.at[5])
    fetch.start()
    shard = shard_of(me)
    r.packs[shard, 0:64, :] = r.keyval_part[...]
    rows = [r.chooser_part[...].astype(f32), r.selector_part[...].astype(f32), r.vectors[...].astype(f32)]
    rows = jnp.concatenate([*rows, jnp.zeros((8, 64), f32)], 0)
    r.packs[shard, 64:112, :] = jnp.concatenate([rows, jnp.zeros((48, 64), f32)], 1).astype(bf16)
    pl.semaphore_wait(barrier, len(peers))
    pack_sends = pack_share.sends()
    for copy in pack_sends:
        copy.start()
    query_gather.start()
    project_gather.start()
    fetch.wait()
    r.cots[ctx] = r.cotangent[...].astype(bf16)
    cot_gather.start()

    values = r.states[...].astype(f32)
    centred = values - jnp.mean(values, -1, keepdims=True)
    inverse = lax.rsqrt(jnp.mean(centred * centred, -1, keepdims=True) + EPS)
    r.flow[...] = centred * inverse

    lane = lanes_of((tokens, 128))
    turned = r.route_ids[...].astype(f32)
    expert_row = rows_of((8, tokens)).astype(f32)
    picked = jnp.logical_or(expert_row == turned[0:1], expert_row == turned[1:2])
    marks = jnp.concatenate([picked.astype(f32), jnp.zeros((8, tokens), f32)], 0).astype(bf16)
    earlier = (rows_of((tokens, tokens)) < lanes_of((tokens, tokens))).astype(f32).astype(bf16)
    ranks = product(marks, earlier)[0:8]
    r.routes[ctx, 0:8, :] = jnp.where(picked, ranks, -1.0)

    ids = jnp.concatenate([r.head_ids[...].astype(f32), jnp.zeros((124, tokens), f32)], 0)
    r.id_columns[...] = jnp.transpose(ids).astype(jnp.int32)
    r.small[48:128, :] = jnp.zeros((80, D), f32)
    pack_share.wait()
    for pair in range(4):
        sides = [r.packs[2 * pair + k, 64:112, :].astype(f32) for k in range(2)]
        both = jnp.where(lanes_of((48, 128)) < 64, sides[0], pltpu.roll(sides[1], 64, 1))
        r.small[0:48, pair * 128 : pair * 128 + 128] = both
    keyval_weight = r.packs[:, 0:64, :].reshape(D, 128)
    shaped = (r.flow[...] * r.small[32:33, :] + r.small[33:34, :]).astype(bf16)
    r.acted[...] = shaped
    keyval_view(ctx)[...] = product(shaped, keyval_weight).astype(bf16)
    keyval_sends = direct_send(keyval_view(ctx), r.direct_sems.at[0], r.direct_recvs.at[0], length)
    for copy in keyval_sends:
        copy.start()
    query_gather.relay()

    id_lanes = [r.id_columns[:, j : j + 1] for j in range(MOA_TOP)]
    choice = product(shaped, r.small[...].astype(bf16), ((1,), (1,)))
    logits = [
        jnp.sum(jnp.where(lane == id_lanes[j], choice, 0.0), -1, keepdims=True)
        for j in range(MOA_TOP)
    ]
    peak = jnp.maximum(jnp.maximum(logits[0], logits[1]), jnp.maximum(logits[2], logits[3]))
    powers = [jnp.exp(item - peak) for item in logits]
    total = powers[0] + powers[1] + powers[2] + powers[3]
    gates = [item / total for item in powers]
    r.head_gates[...] = jnp.where(
        lane == 0,
        gates[0],
        jnp.where(lane == 1, gates[1], jnp.where(lane == 2, gates[2], gates[3])),
    )

    query_gather.relay_rest()
    project_gather.relay()
    inner_gather.start()
    outer_gathers[0].start()
    query_gather.finish()
    for part in range(6):
        columns = slice(part * 256, part * 256 + 256)
        r.mixture[:, columns] = product(r.acted[...], r.query[:, columns]).astype(bf16)
    cot_gather.relay(1)

    low_half = lane < HS
    side = lane // HS
    for j in range(MOA_TOP):
        wanted = id_lanes[j] - side
        chosen = jnp.zeros((tokens, 128), f32)
        for pair in range(MOA_EXPERTS // 2):
            block = r.mixture[:, pair * 128 : pair * 128 + 128].astype(f32)
            chosen = chosen + jnp.where(wanted == 2 * pair, block, 0.0)
        folded = chosen + pltpu.roll(chosen, HS, 1)
        r.queries[j * tokens : (j + 1) * tokens, :] = (
            jnp.where(low_half, folded, 0.0) * HS ** (-0.5)
        ).astype(bf16)

    project_gather.relay_rest()
    direct_wait(keyval_view, r.direct_sems.at[0], r.direct_recvs.at[0], length)
    chunk = 256

    def attend(turn, carried):
        rows = pl.ds(pl.multiple_of(turn * chunk, chunk), chunk)
        scores = product(r.queries[rows, :], r.keyval[...], ((1,), (1,)))
        top = jnp.max(scores, -1, keepdims=True)
        weights = jnp.exp(scores - top)
        mass = jnp.sum(weights, -1, keepdims=True)
        seen = product(weights.astype(bf16), r.keyval[...]) / mass
        r.heads[rows, :] = jnp.where(lanes_of((chunk, 128)) < HS, top + jnp.log(mass), seen)
        return carried

    lax.fori_loop(0, MOA_TOP * tokens // chunk, attend, 0)

    spread = []
    for j in range(MOA_TOP):
        head = r.heads[j * tokens : (j + 1) * tokens, :]
        both = jnp.where(low_half, pltpu.roll(head, HS, 1), head)
        spread.append(both * r.head_gates[:, j : j + 1])
    for pair in range(MOA_EXPERTS // 2):
        block = jnp.zeros((tokens, 128), f32)
        for j in range(MOA_TOP):
            block = jnp.where(id_lanes[j] - side == 2 * pair, spread[j], block)
        r.mixture[:, pair * 128 : pair * 128 + 128] = block.astype(bf16)

    project_gather.finish()
    between = r.states[...].astype(f32) + product(r.mixture[...], r.project[...])
    r.middle[...] = between
    centred = between - jnp.mean(between, -1, keepdims=True)
    inverse = lax.rsqrt(jnp.mean(centred * centred, -1, keepdims=True) + EPS)
    entry = (centred * inverse * r.small[34:35, :] + r.small[35:36, :]).astype(bf16)
    r.entering[ctx] = entry
    entering_gather.start()
    logits = product(r.small[16:32, :].astype(bf16), entry, ((1,), (1,)))[8:16]
    peak = jnp.max(jnp.where(picked, logits, -1e30), 0, keepdims=True)
    powers = jnp.where(picked, jnp.exp(jnp.where(picked, logits - peak, 0.0)), 0.0)
    r.routes[ctx, 8:16, :] = powers / jnp.sum(powers, 0, keepdims=True)
    route_sends = direct_send(r.routes.at[ctx], r.direct_sems.at[1], r.direct_recvs.at[1], length)
    for copy in route_sends:
        copy.start()

    def first_half(source):
        def one(expert, carried):
            chosen = picks(r, source, expert).astype(bf16)
            rows = product(chosen, r.entering[source]).astype(bf16)
            r.slot_rows[expert, slots(source), :] = rows

            def part(index, kept):
                columns = pl.ds(pl.multiple_of(index * 512, 512), 512)
                before = product(rows, r.inner[expert, :, columns])
                value, gradient = gelu_parts(before)
                r.active[expert, slots(source), columns] = value.astype(bf16)
                r.slope[expert, slots(source), columns] = gradient.astype(bf16)
                return kept

            return lax.fori_loop(0, 4, part, carried)

        lax.fori_loop(0, EXP_DEV, one, 0)

    def second_half(first, count):
        rows = pl.ds(pl.multiple_of(first * CAP, CAP), count * CAP)

        def one(expert, carried):
            value = product(r.active[expert, rows, :], r.outer[expert])
            r.result[expert, rows, :] = value.astype(bf16)
            return carried

        lax.fori_loop(0, EXP_DEV, one, 0)

    def score(source, carried):
        lines = []
        for expert in range(EXP_DEV):
            chosen = picks(r, source, expert)
            cot_rows = product(chosen.astype(bf16), r.cots[source]).astype(bf16)
            r.slot_cot[expert, slots(source), :] = cot_rows
            rows = r.result[expert, slots(source), :].astype(f32)
            toward = jnp.sum(rows * r.small[36:37, :], -1, keepdims=True)
            against = jnp.sum(rows * cot_rows.astype(f32), -1, keepdims=True)
            gate_row = r.routes[source, pl.ds(8 + EXP_DEV * ctx + expert, 1), :]
            gate = jnp.sum(chosen * gate_row, -1, keepdims=True)
            r.result[expert, slots(source), :] = (rows * gate).astype(bf16)
            lines.append(jnp.sum(chosen * toward, 0, keepdims=True))
            lines.append(jnp.sum(chosen * against, 0, keepdims=True))
        lines.append(jnp.zeros((8 - 2 * EXP_DEV, tokens), f32))
        sheet = jnp.concatenate(lines, 0)

        @pl.when(source == ctx)
        def _():
            r.scores_back[ctx] = sheet

        @pl.when(source != ctx)
        def _():
            r.score_sent[source] = sheet
            offset = (source - ctx + length) % length
            remote(
                r.score_sent.at[source],
                r.scores_back.at[ctx],
                r.direct_sems.at[2, offset - 1],
                r.direct_recvs.at[2, offset - 1],
                (source, me[1], me[2]),
            ).start()

        return carried

    lower = ctx < length // 2
    last = jnp.where(lower, length - 1, 0)
    at_end = jnp.logical_or(ctx == 0, ctx == length - 1)

    def arrival(turn):
        along = jnp.where(lower, turn, length - 1 - turn)
        around = jnp.where(turn == 0, ctx, jnp.where(turn == 1, ctx - 1, ctx + 1))
        return jnp.where(at_end, along, around)

    inner_gather.relay()
    outer_gathers[1].start()
    direct_wait(lambda b: r.routes.at[b], r.direct_sems.at[1], r.direct_recvs.at[1], length)
    entering_gather.relay(1)
    inner_gather.relay_rest()
    inner_gather.finish()
    outer_gathers[0].relay()

    def near(turn, carried):
        @pl.when(turn == 1)
        def _():
            entering_gather.relay(2)
            cot_gather.relay(2)

        @pl.when(turn == 2)
        def _():
            outer_gathers[1].relay()
            outer_gathers[0].relay_rest()

        first_half(arrival(turn))
        return carried

    lax.fori_loop(0, length - 1, near, 0)
    outer_gathers[1].relay_rest()
    for item in outer_gathers:
        item.finish()
    second_half(jnp.where(lower, 0, 1), length - 1)
    lax.fori_loop(0, length - 1, lambda turn, carried: score(arrival(turn), carried), 0)
    entering_gather.relay(length - 1)
    first_half(last)
    second_half(last, 1)
    cot_gather.relay(length - 1)
    score(last, 0)
    cot_gather.drain()
    mixed, unused = returns(length, r)
    for index in range(2):
        give_back(length, r, mixed.far + index)
    direct_wait(lambda b: r.scores_back.at[b], r.direct_sems.at[2], r.direct_recvs.at[2], length)
    for step in range(1, length):
        target = moved(me, step, length)
        remote(
            r.score_sent.at[target[0]],
            r.scores_back.at[ctx],
            r.direct_sems.at[2, step - 1],
            r.direct_recvs.at[2, step - 1],
            target,
        ).wait_send()
    for copy in keyval_sends + route_sends:
        copy.wait_send()
    for copy in pack_sends:
        copy.wait_send()
    for item in (query_gather, project_gather, inner_gather, *outer_gathers):
        item.drain()
    entering_gather.drain()


class LineReturn:
    def __init__(self, length, parts, arrived, send, recv):
        self.length, self.parts, self.arrived = length, parts, arrived
        self.send, self.recv = send, recv
        self.me = places()[0]
        ctx = self.me[0]
        self.at_end = jnp.logical_or(ctx == 0, ctx == length - 1)
        self.inside = jnp.logical_not(self.at_end)
        self.next = (ctx + 1 - 2 * (ctx % 2), self.me[1], self.me[2])
        self.far = (1 - ctx // 2) * 2

    def copy(self, block, place, slot, device):
        return remote(
            self.parts.at[block], self.arrived.at[place], self.send.at[slot], self.recv.at[slot], device
        )

    def hand(self, index):
        return self.copy(self.far + index, index, index, self.next)

    def near(self):
        return self.copy(self.next[0], 2, 2, self.next)

    def across(self, index):
        block = self.far + index
        return self.copy(block, 3, 3 + index, (block, self.me[1], self.me[2]))

    def start_far(self, index):
        pl.when(self.at_end)(lambda: self.hand(index).start())

    def pass_on(self, index):
        @pl.when(self.inside)
        def _():
            self.hand(index).wait_recv()
            block = self.far + index
            both = self.parts[block].astype(jnp.float32) + self.arrived[index].astype(jnp.float32)
            self.parts[block] = both.astype(jnp.bfloat16)
            self.across(index).start()

    def start_near(self):
        self.near().start()

    def wait(self):
        self.near().wait_recv()
        self.across(self.me[0] % 2).wait_recv()

    def total(self):
        own = self.parts[self.me[0]].astype(jnp.float32)
        return own + self.arrived[2].astype(jnp.float32) + self.arrived[3].astype(jnp.float32)

    def drain(self):
        self.near().wait_send()
        for index in range(2):
            pl.when(self.at_end)(lambda i=index: self.hand(i).wait_send())
            pl.when(self.inside)(lambda i=index: self.across(i).wait_send())


class PlaneReduce:
    def __init__(self, piece, rows, halves, arrived, send, recv):
        self.piece, self.rows, self.halves, self.arrived = piece, rows, halves, arrived
        self.send, self.recv = send, recv
        self.me, self.twin, self.beside, self.above, self.across = places()
        self.chip, self.core, self.line = self.me[1] // 2, self.me[1] % 2, self.me[2]

    def half(self, chip, core):
        view, half = self.piece(chip, core), self.halves.at[chip]
        return remote(view, half, self.send.at[chip], self.recv.at[chip], self.twin)

    def shard(self, chip, line):
        return self.piece(chip, self.core).at[pl.ds(line * self.rows, self.rows), :]

    def start(self):
        for chip in range(2):
            self.half(chip, 1 - self.core).start()

    def spread(self, slot, chip, line, device):
        return remote(
            self.shard(chip, line),
            self.arrived.at[slot],
            self.send.at[2 + slot],
            self.recv.at[2 + slot],
            device,
        )

    def sends(self):
        return (
            self.spread(0, 1 - self.chip, self.line, self.beside),
            self.spread(1, self.chip, 1 - self.line, self.above),
            self.spread(2, 1 - self.chip, 1 - self.line, self.across),
        )

    def add_halves(self):
        for chip in range(2):
            self.half(chip, self.core).wait_recv()
            view = self.piece(chip, self.core)
            both = view[...].astype(jnp.float32) + self.halves[chip].astype(jnp.float32)
            view[...] = both.astype(jnp.bfloat16)
        for copy in self.sends():
            copy.start()

    def total(self):
        for copy in self.sends():
            copy.wait_recv()
        value = self.shard(self.chip, self.line)[...].astype(jnp.float32)
        for slot in range(3):
            value = value + self.arrived[slot].astype(jnp.float32)
        return value

    def drain(self):
        for chip in range(2):
            self.half(chip, 1 - self.core).wait_send()
        for copy in self.sends():
            copy.wait_send()


class LineSum:
    def __init__(self, length, value, parts, summed, reduce_sems, gather_sems):
        self.length, self.value, self.parts, self.summed = length, value, parts, summed
        self.reduce_sems, self.gather_sems = reduce_sems, gather_sems
        self.me = places()[0]
        self.share = value.shape[0] // length

    def rows(self, block):
        return pl.ds(pl.multiple_of(block * self.share, self.share), self.share)

    def part(self, step):
        target = moved(self.me, step, self.length)
        send, recv = self.reduce_sems
        return remote(
            self.value.at[self.rows(target[0]), :],
            self.parts.at[step - 1],
            send.at[step - 1],
            recv.at[step - 1],
            target,
        )

    def start(self, value):
        self.value[...] = value.astype(jnp.bfloat16)
        for step in range(1, self.length):
            self.part(step).start()

    def view(self, block):
        return self.summed.at[self.rows(block), :]

    def share_out(self):
        for step in range(1, self.length):
            self.part(step).wait_recv()
        value = self.value[self.rows(self.me[0]), :].astype(jnp.float32)
        for step in range(1, self.length):
            value = value + self.parts[step - 1].astype(jnp.float32)
        self.view(self.me[0])[...] = value.astype(jnp.bfloat16)
        for copy in direct_send(self.view(self.me[0]), *self.gather_sems, self.length):
            copy.start()

    def finish(self):
        direct_wait(self.view, *self.gather_sems, self.length)
        return self.summed[...]

    def drain(self):
        for step in range(1, self.length):
            self.part(step).wait_send()
        for copy in direct_send(self.view(self.me[0]), *self.gather_sems, self.length):
            copy.wait_send()


class ExpertReduce:
    def __init__(self, inner, outer, half_in, half_out, side_in, side_out, last_in, last_out, send, recv):
        self.arrays = (inner, outer)
        self.halves = (half_in, half_out)
        self.sides = (side_in, side_out)
        self.lasts = (last_in, last_out)
        self.counts = (64, 256)
        self.send, self.recv = send, recv
        self.me, self.twin, self.beside, self.above, unused = places()
        self.chip, self.core, self.line = self.me[1] // 2, self.me[1] % 2, self.me[2]

    def rows(self, which, chip, core, line, count):
        size = self.counts[which]
        start = pl.multiple_of(((chip * 2 + core) * 2 + line) * size, size)
        return self.arrays[which].at[:, pl.ds(start, count * size), :]

    def copy(self, source, target, slot, device):
        return remote(source, target, self.send.at[slot], self.recv.at[slot], device)

    def half(self, which, chip, core):
        return self.copy(
            self.rows(which, chip, core, 0, 2), self.halves[which].at[chip], 2 * which + chip, self.twin
        )

    def start(self, which):
        for chip in range(2):
            self.half(which, chip, 1 - self.core).start()

    def side(self, which):
        if which == 0:
            source = self.rows(0, 1 - self.chip, self.core, 0, 2)
            return [self.copy(source, self.sides[0], 4, self.beside)]
        return [
            self.copy(
                self.rows(1, chip, self.core, 1 - self.line, 1), self.sides[1].at[chip], 5 + chip, self.above
            )
            for chip in range(2)
        ]

    def add(self, view, other):
        for expert in range(EXP_DEV):
            both = view[expert].astype(jnp.float32) + other[expert].astype(jnp.float32)
            view[expert] = both.astype(jnp.bfloat16)

    def add_halves(self, which):
        def one(chip, carried):
            self.half(which, chip, self.core).wait_recv()
            self.add(self.rows(which, chip, self.core, 0, 2), self.halves[which].at[chip])
            return carried

        lax.fori_loop(0, 2, one, 0)
        for copy in self.side(which):
            copy.start()

    def last(self, which):
        if which == 0:
            source = self.rows(0, self.chip, self.core, 1 - self.line, 1)
            return self.copy(source, self.lasts[0], 7, self.above)
        source = self.rows(1, 1 - self.chip, self.core, self.line, 1)
        return self.copy(source, self.lasts[1], 8, self.beside)

    def add_sides(self, which):
        for copy in self.side(which):
            copy.wait_recv()
        if which == 0:
            self.add(self.rows(0, self.chip, self.core, 0, 2), self.sides[0])
        else:
            for chip in range(2):
                self.add(self.rows(1, chip, self.core, self.line, 1), self.sides[1].at[chip])
        self.last(which).start()

    def total(self, which, result):
        self.last(which).wait_recv()
        view = self.rows(which, self.chip, self.core, self.line, 1)
        for expert in range(EXP_DEV):
            both = view[expert].astype(jnp.float32) + self.lasts[which][expert].astype(jnp.float32)
            result[expert] = both.astype(jnp.bfloat16)

    def drain(self):
        for which in range(2):
            for chip in range(2):
                self.half(which, chip, 1 - self.core).wait_send()
            for copy in self.side(which):
                copy.wait_send()
            self.last(which).wait_send()


def backward_part(length, r):
    f32, bf16 = jnp.float32, jnp.bfloat16
    tokens = r.states.shape[0]
    me = places()[0]
    ctx = me[0]
    lane = lanes_of((tokens, 128))
    low_half = lane < HS
    side = lane // HS
    id_lanes = [r.id_columns[:, j : j + 1] for j in range(MOA_TOP)]

    def sems(row):
        return r.direct_sems.at[row], r.direct_recvs.at[row]

    def from_all(target_ref, row):
        send, recv = sems(row)
        for step in range(1, length):
            view = target_ref.at[step - 1]
            source = moved(me, length - step, length)
            remote(view, view, send.at[step - 1], recv.at[step - 1], source).wait_recv()

    def sent_all(view_of, target_ref, row):
        for step in range(1, length):
            block = moved(me, step, length)[0]
            to_owner(length, r, view_of(block), target_ref, row, block).wait_send()

    r.gsmall[...] = jnp.zeros_like(r.gsmall)
    mid = r.middle[...]
    cot = r.cotangent[...]
    halt_row = r.small[36:37, :]
    reach = jnp.sum(mid * halt_row, -1, keepdims=True)
    gap = jnp.sum(cot * (r.states[...].astype(f32) - mid), -1, keepdims=True)
    turned = jnp.transpose(jnp.where(lane == 0, reach, gap))[0:8]
    gates = r.routes[ctx, 8:16, :]
    toward = jnp.concatenate(
        [r.scores_back[d, 2 * e : 2 * e + 1, :] for d in range(length) for e in range(EXP_DEV)], 0
    )
    against = jnp.concatenate(
        [r.scores_back[d, 2 * e + 1 : 2 * e + 2, :] for d in range(length) for e in range(EXP_DEV)], 0
    )
    halting = jax.nn.sigmoid(turned[0:1] + jnp.sum(gates * toward, 0, keepdims=True))
    stop_grad = turned[1:2] - jnp.sum(gates * against, 0, keepdims=True)
    mass, left = r.remaining[...], r.left_cot[...]
    stopped = mass * halting
    halt_grad = (stop_grad - left) * mass * halting * (1.0 - halting)
    r.rows_out[0:1, :] = mass * (1.0 - halting)
    r.rows_out[1:2, :] = stop_grad * halting + left * (1.0 - halting)
    sheet = jnp.concatenate([1.0 - stopped, halt_grad, stopped, jnp.zeros((5, tokens), f32)], 0)
    r.factors[ctx] = sheet
    factor_sends = direct_send(r.factors.at[ctx], *sems(3), length)
    for copy in factor_sends:
        copy.start()
    mixed, backs = returns(length, r)
    for index in range(2):
        mixed.start_far(index)
    r.columns[...] = jnp.transpose(jnp.concatenate([sheet, jnp.zeros((120, tokens), f32)], 0))
    gate_grad = (1.0 - stopped) * against + halt_grad * toward
    pick_grad = gates * (gate_grad - jnp.sum(gates * gate_grad, 0, keepdims=True))
    coarse = pick_grad.astype(bf16).astype(f32)
    r.pick_grads[...] = jnp.concatenate([coarse, pick_grad - coarse], 0).astype(bf16)
    sums = product(r.pick_grads[...], r.entering[ctx])
    r.gsmall[24:32, :] = sums[0:8] + sums[8:16]
    keep_col, halt_col = r.columns[:, 0:1], r.columns[:, 1:2]
    r.flow[...] = keep_col * cot + halt_col * halt_row
    r.grad_states[...] = r.columns[:, 2:3] * cot
    r.gsmall[36:37, :] = jnp.sum(halt_col * mid, 0, keepdims=True)

    def rows_back(block):
        @pl.when(block != ctx)
        def _():
            slot = (ctx - block + length) % length - 1
            view = r.factors.at[block]
            send, recv = sems(3)
            remote(view, view, send.at[slot], recv.at[slot], (block, me[1], me[2])).wait_recv()

        for expert in range(EXP_DEV):
            chosen = picks(r, block, expert)
            keep = jnp.sum(chosen * r.factors[block, 0:1, :], -1, keepdims=True)
            halt = jnp.sum(chosen * r.factors[block, 1:2, :], -1, keepdims=True)
            gate_row = r.routes[block, pl.ds(8 + EXP_DEV * ctx + expert, 1), :]
            gate = jnp.sum(chosen * gate_row, -1, keepdims=True)
            rows = r.result[expert, slots(block), :].astype(f32)
            r.gsmall[36:37, :] += jnp.sum(halt * rows, 0, keepdims=True)
            incoming = r.slot_cot[expert, slots(block), :].astype(f32)
            rows_grad = (gate * (keep * incoming + halt * halt_row)).astype(bf16)
            r.slot_cot[expert, slots(block), :] = rows_grad

    side_blocks = length // 2
    side_rows = side_blocks * CAP

    def side_back(turn, carried):
        half = jnp.where(turn == 0, 1 - ctx // side_blocks, ctx // side_blocks)

        def prepare(index, kept):
            rows_back(half * side_blocks + index)
            return kept

        lax.fori_loop(0, side_blocks, prepare, 0)
        rows = pl.ds(pl.multiple_of(half * side_rows, side_rows), side_rows)

        def one(expert, kept):
            def part(index, inside):
                columns = pl.ds(pl.multiple_of(index * 512, 512), 512)
                back = product(r.slot_cot[expert, rows, :], r.outer[expert, columns, :], ((1,), (1,)))
                slope = r.slope[expert, rows, columns].astype(f32)
                r.slope[expert, rows, columns] = (back * slope).astype(bf16)
                return inside

            lax.fori_loop(0, 4, part, 0)
            sent = product(r.slope[expert, rows, :], r.inner[expert], ((1,), (1,)))
            r.slot_back[expert] = sent.astype(bf16)
            return kept

        lax.fori_loop(0, EXP_DEV, one, 0)

        def send(index, kept):
            block = half * side_blocks + index
            total = 0.0
            for expert in range(EXP_DEV):
                chosen = picks(r, block, expert).astype(bf16)
                total = total + product(chosen, r.slot_back[expert, slots(index), :], ((0,), (0,)))
            r.entering[block] = total.astype(bf16)
            return kept

        lax.fori_loop(0, side_blocks, send, 0)

        @pl.when(turn == 0)
        def _():
            for index in range(2):
                backs.start_far(index)
            mixed.pass_on(0)

        return carried

    lax.fori_loop(0, 2, side_back, 0)
    backs.start_near()
    mixed.pass_on(1)
    give_back(length, r, backs.next[0])
    mixed.start_near()
    give_back(length, r, ctx)

    experts = ExpertReduce(
        r.inner, r.outer, r.half_in, r.half_out, r.side_in, r.side_out, r.last_in, r.last_out,
        r.expert_send, r.expert_recv,
    )

    def outer_grad(turn, carried):
        expert, part = turn // 4, turn % 4
        columns = pl.ds(pl.multiple_of(part * 512, 512), 512)
        value = product(r.active[expert, :, columns], r.slot_cot[expert], ((0,), (0,)))
        r.outer[expert, columns, :] = value.astype(bf16)
        return carried

    lax.fori_loop(0, 4 * EXP_DEV, outer_grad, 0)
    experts.start(1)
    backs.pass_on(0)

    def inner_grad(turn, carried):
        expert, part = turn // 4, turn % 4
        columns = pl.ds(pl.multiple_of(part * 512, 512), 512)
        value = product(r.slot_rows[expert], r.slope[expert, :, columns], ((0,), (0,)))
        r.inner[expert, :, columns] = value.astype(bf16)
        return carried

    lax.fori_loop(0, 4 * EXP_DEV, inner_grad, 0)
    experts.start(0)
    experts.add_halves(1)
    backs.pass_on(1)
    experts.add_halves(0)

    backs.wait()
    mid = r.middle[...]
    selector = r.small[24:32, :]
    double = jnp.concatenate([selector, selector], 0).astype(bf16)
    back = product(r.pick_grads[...], double, ((0,), (0,))) + backs.total()
    centred = mid - jnp.mean(mid, -1, keepdims=True)
    inverse = lax.rsqrt(jnp.mean(centred * centred, -1, keepdims=True) + EPS)
    plain = centred * inverse
    r.gsmall[34:35, :] = jnp.sum(back * plain, 0, keepdims=True)
    r.gsmall[35:36, :] = jnp.sum(back, 0, keepdims=True)
    scaled = back * r.small[34:35, :]
    level = jnp.mean(scaled, -1, keepdims=True)
    tilt = jnp.mean(scaled * plain, -1, keepdims=True)
    flow = r.flow[...] + inverse * (scaled - level - plain * tilt)
    r.flow[...] = flow
    attn_grad = flow.astype(bf16)

    def project_piece(chip, core):
        column = pl.multiple_of((chip * 2 + core) * 512, 512)
        return r.active.at[1, pl.ds(0, 384), pl.ds(column, 512)]

    for part in range(4):
        value = product(r.mixture[:, part * 384 : part * 384 + 384], attn_grad, ((0,), (0,)))
        r.active[1, 0:384, part * 512 : part * 512 + 512] = value.astype(bf16)

    def reducer(index, piece, rows, halves, arrived):
        return PlaneReduce(piece, rows, halves, arrived, r.dense_send.at[index], r.dense_recv.at[index])

    project_reduce = reducer(0, project_piece, 192, r.project_half, r.project_in)
    project_reduce.start()

    chosen = [jnp.zeros((tokens, 128), f32) for unused in range(MOA_TOP)]
    for part in range(6):
        value = product(attn_grad, r.project[part * 256 : part * 256 + 256, :], ((1,), (1,)))
        for pair in range(2):
            block = value[:, pair * 128 : pair * 128 + 128]
            for j in range(MOA_TOP):
                wanted = id_lanes[j] - side == 2 * (2 * part + pair)
                chosen[j] = chosen[j] + jnp.where(wanted, block, 0.0)
    gate_lanes = [r.head_gates[:, j : j + 1] for j in range(MOA_TOP)]
    gate_grads = []
    for j in range(MOA_TOP):
        rows = slice(j * tokens, (j + 1) * tokens)
        head = r.heads[rows, :]
        folded = jnp.where(low_half, 0.0, chosen[j] + pltpu.roll(chosen[j], HS, 1))
        gate_grads.append(jnp.sum(folded * head, -1, keepdims=True))
        grads = (gate_lanes[j] * folded).astype(bf16)
        r.heads_grad[rows, :] = grads
        delta = jnp.sum(grads.astype(f32) * head, -1, keepdims=True)
        pair = jnp.transpose(jnp.where(lane == 0, head[:, 0:1], delta))
        r.stats[:, rows] = pair[0:8]
    common = sum(g * v for g, v in zip(gate_lanes, gate_grads))
    logit = jnp.zeros((tokens, 128), f32)
    for j in range(MOA_TOP):
        logit = jnp.where(lane == id_lanes[j], gate_lanes[j] * (gate_grads[j] - common), logit)
    coarse = logit.astype(bf16)
    fine = (logit - coarse.astype(f32)).astype(bf16)
    sums = product(coarse, r.acted[...], ((0,), (0,))) + product(fine, r.acted[...], ((0,), (0,)))
    r.gsmall[0:24, :] = sums[0:24]
    chooser = r.small[...].astype(bf16)
    r.cotangent[...] = product(coarse, chooser) + product(fine, chooser)
    project_reduce.add_halves()

    r.kv_grad[...] = jnp.zeros_like(r.kv_grad)
    chunk = 256

    half_keys = length * tokens // 2

    def attend_back(turn, carried):
        @pl.when(turn == 4)
        def _():
            experts.add_sides(1)

        @pl.when(turn == 8)
        def _():
            experts.add_sides(0)

        rows = pl.ds(pl.multiple_of((turn // 2) * chunk, chunk), chunk)
        keys = pl.ds(pl.multiple_of((turn % 2) * half_keys, half_keys), half_keys)
        query, grads, keyval = r.queries[rows, :], r.heads_grad[rows, :], r.keyval[keys, :]
        scores = product(keyval, query, ((1,), (1,)))
        weights = jnp.exp(scores - r.stats[0:1, rows])
        upward = product(keyval, grads, ((1,), (1,)))
        score_grad = (weights * (upward - r.stats[1:2, rows])).astype(bf16)
        r.kv_grad[keys, :] += product(score_grad, query) + product(weights.astype(bf16), grads)
        down = product(score_grad, keyval, ((0,), (0,))) * HS ** (-0.5)

        @pl.when(turn % 2 == 0)
        def _():
            r.heads[rows, :] = down

        @pl.when(turn % 2 == 1)
        def _():
            r.heads[rows, :] += down

        return carried

    lax.fori_loop(0, 2 * MOA_TOP * tokens // chunk, attend_back, 0)

    def send_keyval(turn, carried):
        block = (ctx + turn) % length
        rows = pl.ds(pl.multiple_of(block * tokens, tokens), tokens)

        @pl.when(turn > 0)
        def _():
            r.heads_grad[rows, :] = r.kv_grad[rows, :].astype(bf16)
            to_owner(length, r, r.heads_grad.at[rows, :], r.kv_in, 6, block).start()

        return carried

    lax.fori_loop(0, length, send_keyval, 0)
    spread = []
    for j in range(MOA_TOP):
        piece = r.heads[j * tokens : (j + 1) * tokens, :]
        spread.append(jnp.where(low_half, piece, pltpu.roll(piece, HS, 1)))
    for pair in range(MOA_EXPERTS // 2):
        block = jnp.zeros((tokens, 128), f32)
        for j in range(MOA_TOP):
            block = jnp.where(id_lanes[j] - side == 2 * pair, spread[j], block)
        r.mixture[:, pair * 128 : pair * 128 + 128] = block.astype(bf16)
    for part in range(4):
        columns = slice(part * 384, part * 384 + 384)
        value = product(r.acted[...], r.mixture[:, columns], ((0,), (0,)))
        r.active[0, 0:512, columns] = value.astype(bf16)

    def wide_piece(first, width):
        def piece(chip, core):
            start = pl.multiple_of((chip * 2 + core) * 128, 128)
            return r.active.at[0, pl.ds(start, 128), pl.ds(first, width)]

        return piece

    query_reduce = reducer(1, wide_piece(0, 1536), 64, r.query_half, r.query_in)
    query_reduce.start()
    r.cotangent[...] += product(r.mixture[...], r.query[...], ((1,), (1,)))
    project_line = LineSum(length, r.project_value, r.project_parts, r.project_sum, sems(7), sems(8))
    project_line.start(project_reduce.total())
    query_reduce.add_halves()

    own_rows = pl.ds(pl.multiple_of(ctx * tokens, tokens), tokens)
    from_all(r.kv_in, 6)
    keyval_grad = r.kv_grad[own_rows, :]
    for step in range(length - 1):
        keyval_grad = keyval_grad + r.kv_in[step].astype(f32)
    keyval_grad = keyval_grad.astype(bf16)
    back = r.cotangent[...] + product(keyval_grad, r.packs[:, 0:64, :].reshape(D, 128), ((1,), (1,)))
    values = r.states[...].astype(f32)
    centred = values - jnp.mean(values, -1, keepdims=True)
    inverse = lax.rsqrt(jnp.mean(centred * centred, -1, keepdims=True) + EPS)
    plain = centred * inverse
    r.gsmall[32:33, :] = jnp.sum(back * plain, 0, keepdims=True)
    r.gsmall[33:34, :] = jnp.sum(back, 0, keepdims=True)
    r.active[0, 0:512, 1536:1664] = product(r.acted[...], keyval_grad, ((0,), (0,))).astype(bf16)
    r.active[0, 0:512, 1664:1792] = jnp.transpose(r.gsmall[...]).astype(bf16)
    small_reduce = reducer(2, wide_piece(1536, 256), 64, r.small_half, r.small_in)
    small_reduce.start()
    scaled = back * r.small[32:33, :]
    level = jnp.mean(scaled, -1, keepdims=True)
    tilt = jnp.mean(scaled * plain, -1, keepdims=True)
    r.grad_states[...] = (
        r.grad_states[...] + r.flow[...] + inverse * (scaled - level - plain * tilt)
    )
    small_reduce.add_halves()
    project_line.share_out()
    query_line = LineSum(length, r.query_value, r.query_parts, r.query_sum, sems(9), sems(10))
    query_line.start(query_reduce.total())
    small_line = LineSum(length, r.small_value, r.small_parts, r.small_sum, sems(11), sems(12))
    small_line.start(small_reduce.total())

    experts.total(1, r.grad_outer)
    experts.total(0, r.grad_inner)
    mixed.wait()
    final = r.middle[...] + mixed.total()
    r.new_states[...] = (
        r.columns[:, 2:3] * r.states[...].astype(f32) + r.columns[:, 0:1] * final
    ).astype(bf16)
    query_line.share_out()
    small_line.share_out()
    r.grad_project[...] = project_line.finish()
    r.grad_query[...] = query_line.finish()
    r.grad_small[...] = small_line.finish()

    for copy in factor_sends:
        copy.wait_send()
    mixed.drain()
    backs.drain()
    sent_all(
        lambda b: r.heads_grad.at[pl.ds(pl.multiple_of(b * tokens, tokens), tokens), :], r.kv_in, 6
    )
    for item in (project_reduce, query_reduce, small_reduce, experts):
        item.drain()
    for item in (project_line, query_line, small_line):
        item.drain()


def whole_kernel(length, names, *refs):
    r = SimpleNamespace(**dict(zip(names, refs)))
    forward_part(length, r)
    backward_part(length, r)


def write_kernel(
    new_states, rows_out, grad_states, grad_query, grad_project, grad_small, grad_inner, grad_outer, *outs
):
    f32 = jnp.float32
    outs[0][0] = new_states[...]
    outs[1][...] = rows_out[0:1, :]
    outs[2][0] = grad_states[...]
    outs[3][...] = rows_out[1:2, :]
    outs[4][...] = grad_query[...].astype(f32)
    outs[5][...] = grad_small[:, 0:128].astype(f32)
    outs[6][...] = grad_project[...].astype(f32)
    turned = jnp.transpose(grad_small[:, 128:256].astype(f32))
    outs[7][...] = turned[0:24]
    outs[8][...] = turned[24:32]
    for index in range(5):
        outs[9 + index][...] = turned[32 + index : 33 + index]
    outs[14][...] = grad_inner[...].astype(f32)
    outs[15][...] = grad_outer[...].astype(f32)


def write_out(tokens, *results):
    f32, bf16 = jnp.float32, jnp.bfloat16
    shape = jax.ShapeDtypeStruct
    outs = (
        shape((1, tokens, D), bf16),
        shape((1, tokens), f32),
        shape((1, tokens, D), f32),
        shape((1, tokens), f32),
        shape((64, MOA_EXPERTS * HS), f32),
        shape((64, 128), f32),
        shape((192, D), f32),
        shape((MOA_EXPERTS, 64), f32),
        shape((8, 64), f32),
        *[shape((1, 64), f32)] * 5,
        shape((EXP_DEV, 64, FF), f32),
        shape((EXP_DEV, 256, D), f32),
    )
    in_vmem = pl.BlockSpec(memory_space=pltpu.VMEM)
    final = pl.pallas_call(
        write_kernel,
        out_shape=outs,
        in_specs=[in_vmem] * len(results),
        out_specs=[in_vmem] * len(outs),
        compiler_params=pltpu.CompilerParams(vmem_limit_bytes=LIMIT_MIB * 2**20),
        name="write_out",
    )(*results)
    vectors = [item.reshape(64) for item in final[9:14]]
    return (*final[0:7], final[7].T, final[8].T, *vectors, *final[14:16])


def fast_body(
    states,
    remaining,
    moa_ids,
    ffn_ids,
    out_cotangent,
    left_cotangent,
    query_weight,
    keyval_weight,
    project_weight,
    chooser,
    selector,
    gain_one,
    bias_one,
    gain_two,
    bias_two,
    halt_weight,
    expert_in,
    expert_out,
):
    f32, bf16 = jnp.float32, jnp.bfloat16
    length = lax.axis_size("ctx")
    tokens = states.shape[1]
    rows = length * CAP
    wide = MOA_EXPERTS * HS
    nothing = jnp.zeros_like(gain_one)
    vectors = jnp.stack(
        [gain_one, bias_one, gain_two, bias_two, halt_weight, nothing, nothing, nothing], 0
    )
    inputs = dict(
        states=states[0],
        cotangent_part=out_cotangent[0],
        head_ids=moa_ids[0].T,
        route_ids=ffn_ids[0].T,
        remaining=remaining,
        left_cot=left_cotangent,
        keyval_part=keyval_weight,
        chooser_part=chooser.T,
        selector_part=selector.T,
        vectors=vectors,
        query_part=query_weight,
        project_part=project_weight,
        inner_part=expert_in,
        outer_part=expert_out,
    )
    in_place = ("cotangent_part", "query_part", "project_part", "inner_part", "outer_part")
    shape = jax.ShapeDtypeStruct
    outputs = dict(
        new_states=shape((tokens, D), bf16),
        rows_out=shape((8, tokens), f32),
        grad_states=shape((tokens, D), f32),
        grad_query=shape((64, wide), bf16),
        grad_project=shape((192, D), bf16),
        grad_small=shape((64, 256), bf16),
        grad_inner=shape((EXP_DEV, 64, FF), bf16),
        grad_outer=shape((EXP_DEV, 256, D), bf16),
    )
    vmem, dma = pltpu.VMEM, pltpu.SemaphoreType.DMA
    scratch = dict(
        slot_rows=vmem((EXP_DEV, rows, D), bf16),
        active=vmem((EXP_DEV, rows, FF), bf16),
        slope=vmem((EXP_DEV, rows, FF), bf16),
        result=vmem((EXP_DEV, rows, D), bf16),
        slot_cot=vmem((EXP_DEV, rows, D), bf16),
        inner=vmem((EXP_DEV, D, FF), bf16),
        outer=vmem((EXP_DEV, FF, D), bf16),
        query=vmem((D, wide), bf16),
        project=vmem((wide, D), bf16),
        packs=vmem((8, 112, 128), bf16),
        id_columns=vmem((tokens, 128), jnp.int32),
        cotangent=vmem((tokens, D), f32),
        acted=vmem((tokens, D), bf16),
        mixture=vmem((tokens, wide), bf16),
        queries=vmem((MOA_TOP * tokens, 128), bf16),
        heads=vmem((MOA_TOP * tokens, 128), f32),
        keyval=vmem((length * tokens, 128), bf16),
        head_gates=vmem((tokens, 128), f32),
        middle=vmem((tokens, D), f32),
        entering=vmem((length, tokens, D), bf16),
        cots=vmem((length, tokens, D), bf16),
        routes=vmem((length, 16, tokens), f32),
        scores_back=vmem((length, 8, tokens), f32),
        small=vmem((128, D), f32),
        score_sent=vmem((length, 8, tokens), f32),
        factors=vmem((length, 8, tokens), f32),
        columns=vmem((tokens, 128), f32),
        pick_grads=vmem((16, tokens), bf16),
        gsmall=vmem((128, D), f32),
        flow=vmem((tokens, D), f32),
        slot_back=vmem((EXP_DEV, rows // 2, D), bf16),
        back_in=vmem((4, tokens, D), bf16),
        mix_in=vmem((4, tokens, D), bf16),
        half_in=vmem((2, EXP_DEV, 128, FF), bf16),
        half_out=vmem((2, EXP_DEV, 512, D), bf16),
        side_in=vmem((EXP_DEV, 128, FF), bf16),
        side_out=vmem((2, EXP_DEV, 256, D), bf16),
        last_in=vmem((EXP_DEV, 64, FF), bf16),
        last_out=vmem((EXP_DEV, 256, D), bf16),
        heads_grad=vmem((MOA_TOP * tokens, 128), bf16),
        stats=vmem((8, MOA_TOP * tokens), f32),
        kv_grad=vmem((length * tokens, 128), f32),
        kv_in=vmem((length - 1, tokens, 128), bf16),
        project_half=vmem((2, 384, D), bf16),
        project_in=vmem((3, 192, D), bf16),
        query_half=vmem((2, 128, wide), bf16),
        query_in=vmem((3, 64, wide), bf16),
        small_half=vmem((2, 128, 256), bf16),
        small_in=vmem((3, 64, 256), bf16),
        project_value=vmem((192, D), bf16),
        project_parts=vmem((length - 1, 192 // length, D), bf16),
        project_sum=vmem((192, D), bf16),
        query_value=vmem((64, wide), bf16),
        query_parts=vmem((length - 1, 64 // length, wide), bf16),
        query_sum=vmem((64, wide), bf16),
        small_value=vmem((64, 256), bf16),
        small_parts=vmem((length - 1, 64 // length, 256), bf16),
        small_sum=vmem((64, 256), bf16),
        pack_send=dma((7,)),
        pack_recv=dma((7,)),
        plane_send=dma((5, 9)),
        plane_recv=dma((5, 9)),
        plane_local=dma((6,)),
        line_send=dma((2, 2, length)),
        line_recv=dma((2, 2, length)),
        direct_sems=dma((13, length)),
        direct_recvs=dma((13, length)),
        return_send=dma((2, 5)),
        return_recv=dma((2, 5)),
        expert_send=dma((9,)),
        expert_recv=dma((9,)),
        dense_send=dma((3, 5)),
        dense_recv=dma((3, 5)),
    )
    in_vmem = pl.BlockSpec(memory_space=pltpu.VMEM)
    anywhere = pl.BlockSpec(memory_space=pl.ANY)
    names = (*inputs, *outputs, *scratch)
    results = pl.pallas_call(
        partial(whole_kernel, length, names),
        out_shape=tuple(outputs.values()),
        in_specs=[anywhere if name in in_place else in_vmem for name in inputs],
        out_specs=[in_vmem] * len(outputs),
        scratch_shapes=list(scratch.values()),
        compiler_params=pltpu.CompilerParams(
            collective_id=0, has_side_effects=True, vmem_limit_bytes=LIMIT_MIB * 2**20
        ),
        name="layer_step",
    )(*inputs.values())
    return write_out(tokens, *results)


def solution(mesh):
    in_specs = (
        P(("seq", "wsh"), "ctx", None),
        P(("seq", "wsh"), "ctx"),
        P(("seq", "wsh"), "ctx", None),
        P(("seq", "wsh"), "ctx", None),
        P(("seq", "wsh"), "ctx", None),
        P(("seq", "wsh"), "ctx"),
        P(("seq", "wsh"), None),
        P(("seq", "wsh"), None),
        P(("seq", "wsh"), None),
        P(("seq", "wsh"), None),
        P(("seq", "wsh"), None),
        P(("seq", "wsh")),
        P(("seq", "wsh")),
        P(("seq", "wsh")),
        P(("seq", "wsh")),
        P(("seq", "wsh")),
        P("ctx", ("seq", "wsh"), None),
        P("ctx", ("seq", "wsh"), None),
    )
    out_specs = (
        P(("seq", "wsh"), "ctx", None),
        P(("seq", "wsh"), "ctx"),
        P(("seq", "wsh"), "ctx", None),
        P(("seq", "wsh"), "ctx"),
        P(("seq", "wsh"), None),
        P(("seq", "wsh"), None),
        P(("seq", "wsh"), None),
        P(("seq", "wsh"), None),
        P(("seq", "wsh"), None),
        P(("seq", "wsh")),
        P(("seq", "wsh")),
        P(("seq", "wsh")),
        P(("seq", "wsh")),
        P(("seq", "wsh")),
        P("ctx", ("seq", "wsh"), None),
        P("ctx", ("seq", "wsh"), None),
    )
    body = fast_body if mesh.shape["ctx"] == 4 else general_body
    return jax.shard_map(body, mesh=mesh, in_specs=in_specs, out_specs=out_specs, check_vma=False)
```

```python
from functools import partial
from types import SimpleNamespace

import jax
import jax.numpy as jnp
from jax import lax
from jax.experimental import pallas as pl
from jax.experimental.pallas import tpu as pltpu
from jax.sharding import PartitionSpec as P

D = 512
HS = 64
MOA_EXPERTS = 24
MOA_TOP = 4
EXP_DEV = 2
FFN_TOP = 2
FF = 2048


EPS = 1e-05
HIGH = lax.Precision.HIGHEST


def shifted(x, axis, by):
    length = lax.axis_size(axis)
    return lax.ppermute(x, axis, [(i, (i + by) % length) for i in range(length)])


def layer_norm(values, gain, bias):
    centred = values - jnp.mean(values, -1, keepdims=True)
    inverse = lax.rsqrt(jnp.mean(centred * centred, -1, keepdims=True) + EPS)
    normal = centred * inverse
    return (normal * gain + bias, normal, inverse)


def norm_back(incoming, normal, inverse, gain):
    scaled = incoming * gain
    inner_term = (
        scaled
        - jnp.mean(scaled, -1, keepdims=True)
        - normal * jnp.mean(scaled * normal, -1, keepdims=True)
    )
    return (inverse * inner_term, jnp.sum(incoming * normal, 0), jnp.sum(incoming, 0))


def one_hot(index, count):
    return (index[..., None] == jnp.arange(count, dtype=jnp.int32)).astype(jnp.float32)


def choose_back(gates, upstream):
    return gates * (upstream - jnp.sum(gates * upstream, -1, keepdims=True))


def block_rows(row_count):
    if row_count > 512 and row_count % 512 == 0:
        return 512
    return row_count


def expert_slots(route_ids, experts):
    flat_ids = route_ids.reshape(-1)
    table = (flat_ids[:, None] == jnp.arange(experts, dtype=jnp.int32)[None, :]).astype(jnp.float32)
    place = jnp.arange(flat_ids.shape[0], dtype=jnp.int32)
    before = (place[None, :] < place[:, None]).astype(jnp.bfloat16)
    earlier = jnp.dot(before, table.astype(jnp.bfloat16), preferred_element_type=jnp.float32)
    return jnp.sum(earlier * table, 1).astype(jnp.int32).reshape(route_ids.shape)


def general_body(
    states,
    remaining,
    moa_ids,
    ffn_ids,
    out_cotangent,
    left_cotangent,
    query_weight,
    keyval_weight,
    project_weight,
    chooser,
    selector,
    gain_one,
    bias_one,
    gain_two,
    bias_two,
    halt_weight,
    expert_in,
    expert_out,
):
    tokens = states.shape[1]
    devices = lax.axis_size("ctx")
    experts = EXP_DEV * devices
    capacity = max(2, (4 * tokens + experts - 1) // experts)
    rows_total = tokens * MOA_TOP
    scaling = HS ** (-0.5)
    f32 = jnp.float32
    bf16 = jnp.bfloat16
    (
        query_full,
        keyval_full,
        project_full,
        chooser_full,
        selector_full,
        gainone_full,
        biasone_full,
        gaintwo_full,
        biastwo_full,
        halt_full,
    ) = (
        lax.all_gather(query_weight, ("seq", "wsh"), axis=0, tiled=True),
        lax.all_gather(keyval_weight, ("seq", "wsh"), axis=0, tiled=True),
        lax.all_gather(project_weight, ("seq", "wsh"), axis=0, tiled=True),
        lax.all_gather(chooser, ("seq", "wsh"), axis=0, tiled=True),
        lax.all_gather(selector, ("seq", "wsh"), axis=0, tiled=True),
        lax.all_gather(gain_one, ("seq", "wsh"), axis=0, tiled=True),
        lax.all_gather(bias_one, ("seq", "wsh"), axis=0, tiled=True),
        lax.all_gather(gain_two, ("seq", "wsh"), axis=0, tiled=True),
        lax.all_gather(bias_two, ("seq", "wsh"), axis=0, tiled=True),
        lax.all_gather(halt_weight, ("seq", "wsh"), axis=0, tiled=True),
    )
    inner_full, outer_full = (
        lax.all_gather(expert_in, ("seq", "wsh"), axis=1, tiled=True),
        lax.all_gather(expert_out, ("seq", "wsh"), axis=1, tiled=True),
    )
    gain_first = gainone_full.astype(f32)
    gain_second = gaintwo_full.astype(f32)
    halt_vector = halt_full.astype(f32)
    resident = states[0].astype(f32)
    normed_one, normal_one, inverse_one = layer_norm(resident, gain_first, biasone_full.astype(f32))
    acted = normed_one.astype(bf16)
    query_all = (
        jnp.dot(acted, query_full, preferred_element_type=f32)
        .astype(bf16)
        .reshape(tokens, MOA_EXPERTS, HS)
    )
    head_ids = moa_ids[0]
    query_sel = jnp.take_along_axis(query_all, head_ids[:, :, None], axis=1).reshape(rows_total, HS)
    keyval = jnp.dot(acted, keyval_full, preferred_element_type=f32).astype(bf16)
    chosen = one_hot(head_ids, MOA_EXPERTS)
    head_logits = jnp.sum(
        chosen * jnp.dot(acted, chooser_full, preferred_element_type=f32)[:, None, :], -1
    )
    head_gates = jax.nn.softmax(head_logits, -1)
    start_state = (
        jnp.full((rows_total,), -1e30, f32),
        jnp.zeros((rows_total,), f32),
        jnp.zeros((rows_total, HS), f32),
    )
    running = start_state
    shard_rows = lax.all_gather(keyval, "ctx", axis=0, tiled=True)
    block_size = block_rows(shard_rows.shape[0])
    grouped = shard_rows.reshape(shard_rows.shape[0] // block_size, block_size, 2 * HS)

    def absorb(carried, key_block):
        row_peak, row_total, gathered = carried
        scores = jnp.dot(query_sel, key_block[:, :HS].T, preferred_element_type=f32) * scaling
        new_peak = jnp.maximum(row_peak, jnp.max(scores, -1))
        fading = jnp.exp(row_peak - new_peak)
        weights = jnp.exp(scores - new_peak[:, None])
        row_total = row_total * fading + jnp.sum(weights, -1)
        gathered = gathered * fading[:, None] + jnp.dot(
            weights.astype(bf16), key_block[:, HS:], preferred_element_type=f32
        )
        return ((new_peak, row_total, gathered), None)

    running, unused = lax.scan(absorb, running, grouped)
    row_peak, row_total, gathered = running
    heads_out = gathered / row_total[:, None]
    log_total = row_peak + jnp.log(row_total)
    heads_view = heads_out.reshape(tokens, MOA_TOP, HS)
    mixed_sel = (head_gates[:, :, None] * heads_view).astype(bf16)
    chosen_low = chosen.astype(bf16)
    mixture = jnp.sum(chosen_low[:, :, :, None] * mixed_sel[:, :, None, :], 1).reshape(
        tokens, MOA_EXPERTS * HS
    )
    middle = resident + jnp.dot(mixture, project_full, preferred_element_type=f32)
    normed_two, normal_two, inverse_two = layer_norm(middle, gain_second, biastwo_full.astype(f32))
    entering = normed_two.astype(bf16)
    route_ids = ffn_ids[0]
    picked = one_hot(route_ids, experts)
    expert_logits = jnp.sum(
        picked * jnp.dot(entering, selector_full, preferred_element_type=f32)[:, None, :], -1
    )
    expert_gates = jax.nn.softmax(expert_logits, -1)
    slots = expert_slots(route_ids, experts)
    target = (route_ids * capacity + slots).reshape(-1)
    copies = jnp.broadcast_to(entering[:, None, :], (tokens, FFN_TOP, D)).reshape(-1, D)
    outgoing = (
        jnp.zeros((experts * capacity, D), bf16)
        .at[target]
        .set(copies)
        .reshape(devices, EXP_DEV, capacity, D)
    )
    arrived_rows = lax.all_to_all(outgoing, "ctx", split_axis=0, concat_axis=0, tiled=True)
    before = jnp.einsum("nekd,edf->nekf", arrived_rows, inner_full, preferred_element_type=f32)
    activated = jax.nn.gelu(before, approximate=False).astype(bf16)
    result_rows = jnp.einsum(
        "nekf,efd->nekd", activated, outer_full, preferred_element_type=f32
    ).astype(bf16)
    returned = lax.all_to_all(result_rows, "ctx", split_axis=0, concat_axis=0, tiled=True).reshape(
        experts * capacity, D
    )
    expert_rows = returned[target].reshape(tokens, FFN_TOP, D).astype(f32)
    final = middle + jnp.sum(expert_gates[:, :, None] * expert_rows, 1)
    halting = jax.nn.sigmoid(jnp.dot(final, halt_vector, precision=HIGH))
    left_mass = remaining[0]
    stopped = left_mass * halting
    new_states = (stopped[:, None] * resident + (1.0 - stopped)[:, None] * final).astype(bf16)
    remaining_next = left_mass * (1.0 - halting)
    out_grad = out_cotangent[0]
    left_grad = left_cotangent[0]
    stop_grad = jnp.sum(out_grad * (resident - final), -1)
    grad_remaining = stop_grad * halting + left_grad * (1.0 - halting)
    halt_logit_grad = (stop_grad - left_grad) * left_mass * halting * (1.0 - halting)
    grad_halt = jnp.sum(halt_logit_grad[:, None] * final, 0)
    grad_final = (1.0 - stopped)[:, None] * out_grad + halt_logit_grad[:, None] * halt_vector
    gate_grad = jnp.sum(grad_final[:, None, :] * expert_rows, -1)
    selector_logit_grad = jnp.sum(choose_back(expert_gates, gate_grad)[:, :, None] * picked, 1)
    entering_wide = entering.astype(f32)
    grad_selector = jnp.dot(entering_wide.T, selector_logit_grad, precision=HIGH)
    rows_grad = (expert_gates[:, :, None] * grad_final[:, None, :]).astype(bf16).reshape(-1, D)
    grad_outgoing = (
        jnp.zeros((experts * capacity, D), bf16)
        .at[target]
        .set(rows_grad)
        .reshape(devices, EXP_DEV, capacity, D)
    )
    grad_arrived = lax.all_to_all(grad_outgoing, "ctx", split_axis=0, concat_axis=0, tiled=True)
    grad_activated = jnp.einsum(
        "nekd,efd->nekf", grad_arrived, outer_full, preferred_element_type=f32
    )
    activated_again, gelu_back = jax.vjp(partial(jax.nn.gelu, approximate=False), before)
    before_grad = gelu_back(grad_activated)[0].astype(bf16)
    outer_grad = jnp.einsum(
        "nekf,nekd->efd", activated_again.astype(bf16), grad_arrived, preferred_element_type=f32
    )
    inner_grad = jnp.einsum("nekd,nekf->edf", arrived_rows, before_grad, preferred_element_type=f32)
    grad_sent = jnp.einsum(
        "nekf,edf->nekd", before_grad, inner_full, preferred_element_type=f32
    ).astype(bf16)
    grad_back = lax.all_to_all(grad_sent, "ctx", split_axis=0, concat_axis=0, tiled=True).reshape(
        experts * capacity, D
    )
    entering_grad = jnp.sum(grad_back[target].reshape(tokens, FFN_TOP, D).astype(f32), 1)
    entering_grad = entering_grad + jnp.dot(
        selector_logit_grad, selector_full.astype(f32).T, precision=HIGH
    )
    middle_extra, grad_gain_two, grad_bias_two = norm_back(
        entering_grad, normal_two, inverse_two, gain_second
    )
    middle_grad = grad_final + middle_extra
    attn_grad = middle_grad.astype(bf16)
    grad_project = jnp.dot(mixture.T, attn_grad, preferred_element_type=f32)
    mix_grad = jnp.dot(attn_grad, project_full.T, preferred_element_type=f32).reshape(
        tokens, MOA_EXPERTS, HS
    )
    mix_sel_grad = jnp.take_along_axis(mix_grad, head_ids[:, :, None], axis=1)
    head_gate_grad = jnp.sum(mix_sel_grad * heads_view, -1)
    chooser_logit_grad = jnp.sum(choose_back(head_gates, head_gate_grad)[:, :, None] * chosen, 1)
    acted_wide = acted.astype(f32)
    grad_chooser = jnp.dot(acted_wide.T, chooser_logit_grad, precision=HIGH)
    acted_grad = jnp.dot(chooser_logit_grad, chooser_full.astype(f32).T, precision=HIGH)
    heads_grad = (head_gates[:, :, None] * mix_sel_grad).astype(bf16).reshape(rows_total, HS)
    row_delta = jnp.sum(heads_grad.astype(f32) * heads_out, -1)

    def cycle_turn(turn_index, carried):
        visiting, grads_visiting, query_grad = carried
        block_size = block_rows(tokens)

        def per_block(query_acc, key_block):
            scores = jnp.dot(query_sel, key_block[:, :HS].T, preferred_element_type=f32) * scaling
            probability = jnp.exp(scores - log_total[:, None])
            prob_grad = jnp.dot(heads_grad, key_block[:, HS:].T, preferred_element_type=f32)
            score_grad = (probability * (prob_grad - row_delta[:, None])).astype(bf16)
            query_acc = (
                query_acc
                + jnp.dot(score_grad, key_block[:, :HS], preferred_element_type=f32) * scaling
            )
            keys_grad = jnp.dot(score_grad.T, query_sel, preferred_element_type=f32) * scaling
            values_grad = jnp.dot(
                probability.astype(bf16).T, heads_grad, preferred_element_type=f32
            )
            return (query_acc, jnp.concatenate([keys_grad, values_grad], -1))

        query_grad, block_grads = lax.scan(
            per_block, query_grad, visiting.reshape(tokens // block_size, block_size, 2 * HS)
        )
        grads_visiting = grads_visiting + block_grads.reshape(tokens, 2 * HS)
        visiting = shifted(visiting, "ctx", 1)
        grads_visiting = shifted(grads_visiting.astype(jnp.bfloat16), "ctx", 1).astype(
            grads_visiting.dtype
        )
        return (visiting, grads_visiting, query_grad)

    cycle_state = (keyval, jnp.zeros((tokens, 2 * HS), f32), jnp.zeros((rows_total, HS), f32))
    unused_keys, keyval_grad, query_grad = lax.fori_loop(0, devices, cycle_turn, cycle_state)
    query_sel_grad = query_grad.astype(bf16).reshape(tokens, MOA_TOP, HS)
    query_all_grad = jnp.sum(chosen_low[:, :, :, None] * query_sel_grad[:, :, None, :], 1).reshape(
        tokens, MOA_EXPERTS * HS
    )
    keyval_low = keyval_grad.astype(bf16)
    grad_query = jnp.dot(acted.T, query_all_grad, preferred_element_type=f32)
    grad_keyval = jnp.dot(acted.T, keyval_low, preferred_element_type=f32)
    acted_grad = acted_grad + jnp.dot(query_all_grad, query_full.T, preferred_element_type=f32)
    acted_grad = acted_grad + jnp.dot(keyval_low, keyval_full.T, preferred_element_type=f32)
    resident_grad, grad_gain_one, grad_bias_one = norm_back(
        acted_grad, normal_one, inverse_one, gain_first
    )
    grad_states = middle_grad + resident_grad + stopped[:, None] * out_grad
    dense_grads = (
        grad_query,
        grad_keyval,
        grad_project,
        grad_chooser,
        grad_selector,
        grad_gain_one,
        grad_bias_one,
        grad_gain_two,
        grad_bias_two,
        grad_halt,
    )
    totals = (
        lax.psum(dense_grads[0].astype(jnp.bfloat16), "ctx").astype(jnp.float32),
        lax.psum(dense_grads[1].astype(jnp.bfloat16), "ctx").astype(jnp.float32),
        lax.psum(dense_grads[2].astype(jnp.bfloat16), "ctx").astype(jnp.float32),
        lax.psum(dense_grads[3].astype(jnp.bfloat16), "ctx").astype(jnp.float32),
        lax.psum(dense_grads[4].astype(jnp.bfloat16), "ctx").astype(jnp.float32),
        lax.psum(dense_grads[5].astype(jnp.bfloat16), "ctx").astype(jnp.float32),
        lax.psum(dense_grads[6].astype(jnp.bfloat16), "ctx").astype(jnp.float32),
        lax.psum(dense_grads[7].astype(jnp.bfloat16), "ctx").astype(jnp.float32),
        lax.psum(dense_grads[8].astype(jnp.bfloat16), "ctx").astype(jnp.float32),
        lax.psum(dense_grads[9].astype(jnp.bfloat16), "ctx").astype(jnp.float32),
    )
    shards = (
        lax.psum_scatter(
            totals[0].astype(jnp.bfloat16), ("seq", "wsh"), scatter_dimension=0, tiled=True
        ).astype(jnp.float32),
        lax.psum_scatter(
            totals[1].astype(jnp.bfloat16), ("seq", "wsh"), scatter_dimension=0, tiled=True
        ).astype(jnp.float32),
        lax.psum_scatter(
            totals[2].astype(jnp.bfloat16), ("seq", "wsh"), scatter_dimension=0, tiled=True
        ).astype(jnp.float32),
        lax.psum_scatter(
            totals[3].astype(jnp.bfloat16), ("seq", "wsh"), scatter_dimension=0, tiled=True
        ).astype(jnp.float32),
        lax.psum_scatter(
            totals[4].astype(jnp.bfloat16), ("seq", "wsh"), scatter_dimension=0, tiled=True
        ).astype(jnp.float32),
        lax.psum_scatter(
            totals[5].astype(jnp.bfloat16), ("seq", "wsh"), scatter_dimension=0, tiled=True
        ).astype(jnp.float32),
        lax.psum_scatter(
            totals[6].astype(jnp.bfloat16), ("seq", "wsh"), scatter_dimension=0, tiled=True
        ).astype(jnp.float32),
        lax.psum_scatter(
            totals[7].astype(jnp.bfloat16), ("seq", "wsh"), scatter_dimension=0, tiled=True
        ).astype(jnp.float32),
        lax.psum_scatter(
            totals[8].astype(jnp.bfloat16), ("seq", "wsh"), scatter_dimension=0, tiled=True
        ).astype(jnp.float32),
        lax.psum_scatter(
            totals[9].astype(jnp.bfloat16), ("seq", "wsh"), scatter_dimension=0, tiled=True
        ).astype(jnp.float32),
    )
    inner_shard, outer_shard = (
        lax.psum_scatter(
            inner_grad.astype(jnp.bfloat16), ("seq", "wsh"), scatter_dimension=1, tiled=True
        ).astype(jnp.float32),
        lax.psum_scatter(
            outer_grad.astype(jnp.bfloat16), ("seq", "wsh"), scatter_dimension=1, tiled=True
        ).astype(jnp.float32),
    )
    return (
        new_states[None],
        remaining_next[None],
        grad_states[None],
        grad_remaining[None],
        shards[0],
        shards[1],
        shards[2],
        shards[3],
        shards[4],
        shards[5],
        shards[6],
        shards[7],
        shards[8],
        shards[9],
        inner_shard,
        outer_shard,
    )


MESH = pl.DeviceIdType.MESH
CAP = 192
LIMIT_MIB = 62
KEEP = 0.7071067811865476
SPREAD = 0.3989422804014327
ERF_P = 0.3275911
ERF_A = (0.254829592, -0.284496736, 1.421413741, -1.453152027, 1.061405429)


def remote(source, target, send_sem, recv_sem, device):
    return pltpu.make_async_remote_copy(
        src_ref=source,
        dst_ref=target,
        send_sem=send_sem,
        recv_sem=recv_sem,
        device_id=device,
        device_id_type=MESH,
    )


def places():
    ctx, seq, wsh = (lax.axis_index(name) for name in ("ctx", "seq", "wsh"))
    chip, core = seq // 2, seq % 2
    over = (1 - chip) * 2 + core
    twin = (ctx, chip * 2 + 1 - core, wsh)
    beside = (ctx, over, wsh)
    above = (ctx, seq, 1 - wsh)
    across = (ctx, over, 1 - wsh)
    return (ctx, seq, wsh), twin, beside, above, across


def shard_of(place):
    return place[1] * 2 + place[2]


def moved(place, offset, length):
    return ((place[0] + offset) % length, place[1], place[2])


def plane_peer(place, step):
    shard = (shard_of(place) + step) % 8
    return (place[0], shard // 2, shard % 2)


class PlaneGather:
    def __init__(self, shard, full, halves, send, recv, local):
        self.shard, self.full, self.halves = shard, full, halves
        self.send, self.recv, self.local = send, recv, local
        self.me, self.twin, self.beside, self.above, self.across = places()

    def pair(self, view, slot, device):
        return remote(view, view, self.send.at[slot], self.recv.at[slot], device)

    def own(self, slot, device):
        target = self.full(shard_of(self.me))
        return remote(self.shard, target, self.send.at[slot], self.recv.at[slot], device)

    def keep(self):
        return pltpu.make_async_copy(self.shard, self.full(shard_of(self.me)), self.local)

    def start(self):
        self.own(0, self.twin).start()
        self.own(1, self.beside).start()
        self.own(2, self.above).start()
        if self.halves is None:
            self.own(3, self.across).start()
        self.keep().start()

    def arrive(self, slot, place):
        self.pair(self.full(shard_of(place)), slot, self.twin).wait_recv()

    def relay(self):
        if self.halves is None:
            for slot, place in ((1, self.beside), (2, self.above), (3, self.across)):
                self.arrive(slot, place)
                self.pair(self.full(shard_of(place)), slot + 3, self.twin).start()
            return
        self.arrive(1, self.beside)
        self.pair(self.halves(shard_of(self.beside), 1), 7, self.above).start()
        self.pair(self.full(shard_of(self.beside)), 4, self.twin).start()
        self.arrive(2, self.above)
        self.pair(self.halves(shard_of(self.above), 0), 3, self.beside).start()
        self.pair(self.full(shard_of(self.above)), 5, self.twin).start()

    def relay_rest(self):
        shard = shard_of(self.across)
        for slot, half in ((3, 0), (7, 1)):
            view = self.halves(shard, half)
            self.pair(view, slot, self.twin).wait_recv()
            self.pair(view, 6 if half == 0 else 8, self.twin).start()

    def finish(self):
        self.keep().wait()
        ctx, seq, wsh = self.twin
        over = (1 - seq // 2) * 2 + seq % 2
        self.arrive(0, self.twin)
        self.arrive(4, (ctx, over, wsh))
        self.arrive(5, (ctx, seq, 1 - wsh))
        rest = shard_of((ctx, over, 1 - wsh))
        if self.halves is None:
            self.pair(self.full(rest), 6, self.twin).wait_recv()
        else:
            self.pair(self.halves(rest, 0), 6, self.twin).wait_recv()
            self.pair(self.halves(rest, 1), 8, self.twin).wait_recv()

    def drain(self):
        self.own(0, self.twin).wait_send()
        self.own(1, self.beside).wait_send()
        self.own(2, self.above).wait_send()
        beside, above, across = (shard_of(p) for p in (self.beside, self.above, self.across))
        self.pair(self.full(beside), 4, self.twin).wait_send()
        self.pair(self.full(above), 5, self.twin).wait_send()
        if self.halves is None:
            self.own(3, self.across).wait_send()
            self.pair(self.full(across), 6, self.twin).wait_send()
        else:
            self.pair(self.halves(above, 0), 3, self.beside).wait_send()
            self.pair(self.halves(beside, 1), 7, self.above).wait_send()
            self.pair(self.halves(across, 0), 6, self.twin).wait_send()
            self.pair(self.halves(across, 1), 8, self.twin).wait_send()


class PlaneShare:
    def __init__(self, blocks, send, recv):
        self.blocks, self.send, self.recv = blocks, send, recv
        self.me = places()[0]
        self.shard = shard_of(self.me)

    def copy(self, shard, step, device):
        view = self.blocks.at[shard]
        return remote(view, view, self.send.at[step - 1], self.recv.at[step - 1], device)

    def sends(self):
        return [self.copy(self.shard, step, plane_peer(self.me, step)) for step in range(1, 8)]

    def wait(self):
        for step in range(1, 8):
            source = plane_peer(self.me, 8 - step)
            self.copy(shard_of(source), step, source).wait_recv()


class LineGather:
    def __init__(self, length, blocks, send, recv):
        self.length, self.blocks, self.send, self.recv = length, blocks, send, recv
        self.me = places()[0]

    def hop(self, block, way, step, device):
        view = self.blocks(block)
        return remote(view, view, self.send.at[way, step], self.recv.at[way, step], device)

    def ways(self, step):
        ctx = self.me[0]
        left = (ctx - 1, self.me[1], self.me[2])
        right = (ctx + 1, self.me[1], self.me[2])
        return (
            (0, ctx - step, ctx - step >= 0, right, ctx + 1 < self.length),
            (1, ctx + step, ctx + step < self.length, left, ctx - 1 >= 0),
        )

    def start(self):
        for way, block, unused, device, there in self.ways(0):
            pl.when(there)(lambda b=block, w=way, d=device: self.hop(b, w, 0, d).start())

    def relay(self, step):
        for way, block, come, device, there in self.ways(step):

            def pass_on(way=way, block=block, device=device, there=there):
                self.hop(block, way, step - 1, device).wait_recv()
                if step < self.length - 1:
                    pl.when(there)(lambda: self.hop(block, way, step, device).start())

            pl.when(come)(pass_on)

    def drain(self):
        for step in range(self.length - 1):
            for way, block, come, device, there in self.ways(step):
                pl.when(jnp.logical_and(come, there))(
                    lambda b=block, w=way, d=device, s=step: self.hop(b, w, s, d).wait_send()
                )


def direct_send(view, send, recv, length):
    me = places()[0]
    return [
        remote(view, view, send.at[step - 1], recv.at[step - 1], moved(me, step, length))
        for step in range(1, length)
    ]


def direct_wait(view_of, send, recv, length):
    me = places()[0]
    for step in range(1, length):
        source = moved(me, length - step, length)
        view = view_of(source[0])
        remote(view, view, send.at[step - 1], recv.at[step - 1], source).wait_recv()


def lanes_of(shape):
    return lax.broadcasted_iota(jnp.int32, shape, 1)


def rows_of(shape):
    return lax.broadcasted_iota(jnp.int32, shape, 0)


def product(left, right, dims=((1,), (0,))):
    return lax.dot_general(left, right, (dims, ((), ())), preferred_element_type=jnp.float32)


def gelu_parts(values):
    near = jnp.abs(values) * KEEP
    turn = 1.0 / (1.0 + ERF_P * near)
    bell = jnp.exp(-near * near)
    series = ERF_A[4]
    for term in ERF_A[3::-1]:
        series = series * turn + term
    tail = 0.5 * series * turn * bell
    share = jnp.where(values >= 0, 1.0 - tail, tail)
    return values * share, share + values * bell * SPREAD


def picks(r, block, expert):
    tokens = r.states.shape[0]
    row = r.routes[block, pl.ds(EXP_DEV * lax.axis_index("ctx") + expert, 1), :]
    return (rows_of((CAP, tokens)).astype(jnp.float32) == row).astype(jnp.float32)


def slots(block):
    return pl.ds(pl.multiple_of(block * CAP, CAP), CAP)


def to_owner(length, r, view, target, row, block):
    me = places()[0]
    slot = (block - me[0] + length) % length - 1
    send, recv = r.direct_sems.at[row, slot], r.direct_recvs.at[row, slot]
    return remote(view, target.at[slot], send, recv, (block, me[1], me[2]))


def give_back(length, r, block):
    total = 0.0
    for expert in range(EXP_DEV):
        chosen = picks(r, block, expert).astype(jnp.bfloat16)
        total = total + product(chosen, r.result[expert, slots(block), :], ((0,), (0,)))
    r.cots[block] = total.astype(jnp.bfloat16)


def returns(length, r):
    return (
        LineReturn(length, r.cots, r.mix_in, r.return_send.at[0], r.return_recv.at[0]),
        LineReturn(length, r.entering, r.back_in, r.return_send.at[1], r.return_recv.at[1]),
    )


def forward_part(length, r):
    f32, bf16 = jnp.float32, jnp.bfloat16
    tokens = r.states.shape[0]
    me, twin, beside, above, across = places()
    ctx = me[0]
    peers = [plane_peer(me, k) for k in range(1, 8)] + [moved(me, k, length) for k in range(1, length)]
    barrier = pltpu.get_barrier_semaphore()
    for peer in peers:
        pl.semaphore_signal(barrier, inc=1, device_id=peer, device_id_type=MESH)

    def gather(index, shard, full, halves=None):
        return PlaneGather(
            shard, full, halves, r.plane_send.at[index], r.plane_recv.at[index], r.plane_local.at[index]
        )

    def rows_view(ref, rows):
        return lambda shard: ref.at[pl.ds(shard * rows, rows), :]

    def half_view(ref, rows):
        return lambda shard, half: ref.at[pl.ds(shard * rows + half * (rows // 2), rows // 2), :]

    pack_share = PlaneShare(r.packs, r.pack_send, r.pack_recv)
    query_gather = gather(0, r.query_part, rows_view(r.query, 64), half_view(r.query, 64))
    project_gather = gather(1, r.project_part, rows_view(r.project, 192), half_view(r.project, 192))
    inner_gather = gather(
        2,
        r.inner_part,
        lambda shard: r.inner.at[:, pl.ds(shard * 64, 64), :],
        lambda shard, half: r.inner.at[half, pl.ds(shard * 64, 64), :],
    )
    outer_gathers = [
        gather(
            3 + k, r.outer_part.at[k], rows_view(r.outer.at[k], 256), half_view(r.outer.at[k], 256)
        )
        for k in range(EXP_DEV)
    ]
    cot_gather = LineGather(length, lambda b: r.cots.at[b], r.line_send.at[0], r.line_recv.at[0])
    entering_gather = LineGather(length, lambda b: r.entering.at[b], r.line_send.at[1], r.line_recv.at[1])

    def keyval_view(block):
        return r.keyval.at[pl.ds(block * tokens, tokens), :]

    fetch = pltpu.make_async_copy(r.cotangent_part, r.cotangent, r.plane_local.at[5])
    fetch.start()
    shard = shard_of(me)
    r.packs[shard, 0:64, :] = r.keyval_part[...]
    rows = [r.chooser_part[...].astype(f32), r.selector_part[...].astype(f32), r.vectors[...].astype(f32)]
    rows = jnp.concatenate([*rows, jnp.zeros((8, 64), f32)], 0)
    r.packs[shard, 64:112, :] = jnp.concatenate([rows, jnp.zeros((48, 64), f32)], 1).astype(bf16)
    pl.semaphore_wait(barrier, len(peers))
    pack_sends = pack_share.sends()
    for copy in pack_sends:
        copy.start()
    query_gather.start()
    project_gather.start()
    fetch.wait()
    r.cots[ctx] = r.cotangent[...].astype(bf16)
    cot_gather.start()

    values = r.states[...].astype(f32)
    centred = values - jnp.mean(values, -1, keepdims=True)
    inverse = lax.rsqrt(jnp.mean(centred * centred, -1, keepdims=True) + EPS)
    r.grad_states[...] = centred * inverse

    lane = lanes_of((tokens, 128))
    turned = r.route_ids[...].astype(f32)
    expert_row = rows_of((8, tokens)).astype(f32)
    picked = jnp.logical_or(expert_row == turned[0:1], expert_row == turned[1:2])
    marks = jnp.concatenate([picked.astype(f32), jnp.zeros((8, tokens), f32)], 0).astype(bf16)
    earlier = (rows_of((tokens, tokens)) < lanes_of((tokens, tokens))).astype(f32).astype(bf16)
    ranks = product(marks, earlier)[0:8]
    r.routes[ctx, 0:8, :] = jnp.where(picked, ranks, -1.0)

    ids = jnp.concatenate([r.head_ids[...].astype(f32), jnp.zeros((124, tokens), f32)], 0)
    r.id_columns[...] = jnp.transpose(ids).astype(jnp.int32)
    r.small[48:128, :] = jnp.zeros((80, D), f32)
    pack_share.wait()
    for pair in range(4):
        sides = [r.packs[2 * pair + k, 64:112, :].astype(f32) for k in range(2)]
        both = jnp.where(lanes_of((48, 128)) < 64, sides[0], pltpu.roll(sides[1], 64, 1))
        r.small[0:48, pair * 128 : pair * 128 + 128] = both
    keyval_weight = r.packs[:, 0:64, :].reshape(D, 128)
    shaped = (r.grad_states[...] * r.small[32:33, :] + r.small[33:34, :]).astype(bf16)
    r.acted[...] = shaped
    keyval_view(ctx)[...] = product(shaped, keyval_weight).astype(bf16)
    keyval_sends = direct_send(keyval_view(ctx), r.direct_sems.at[0], r.direct_recvs.at[0], length)
    for copy in keyval_sends:
        copy.start()
    query_gather.relay()

    id_lanes = [r.id_columns[:, j : j + 1] for j in range(MOA_TOP)]
    choice = product(shaped, r.small[...].astype(bf16), ((1,), (1,)))
    logits = [
        jnp.sum(jnp.where(lane == id_lanes[j], choice, 0.0), -1, keepdims=True)
        for j in range(MOA_TOP)
    ]
    peak = jnp.maximum(jnp.maximum(logits[0], logits[1]), jnp.maximum(logits[2], logits[3]))
    powers = [jnp.exp(item - peak) for item in logits]
    total = powers[0] + powers[1] + powers[2] + powers[3]
    gates = [item / total for item in powers]
    r.columns[...] = jnp.where(
        lane == 8,
        gates[0],
        jnp.where(lane == 9, gates[1], jnp.where(lane == 10, gates[2], gates[3])),
    )

    query_gather.relay_rest()
    project_gather.relay()
    inner_gather.start()
    outer_gathers[0].start()
    query_gather.finish()
    for part in range(6):
        columns = slice(part * 256, part * 256 + 256)
        r.mixture[:, columns] = product(r.acted[...], r.query[:, columns]).astype(bf16)
    cot_gather.relay(1)

    low_half = lane < HS
    side = lane // HS
    for j in range(MOA_TOP):
        wanted = id_lanes[j] - side
        chosen = jnp.zeros((tokens, 128), f32)
        for pair in range(MOA_EXPERTS // 2):
            block = r.mixture[:, pair * 128 : pair * 128 + 128].astype(f32)
            chosen = chosen + jnp.where(wanted == 2 * pair, block, 0.0)
        folded = chosen + pltpu.roll(chosen, HS, 1)
        r.queries[j * tokens : (j + 1) * tokens, :] = (
            jnp.where(low_half, folded, 0.0) * HS ** (-0.5)
        ).astype(bf16)

    project_gather.relay_rest()
    direct_wait(keyval_view, r.direct_sems.at[0], r.direct_recvs.at[0], length)
    chunk = 256

    def attend(turn, carried):
        rows = pl.ds(pl.multiple_of(turn * chunk, chunk), chunk)
        scores = product(r.queries[rows, :], r.keyval[...], ((1,), (1,)))
        top = jnp.max(scores, -1, keepdims=True)
        weights = jnp.exp(scores - top)
        mass = jnp.sum(weights, -1, keepdims=True)
        seen = product(weights.astype(bf16), r.keyval[...]) / mass
        r.heads[rows, :] = jnp.where(lanes_of((chunk, 128)) < HS, top + jnp.log(mass), seen)
        return carried

    lax.fori_loop(0, MOA_TOP * tokens // chunk, attend, 0)

    spread = []
    for j in range(MOA_TOP):
        head = r.heads[j * tokens : (j + 1) * tokens, :]
        both = jnp.where(low_half, pltpu.roll(head, HS, 1), head)
        spread.append(both * r.columns[:, 8 + j : 9 + j])
    for pair in range(MOA_EXPERTS // 2):
        block = jnp.zeros((tokens, 128), f32)
        for j in range(MOA_TOP):
            block = jnp.where(id_lanes[j] - side == 2 * pair, spread[j], block)
        r.mixture[:, pair * 128 : pair * 128 + 128] = block.astype(bf16)

    project_gather.finish()
    between = r.states[...].astype(f32) + product(r.mixture[...], r.project[...])
    r.middle[...] = between
    reach = jnp.sum(between * r.small[36:37, :], -1, keepdims=True)
    gap = jnp.sum(r.cotangent[...] * (r.states[...].astype(f32) - between), -1, keepdims=True)
    centred = between - jnp.mean(between, -1, keepdims=True)
    inverse = lax.rsqrt(jnp.mean(centred * centred, -1, keepdims=True) + EPS)
    entry = (centred * inverse * r.small[34:35, :] + r.small[35:36, :]).astype(bf16)
    r.entering[ctx] = entry
    entering_gather.start()
    logits = product(r.small[16:32, :].astype(bf16), entry, ((1,), (1,)))[8:16]
    peak = jnp.max(jnp.where(picked, logits, -1e30), 0, keepdims=True)
    powers = jnp.where(picked, jnp.exp(jnp.where(picked, logits - peak, 0.0)), 0.0)
    r.routes[ctx, 8:16, :] = powers / jnp.sum(powers, 0, keepdims=True)
    r.routes[ctx, 16:24, :] = jnp.transpose(jnp.where(lane == 0, reach, gap))[0:8]
    r.routes[ctx, 18:19, :] = r.remaining[...]
    r.routes[ctx, 19:20, :] = r.left_cot[...]
    route_sends = direct_send(r.routes.at[ctx], r.direct_sems.at[1], r.direct_recvs.at[1], length)
    for copy in route_sends:
        copy.start()

    def first_half(source):
        def one(expert, carried):
            chosen = picks(r, source, expert).astype(bf16)
            rows = product(chosen, r.entering[source]).astype(bf16)
            r.slot_rows[expert, slots(source), :] = rows

            def part(index, kept):
                columns = pl.ds(pl.multiple_of(index * 512, 512), 512)
                before = product(rows, r.inner[expert, :, columns])
                value, gradient = gelu_parts(before)
                r.active[expert, slots(source), columns] = value.astype(bf16)
                r.slope[expert, slots(source), columns] = gradient.astype(bf16)
                return kept

            return lax.fori_loop(0, 4, part, carried)

        lax.fori_loop(0, EXP_DEV, one, 0)

    def second_half(first, count):
        rows = pl.ds(pl.multiple_of(first * CAP, CAP), count * CAP)

        def one(expert, carried):
            value = product(r.active[expert, rows, :], r.outer[expert])
            r.result[expert, rows, :] = value.astype(bf16)
            return carried

        lax.fori_loop(0, EXP_DEV, one, 0)

    def score(source, carried):
        lines = []
        for expert in range(EXP_DEV):
            chosen = picks(r, source, expert)
            cot_rows = product(chosen.astype(bf16), r.cots[source]).astype(bf16)
            r.slot_cot[expert, slots(source), :] = cot_rows
            rows = r.result[expert, slots(source), :].astype(f32)
            toward = jnp.sum(rows * r.small[36:37, :], -1, keepdims=True)
            against = jnp.sum(rows * cot_rows.astype(f32), -1, keepdims=True)
            gate_row = r.routes[source, pl.ds(8 + EXP_DEV * ctx + expert, 1), :]
            gate = jnp.sum(chosen * gate_row, -1, keepdims=True)
            r.result[expert, slots(source), :] = (rows * gate).astype(bf16)
            lines.append(jnp.sum(chosen * toward, 0, keepdims=True))
            lines.append(jnp.sum(chosen * against, 0, keepdims=True))
        lines.append(jnp.zeros((8 - 2 * EXP_DEV, tokens), f32))
        sheet = jnp.concatenate(lines, 0)

        r.scores[ctx, source] = sheet
        return carried

    lower = ctx < length // 2
    last = jnp.where(lower, length - 1, 0)
    at_end = jnp.logical_or(ctx == 0, ctx == length - 1)

    def arrival(turn):
        along = jnp.where(lower, turn, length - 1 - turn)
        around = jnp.where(turn == 0, ctx, jnp.where(turn == 1, ctx - 1, ctx + 1))
        return jnp.where(at_end, along, around)

    inner_gather.relay()
    outer_gathers[1].start()
    direct_wait(lambda b: r.routes.at[b], r.direct_sems.at[1], r.direct_recvs.at[1], length)
    entering_gather.relay(1)
    inner_gather.relay_rest()
    inner_gather.finish()
    outer_gathers[0].relay()

    def near(turn, carried):
        @pl.when(turn == 1)
        def _():
            entering_gather.relay(2)
            cot_gather.relay(2)

        @pl.when(turn == 2)
        def _():
            outer_gathers[1].relay()
            outer_gathers[0].relay_rest()

        first_half(arrival(turn))
        return carried

    lax.fori_loop(0, length - 1, near, 0)
    outer_gathers[1].relay_rest()
    for item in outer_gathers:
        item.finish()
    second_half(jnp.where(lower, 0, 1), length - 1)
    lax.fori_loop(0, length - 1, lambda turn, carried: score(arrival(turn), carried), 0)
    entering_gather.relay(length - 1)
    first_half(last)
    second_half(last, 1)
    cot_gather.relay(length - 1)
    score(last, 0)
    cot_gather.drain()
    score_sends = direct_send(r.scores.at[ctx], r.direct_sems.at[2], r.direct_recvs.at[2], length)
    for copy in score_sends:
        copy.start()
    mixed, unused = returns(length, r)
    for index in range(2):
        give_back(length, r, mixed.far + index)
    direct_wait(lambda b: r.scores.at[b], r.direct_sems.at[2], r.direct_recvs.at[2], length)
    for copy in keyval_sends + route_sends + score_sends:
        copy.wait_send()
    for copy in pack_sends:
        copy.wait_send()
    for item in (query_gather, project_gather, inner_gather, *outer_gathers):
        item.drain()
    entering_gather.drain()


class LineReturn:
    def __init__(self, length, parts, arrived, send, recv):
        self.length, self.parts, self.arrived = length, parts, arrived
        self.send, self.recv = send, recv
        self.me = places()[0]
        ctx = self.me[0]
        self.at_end = jnp.logical_or(ctx == 0, ctx == length - 1)
        self.inside = jnp.logical_not(self.at_end)
        self.next = (ctx + 1 - 2 * (ctx % 2), self.me[1], self.me[2])
        self.far = (1 - ctx // 2) * 2

    def copy(self, block, place, slot, device):
        return remote(
            self.parts.at[block], self.arrived.at[place], self.send.at[slot], self.recv.at[slot], device
        )

    def hand(self, index):
        return self.copy(self.far + index, index, index, self.next)

    def near(self):
        return self.copy(self.next[0], 2, 2, self.next)

    def across(self, index):
        block = self.far + index
        return self.copy(block, 3, 3 + index, (block, self.me[1], self.me[2]))

    def start_far(self, index):
        pl.when(self.at_end)(lambda: self.hand(index).start())

    def pass_on(self, index):
        @pl.when(self.inside)
        def _():
            self.hand(index).wait_recv()
            block = self.far + index
            both = self.parts[block].astype(jnp.float32) + self.arrived[index].astype(jnp.float32)
            self.parts[block] = both.astype(jnp.bfloat16)
            self.across(index).start()

    def start_near(self):
        self.near().start()

    def wait(self):
        self.near().wait_recv()
        self.across(self.me[0] % 2).wait_recv()

    def total(self):
        own = self.parts[self.me[0]].astype(jnp.float32)
        return own + self.arrived[2].astype(jnp.float32) + self.arrived[3].astype(jnp.float32)

    def drain(self):
        self.near().wait_send()
        for index in range(2):
            pl.when(self.at_end)(lambda i=index: self.hand(i).wait_send())
            pl.when(self.inside)(lambda i=index: self.across(i).wait_send())


class PlaneReduce:
    def __init__(self, piece, rows, halves, arrived, send, recv):
        self.piece, self.rows, self.halves, self.arrived = piece, rows, halves, arrived
        self.send, self.recv = send, recv
        self.me, self.twin, self.beside, self.above, self.across = places()
        self.chip, self.core, self.line = self.me[1] // 2, self.me[1] % 2, self.me[2]

    def half(self, chip, core):
        view, half = self.piece(chip, core), self.halves.at[chip]
        return remote(view, half, self.send.at[chip], self.recv.at[chip], self.twin)

    def shard(self, chip, line):
        return self.piece(chip, self.core).at[pl.ds(line * self.rows, self.rows), :]

    def start(self):
        for chip in range(2):
            self.half(chip, 1 - self.core).start()

    def spread(self, slot, chip, line, device):
        return remote(
            self.shard(chip, line),
            self.arrived.at[slot],
            self.send.at[2 + slot],
            self.recv.at[2 + slot],
            device,
        )

    def sends(self):
        return (
            self.spread(0, 1 - self.chip, self.line, self.beside),
            self.spread(1, self.chip, 1 - self.line, self.above),
            self.spread(2, 1 - self.chip, 1 - self.line, self.across),
        )

    def add_halves(self):
        for chip in range(2):
            self.half(chip, self.core).wait_recv()
            view = self.piece(chip, self.core)
            both = view[...].astype(jnp.float32) + self.halves[chip].astype(jnp.float32)
            view[...] = both.astype(jnp.bfloat16)
        for copy in self.sends():
            copy.start()

    def total(self):
        for copy in self.sends():
            copy.wait_recv()
        value = self.shard(self.chip, self.line)[...].astype(jnp.float32)
        for slot in range(3):
            value = value + self.arrived[slot].astype(jnp.float32)
        return value

    def drain(self):
        for chip in range(2):
            self.half(chip, 1 - self.core).wait_send()
        for copy in self.sends():
            copy.wait_send()


class LineSum:
    def __init__(self, length, value, parts, summed, reduce_sems, gather_sems):
        self.length, self.value, self.parts, self.summed = length, value, parts, summed
        self.reduce_sems, self.gather_sems = reduce_sems, gather_sems
        self.me = places()[0]
        self.share = value.shape[0] // length

    def rows(self, block):
        return pl.ds(pl.multiple_of(block * self.share, self.share), self.share)

    def part(self, step):
        target = moved(self.me, step, self.length)
        send, recv = self.reduce_sems
        return remote(
            self.value.at[self.rows(target[0]), :],
            self.parts.at[step - 1],
            send.at[step - 1],
            recv.at[step - 1],
            target,
        )

    def start(self, value):
        self.value[...] = value.astype(jnp.bfloat16)
        for step in range(1, self.length):
            self.part(step).start()

    def view(self, block):
        return self.summed.at[self.rows(block), :]

    def share_out(self):
        for step in range(1, self.length):
            self.part(step).wait_recv()
        value = self.value[self.rows(self.me[0]), :].astype(jnp.float32)
        for step in range(1, self.length):
            value = value + self.parts[step - 1].astype(jnp.float32)
        self.view(self.me[0])[...] = value.astype(jnp.bfloat16)
        for copy in direct_send(self.view(self.me[0]), *self.gather_sems, self.length):
            copy.start()

    def finish(self):
        direct_wait(self.view, *self.gather_sems, self.length)
        return self.summed[...]

    def drain(self):
        for step in range(1, self.length):
            self.part(step).wait_send()
        for copy in direct_send(self.view(self.me[0]), *self.gather_sems, self.length):
            copy.wait_send()


class ExpertReduce:
    def __init__(self, inner, outer, half_in, half_out, side_in, side_out, last_in, last_out, send, recv):
        self.arrays = (inner, outer)
        self.halves = (half_in, half_out)
        self.sides = (side_in, side_out)
        self.lasts = (last_in, last_out)
        self.counts = (64, 256)
        self.send, self.recv = send, recv
        self.me, self.twin, self.beside, self.above, unused = places()
        self.chip, self.core, self.line = self.me[1] // 2, self.me[1] % 2, self.me[2]

    def rows(self, which, expert, chip, core, line, count):
        size = self.counts[which]
        start = pl.multiple_of(((chip * 2 + core) * 2 + line) * size, size)
        return self.arrays[which].at[expert, pl.ds(start, count * size), :]

    def copy(self, source, target, which, expert, slot, device):
        unit = 2 * which + expert
        return remote(source, target, self.send.at[unit, slot], self.recv.at[unit, slot], device)

    def half(self, which, expert, chip, core):
        source = self.rows(which, expert, chip, core, 0, 2)
        return self.copy(source, self.halves[which].at[chip, expert], which, expert, chip, self.twin)

    def start(self, which):
        for expert in range(EXP_DEV):
            for chip in range(2):
                self.half(which, expert, chip, 1 - self.core).start()

    def side(self, which, expert, index):
        if expert == 0:
            source, device = self.rows(which, 0, 1 - self.chip, self.core, index, 1), self.beside
        else:
            source, device = self.rows(which, 1, index, self.core, 1 - self.line, 1), self.above
        return self.copy(source, self.sides[which].at[expert, index], which, expert, 2 + index, device)

    def add(self, view, other):
        view[...] = (view[...].astype(jnp.float32) + other[...].astype(jnp.float32)).astype(jnp.bfloat16)

    def add_halves(self, which):
        for expert in range(EXP_DEV):
            for chip in range(2):
                self.half(which, expert, chip, self.core).wait_recv()
                self.add(self.rows(which, expert, chip, self.core, 0, 2), self.halves[which].at[chip, expert])
            for index in range(2):
                self.side(which, expert, index).start()

    def last(self, which, expert):
        if expert == 0:
            source, device = self.rows(which, 0, self.chip, self.core, 1 - self.line, 1), self.above
        else:
            source, device = self.rows(which, 1, 1 - self.chip, self.core, self.line, 1), self.beside
        return self.copy(source, self.lasts[which].at[expert], which, expert, 4, device)

    def add_sides(self, which):
        for expert in range(EXP_DEV):
            for index in range(2):
                self.side(which, expert, index).wait_recv()
                chip, line = (self.chip, index) if expert == 0 else (index, self.line)
                self.add(
                    self.rows(which, expert, chip, self.core, line, 1), self.sides[which].at[expert, index]
                )
            self.last(which, expert).start()

    def total(self, which, result):
        for expert in range(EXP_DEV):
            self.last(which, expert).wait_recv()
            view = self.rows(which, expert, self.chip, self.core, self.line, 1)
            both = view[...].astype(jnp.float32) + self.lasts[which][expert].astype(jnp.float32)
            result[expert] = both.astype(jnp.bfloat16)

    def drain(self):
        for which in range(2):
            for expert in range(EXP_DEV):
                for chip in range(2):
                    self.half(which, expert, chip, 1 - self.core).wait_send()
                for index in range(2):
                    self.side(which, expert, index).wait_send()
                self.last(which, expert).wait_send()


def backward_part(length, r):
    f32, bf16 = jnp.float32, jnp.bfloat16
    tokens = r.states.shape[0]
    me = places()[0]
    ctx = me[0]
    lane = lanes_of((tokens, 128))
    low_half = lane < HS
    side = lane // HS
    id_lanes = [r.id_columns[:, j : j + 1] for j in range(MOA_TOP)]

    def sems(row):
        return r.direct_sems.at[row], r.direct_recvs.at[row]

    def from_all(target_ref, row):
        send, recv = sems(row)
        for step in range(1, length):
            view = target_ref.at[step - 1]
            source = moved(me, length - step, length)
            remote(view, view, send.at[step - 1], recv.at[step - 1], source).wait_recv()

    def sent_all(view_of, target_ref, row):
        for step in range(1, length):
            block = moved(me, step, length)[0]
            to_owner(length, r, view_of(block), target_ref, row, block).wait_send()

    r.gsmall[...] = jnp.zeros_like(r.gsmall)
    mid = r.middle[...]
    halt_row = r.small[36:37, :]

    def scalars(block):
        gates = r.routes[block, 8:16, :]
        lines = [
            [r.scores[d, block, 2 * e + k : 2 * e + k + 1, :] for d in range(length) for e in range(EXP_DEV)]
            for k in range(2)
        ]
        toward, against = (jnp.concatenate(item, 0) for item in lines)
        own = r.routes[block, 16:24, :]
        halting = jax.nn.sigmoid(own[0:1] + jnp.sum(gates * toward, 0, keepdims=True))
        stop_grad = own[1:2] - jnp.sum(gates * against, 0, keepdims=True)
        mass, left = own[2:3], own[3:4]
        stopped = mass * halting
        halt_grad = (stop_grad - left) * mass * halting * (1.0 - halting)
        sheet = jnp.concatenate([1.0 - stopped, halt_grad, stopped, jnp.zeros((5, tokens), f32)], 0)
        r.factors[block] = sheet
        return gates, toward, against, halting, stop_grad, mass, left, stopped, halt_grad, sheet

    def other(step, carried):
        scalars((ctx + step) % length)
        return carried

    lax.fori_loop(1, length, other, 0)
    gates, toward, against, halting, stop_grad, mass, left, stopped, halt_grad, sheet = scalars(ctx)
    mixed, backs = returns(length, r)
    mixed.start_far(0)
    r.rows_out[0:1, :] = mass * (1.0 - halting)
    r.rows_out[1:2, :] = stop_grad * halting + left * (1.0 - halting)
    turned = jnp.transpose(jnp.concatenate([sheet, jnp.zeros((120, tokens), f32)], 0))
    r.columns[...] = jnp.where(lane < 8, turned, r.columns[...])
    gate_grad = (1.0 - stopped) * against + halt_grad * toward
    pick_grad = gates * (gate_grad - jnp.sum(gates * gate_grad, 0, keepdims=True))
    coarse = pick_grad.astype(bf16).astype(f32)
    r.pick_grads[...] = jnp.concatenate([coarse, pick_grad - coarse], 0).astype(bf16)
    sums = product(r.pick_grads[...], r.entering[ctx])
    r.gsmall[24:32, :] = sums[0:8] + sums[8:16]
    halt_col = r.columns[:, 1:2]
    r.gsmall[36:37, :] = jnp.sum(halt_col * mid, 0, keepdims=True)

    def rows_back(block):
        for expert in range(EXP_DEV):
            chosen = picks(r, block, expert)
            keep = jnp.sum(chosen * r.factors[block, 0:1, :], -1, keepdims=True)
            halt = jnp.sum(chosen * r.factors[block, 1:2, :], -1, keepdims=True)
            gate_row = r.routes[block, pl.ds(8 + EXP_DEV * ctx + expert, 1), :]
            gate = jnp.sum(chosen * gate_row, -1, keepdims=True)
            rows = r.result[expert, slots(block), :].astype(f32)
            r.gsmall[36:37, :] += jnp.sum(halt * rows, 0, keepdims=True)
            incoming = r.slot_cot[expert, slots(block), :].astype(f32)
            rows_grad = (gate * (keep * incoming + halt * halt_row)).astype(bf16)
            r.slot_cot[expert, slots(block), :] = rows_grad

    side_blocks = length // 2
    side_rows = side_blocks * CAP

    def prepare(turn, carried):
        rows_back((ctx + turn) % length)
        return carried

    def rows_of_half(half):
        return pl.ds(pl.multiple_of(half * side_rows, side_rows), side_rows)

    def hidden_back(half):
        rows = rows_of_half(half)

        def part(turn, carried):
            expert, index = turn // 2, turn % 2
            columns = pl.ds(pl.multiple_of(index * 1024, 1024), 1024)
            back = product(r.slot_cot[expert, rows, :], r.outer[expert, columns, :], ((1,), (1,)))
            slope = r.slope[expert, rows, columns].astype(f32)
            r.slope[expert, rows, columns] = (back * slope).astype(bf16)
            return carried

        lax.fori_loop(0, 2 * EXP_DEV, part, 0)

    def entering_back(half):
        rows = rows_of_half(half)

        def one(expert, carried):
            sent = product(r.slope[expert, rows, :], r.inner[expert], ((1,), (1,)))
            r.slot_back[expert] = sent.astype(bf16)
            return carried

        lax.fori_loop(0, EXP_DEV, one, 0)

        def gather_up(index, carried):
            block = half * side_blocks + index
            total = 0.0
            for expert in range(EXP_DEV):
                chosen = picks(r, block, expert).astype(bf16)
                total = total + product(chosen, r.slot_back[expert, slots(index), :], ((0,), (0,)))
            r.entering[block] = total.astype(bf16)
            return carried

        lax.fori_loop(0, side_blocks, gather_up, 0)

    def outer_grad(turn, carried):
        expert, part = turn // 4, turn % 4
        columns = pl.ds(pl.multiple_of(part * 512, 512), 512)
        value = product(r.active[expert, :, columns], r.slot_cot[expert], ((0,), (0,)))
        r.outer[expert, columns, :] = value.astype(bf16)
        return carried

    def inner_grad(turn, carried):
        expert, part = turn // 4, turn % 4
        columns = pl.ds(pl.multiple_of(part * 512, 512), 512)
        value = product(r.slot_rows[expert], r.slope[expert, :, columns], ((0,), (0,)))
        r.inner[expert, :, columns] = value.astype(bf16)
        return carried

    near, far = ctx // side_blocks, 1 - ctx // side_blocks
    experts = ExpertReduce(
        r.inner, r.outer, r.half_in, r.half_out, r.side_in, r.side_out, r.last_in, r.last_out,
        r.expert_send, r.expert_recv,
    )
    lax.fori_loop(0, length, prepare, 0)
    hidden_back(far)
    entering_back(far)
    for index in range(2):
        backs.start_far(index)
    hidden_back(near)
    lax.fori_loop(0, 4 * EXP_DEV, outer_grad, 0)
    experts.start(1)
    entering_back(near)
    backs.start_near()
    mixed.start_far(1)
    experts.add_halves(1)
    give_back(length, r, backs.next[0])
    mixed.start_near()
    give_back(length, r, ctx)
    backs.pass_on(0)
    lax.fori_loop(0, 4 * EXP_DEV, inner_grad, 0)
    experts.start(0)
    backs.pass_on(1)
    mixed.pass_on(0)
    experts.add_halves(0)
    experts.add_sides(1)

    backs.wait()
    mid = r.middle[...]
    selector = r.small[24:32, :]
    double = jnp.concatenate([selector, selector], 0).astype(bf16)
    back = product(r.pick_grads[...], double, ((0,), (0,))) + backs.total()
    centred = mid - jnp.mean(mid, -1, keepdims=True)
    inverse = lax.rsqrt(jnp.mean(centred * centred, -1, keepdims=True) + EPS)
    plain = centred * inverse
    r.gsmall[34:35, :] = jnp.sum(back * plain, 0, keepdims=True)
    r.gsmall[35:36, :] = jnp.sum(back, 0, keepdims=True)
    scaled = back * r.small[34:35, :]
    level = jnp.mean(scaled, -1, keepdims=True)
    tilt = jnp.mean(scaled * plain, -1, keepdims=True)
    cot = r.cotangent[...]
    flow = r.columns[:, 0:1] * cot + r.columns[:, 1:2] * halt_row
    flow = flow + inverse * (scaled - level - plain * tilt)
    r.grad_states[...] = flow + r.columns[:, 2:3] * cot
    attn_grad = flow.astype(bf16)

    def project_piece(chip, core):
        column = pl.multiple_of((chip * 2 + core) * 512, 512)
        return r.active.at[1, pl.ds(0, 384), pl.ds(column, 512)]

    for part in range(4):
        value = product(r.mixture[:, part * 384 : part * 384 + 384], attn_grad, ((0,), (0,)))
        r.active[1, 0:384, part * 512 : part * 512 + 512] = value.astype(bf16)

    def reducer(index, piece, rows, halves, arrived):
        return PlaneReduce(piece, rows, halves, arrived, r.dense_send.at[index], r.dense_recv.at[index])

    project_reduce = reducer(0, project_piece, 192, r.project_half, r.project_in)
    project_reduce.start()

    chosen = [jnp.zeros((tokens, 128), f32) for unused in range(MOA_TOP)]
    for part in range(6):
        value = product(attn_grad, r.project[part * 256 : part * 256 + 256, :], ((1,), (1,)))
        for pair in range(2):
            block = value[:, pair * 128 : pair * 128 + 128]
            for j in range(MOA_TOP):
                wanted = id_lanes[j] - side == 2 * (2 * part + pair)
                chosen[j] = chosen[j] + jnp.where(wanted, block, 0.0)
    gate_lanes = [r.columns[:, 8 + j : 9 + j] for j in range(MOA_TOP)]
    gate_grads = []
    for j in range(MOA_TOP):
        rows = slice(j * tokens, (j + 1) * tokens)
        head = r.heads[rows, :]
        folded = jnp.where(low_half, 0.0, chosen[j] + pltpu.roll(chosen[j], HS, 1))
        gate_grads.append(jnp.sum(folded * head, -1, keepdims=True))
        grads = (gate_lanes[j] * folded).astype(bf16)
        r.heads_grad[rows, :] = grads
        delta = jnp.sum(grads.astype(f32) * head, -1, keepdims=True)
        pair = jnp.transpose(jnp.where(lane == 0, head[:, 0:1], delta))
        r.stats[:, rows] = pair[0:8]
    common = sum(g * v for g, v in zip(gate_lanes, gate_grads))
    logit = jnp.zeros((tokens, 128), f32)
    for j in range(MOA_TOP):
        logit = jnp.where(lane == id_lanes[j], gate_lanes[j] * (gate_grads[j] - common), logit)
    coarse = logit.astype(bf16)
    fine = (logit - coarse.astype(f32)).astype(bf16)
    sums = product(coarse, r.acted[...], ((0,), (0,))) + product(fine, r.acted[...], ((0,), (0,)))
    r.gsmall[0:24, :] = sums[0:24]
    chooser = r.small[...].astype(bf16)
    r.cotangent[...] = product(coarse, chooser) + product(fine, chooser)
    project_reduce.add_halves()
    mixed.pass_on(1)
    experts.add_sides(0)

    r.kv_grad[...] = jnp.zeros_like(r.kv_grad)
    chunk = 256

    half_keys = length * tokens // 2

    def attend_back(turn, carried):
        rows = pl.ds(pl.multiple_of((turn // 2) * chunk, chunk), chunk)
        keys = pl.ds(pl.multiple_of((turn % 2) * half_keys, half_keys), half_keys)
        query, grads, keyval = r.queries[rows, :], r.heads_grad[rows, :], r.keyval[keys, :]
        scores = product(keyval, query, ((1,), (1,)))
        weights = jnp.exp(scores - r.stats[0:1, rows])
        upward = product(keyval, grads, ((1,), (1,)))
        score_grad = (weights * (upward - r.stats[1:2, rows])).astype(bf16)
        r.kv_grad[keys, :] += product(score_grad, query) + product(weights.astype(bf16), grads)
        down = product(score_grad, keyval, ((0,), (0,))) * HS ** (-0.5)

        @pl.when(turn % 2 == 0)
        def _():
            r.heads[rows, :] = down

        @pl.when(turn % 2 == 1)
        def _():
            r.heads[rows, :] += down

        return carried

    lax.fori_loop(0, 2 * MOA_TOP * tokens // chunk, attend_back, 0)

    def send_keyval(turn, carried):
        block = (ctx + turn) % length
        rows = pl.ds(pl.multiple_of(block * tokens, tokens), tokens)

        @pl.when(turn > 0)
        def _():
            r.heads_grad[rows, :] = r.kv_grad[rows, :].astype(bf16)
            to_owner(length, r, r.heads_grad.at[rows, :], r.kv_in, 6, block).start()

        return carried

    lax.fori_loop(0, length, send_keyval, 0)
    spread = []
    for j in range(MOA_TOP):
        piece = r.heads[j * tokens : (j + 1) * tokens, :]
        spread.append(jnp.where(low_half, piece, pltpu.roll(piece, HS, 1)))
    for pair in range(MOA_EXPERTS // 2):
        block = jnp.zeros((tokens, 128), f32)
        for j in range(MOA_TOP):
            block = jnp.where(id_lanes[j] - side == 2 * pair, spread[j], block)
        r.mixture[:, pair * 128 : pair * 128 + 128] = block.astype(bf16)
    for part in range(4):
        columns = slice(part * 384, part * 384 + 384)
        value = product(r.acted[...], r.mixture[:, columns], ((0,), (0,)))
        r.active[0, 0:512, columns] = value.astype(bf16)

    def wide_piece(first, width):
        def piece(chip, core):
            start = pl.multiple_of((chip * 2 + core) * 128, 128)
            return r.active.at[0, pl.ds(start, 128), pl.ds(first, width)]

        return piece

    query_reduce = reducer(1, wide_piece(0, 1536), 64, r.query_half, r.query_in)
    query_reduce.start()
    r.cotangent[...] += product(r.mixture[...], r.query[...], ((1,), (1,)))
    project_line = LineSum(length, r.project_value, r.project_parts, r.project_sum, sems(7), sems(8))
    project_line.start(project_reduce.total())
    query_reduce.add_halves()

    own_rows = pl.ds(pl.multiple_of(ctx * tokens, tokens), tokens)
    from_all(r.kv_in, 6)
    keyval_grad = r.kv_grad[own_rows, :]
    for step in range(length - 1):
        keyval_grad = keyval_grad + r.kv_in[step].astype(f32)
    keyval_grad = keyval_grad.astype(bf16)
    back = r.cotangent[...] + product(keyval_grad, r.packs[:, 0:64, :].reshape(D, 128), ((1,), (1,)))
    values = r.states[...].astype(f32)
    centred = values - jnp.mean(values, -1, keepdims=True)
    inverse = lax.rsqrt(jnp.mean(centred * centred, -1, keepdims=True) + EPS)
    plain = centred * inverse
    r.gsmall[32:33, :] = jnp.sum(back * plain, 0, keepdims=True)
    r.gsmall[33:34, :] = jnp.sum(back, 0, keepdims=True)
    r.active[0, 0:512, 1536:1664] = product(r.acted[...], keyval_grad, ((0,), (0,))).astype(bf16)
    r.active[0, 0:512, 1664:1792] = jnp.transpose(r.gsmall[...]).astype(bf16)
    small_reduce = reducer(2, wide_piece(1536, 256), 64, r.small_half, r.small_in)
    small_reduce.start()
    scaled = back * r.small[32:33, :]
    level = jnp.mean(scaled, -1, keepdims=True)
    tilt = jnp.mean(scaled * plain, -1, keepdims=True)
    r.grad_states[...] = (
        r.grad_states[...] + inverse * (scaled - level - plain * tilt)
    )
    small_reduce.add_halves()
    project_line.share_out()
    query_line = LineSum(length, r.query_value, r.query_parts, r.query_sum, sems(9), sems(10))
    query_line.start(query_reduce.total())
    small_line = LineSum(length, r.small_value, r.small_parts, r.small_sum, sems(11), sems(12))
    small_line.start(small_reduce.total())

    experts.total(1, r.grad_outer)
    experts.total(0, r.grad_inner)
    mixed.wait()
    final = r.middle[...] + mixed.total()
    r.new_states[...] = (
        r.columns[:, 2:3] * r.states[...].astype(f32) + r.columns[:, 0:1] * final
    ).astype(bf16)
    query_line.share_out()
    small_line.share_out()
    r.grad_project[...] = project_line.finish()
    r.grad_query[...] = query_line.finish()
    r.grad_small[...] = small_line.finish()

    mixed.drain()
    backs.drain()
    sent_all(
        lambda b: r.heads_grad.at[pl.ds(pl.multiple_of(b * tokens, tokens), tokens), :], r.kv_in, 6
    )
    for item in (project_reduce, query_reduce, small_reduce, experts):
        item.drain()
    for item in (project_line, query_line, small_line):
        item.drain()


def whole_kernel(length, names, *refs):
    r = SimpleNamespace(**dict(zip(names, refs)))
    forward_part(length, r)
    backward_part(length, r)


def write_kernel(
    new_states, rows_out, grad_states, grad_query, grad_project, grad_small, grad_inner, grad_outer, *outs
):
    f32 = jnp.float32
    outs[0][0] = new_states[...]
    outs[1][...] = rows_out[0:1, :]
    outs[2][0] = grad_states[...]
    outs[3][...] = rows_out[1:2, :]
    outs[4][...] = grad_query[...].astype(f32)
    outs[5][...] = grad_small[:, 0:128].astype(f32)
    outs[6][...] = grad_project[...].astype(f32)
    turned = jnp.transpose(grad_small[:, 128:256].astype(f32))
    outs[7][...] = turned[0:24]
    outs[8][...] = turned[24:32]
    for index in range(5):
        outs[9 + index][...] = turned[32 + index : 33 + index]
    outs[14][...] = grad_inner[...].astype(f32)
    outs[15][...] = grad_outer[...].astype(f32)


def write_out(tokens, *results):
    f32, bf16 = jnp.float32, jnp.bfloat16
    shape = jax.ShapeDtypeStruct
    outs = (
        shape((1, tokens, D), bf16),
        shape((1, tokens), f32),
        shape((1, tokens, D), f32),
        shape((1, tokens), f32),
        shape((64, MOA_EXPERTS * HS), f32),
        shape((64, 128), f32),
        shape((192, D), f32),
        shape((MOA_EXPERTS, 64), f32),
        shape((8, 64), f32),
        *[shape((1, 64), f32)] * 5,
        shape((EXP_DEV, 64, FF), f32),
        shape((EXP_DEV, 256, D), f32),
    )
    in_vmem = pl.BlockSpec(memory_space=pltpu.VMEM)
    final = pl.pallas_call(
        write_kernel,
        out_shape=outs,
        in_specs=[in_vmem] * len(results),
        out_specs=[in_vmem] * len(outs),
        compiler_params=pltpu.CompilerParams(vmem_limit_bytes=LIMIT_MIB * 2**20),
        name="write_out",
    )(*results)
    vectors = [item.reshape(64) for item in final[9:14]]
    return (*final[0:7], final[7].T, final[8].T, *vectors, *final[14:16])


def fast_body(
    states,
    remaining,
    moa_ids,
    ffn_ids,
    out_cotangent,
    left_cotangent,
    query_weight,
    keyval_weight,
    project_weight,
    chooser,
    selector,
    gain_one,
    bias_one,
    gain_two,
    bias_two,
    halt_weight,
    expert_in,
    expert_out,
):
    f32, bf16 = jnp.float32, jnp.bfloat16
    length = lax.axis_size("ctx")
    tokens = states.shape[1]
    rows = length * CAP
    wide = MOA_EXPERTS * HS
    nothing = jnp.zeros_like(gain_one)
    vectors = jnp.stack(
        [gain_one, bias_one, gain_two, bias_two, halt_weight, nothing, nothing, nothing], 0
    )
    inputs = dict(
        states=states[0],
        cotangent_part=out_cotangent[0],
        head_ids=moa_ids[0].T,
        route_ids=ffn_ids[0].T,
        remaining=remaining,
        left_cot=left_cotangent,
        keyval_part=keyval_weight,
        chooser_part=chooser.T,
        selector_part=selector.T,
        vectors=vectors,
        query_part=query_weight,
        project_part=project_weight,
        inner_part=expert_in,
        outer_part=expert_out,
    )
    in_place = ("cotangent_part", "query_part", "project_part", "inner_part", "outer_part")
    shape = jax.ShapeDtypeStruct
    outputs = dict(
        new_states=shape((tokens, D), bf16),
        rows_out=shape((8, tokens), f32),
        grad_states=shape((tokens, D), f32),
        grad_query=shape((64, wide), bf16),
        grad_project=shape((192, D), bf16),
        grad_small=shape((64, 256), bf16),
        grad_inner=shape((EXP_DEV, 64, FF), bf16),
        grad_outer=shape((EXP_DEV, 256, D), bf16),
    )
    vmem, dma = pltpu.VMEM, pltpu.SemaphoreType.DMA
    scratch = dict(
        slot_rows=vmem((EXP_DEV, rows, D), bf16),
        active=vmem((EXP_DEV, rows, FF), bf16),
        slope=vmem((EXP_DEV, rows, FF), bf16),
        result=vmem((EXP_DEV, rows, D), bf16),
        slot_cot=vmem((EXP_DEV, rows, D), bf16),
        inner=vmem((EXP_DEV, D, FF), bf16),
        outer=vmem((EXP_DEV, FF, D), bf16),
        query=vmem((D, wide), bf16),
        project=vmem((wide, D), bf16),
        packs=vmem((8, 112, 128), bf16),
        id_columns=vmem((tokens, 128), jnp.int32),
        cotangent=vmem((tokens, D), f32),
        acted=vmem((tokens, D), bf16),
        mixture=vmem((tokens, wide), bf16),
        queries=vmem((MOA_TOP * tokens, 128), bf16),
        heads=vmem((MOA_TOP * tokens, 128), f32),
        keyval=vmem((length * tokens, 128), bf16),
        middle=vmem((tokens, D), f32),
        entering=vmem((length, tokens, D), bf16),
        cots=vmem((length, tokens, D), bf16),
        routes=vmem((length, 24, tokens), f32),
        scores=vmem((length, length, 8, tokens), f32),
        small=vmem((128, D), f32),
        factors=vmem((length, 8, tokens), f32),
        columns=vmem((tokens, 128), f32),
        pick_grads=vmem((16, tokens), bf16),
        gsmall=vmem((128, D), f32),
        slot_back=vmem((EXP_DEV, rows // 2, D), bf16),
        back_in=vmem((4, tokens, D), bf16),
        mix_in=vmem((4, tokens, D), bf16),
        half_in=vmem((2, EXP_DEV, 128, FF), bf16),
        half_out=vmem((2, EXP_DEV, 512, D), bf16),
        side_in=vmem((EXP_DEV, 2, 64, FF), bf16),
        side_out=vmem((EXP_DEV, 2, 256, D), bf16),
        last_in=vmem((EXP_DEV, 64, FF), bf16),
        last_out=vmem((EXP_DEV, 256, D), bf16),
        heads_grad=vmem((MOA_TOP * tokens, 128), bf16),
        stats=vmem((8, MOA_TOP * tokens), f32),
        kv_grad=vmem((length * tokens, 128), f32),
        kv_in=vmem((length - 1, tokens, 128), bf16),
        project_half=vmem((2, 384, D), bf16),
        project_in=vmem((3, 192, D), bf16),
        query_half=vmem((2, 128, wide), bf16),
        query_in=vmem((3, 64, wide), bf16),
        small_half=vmem((2, 128, 256), bf16),
        small_in=vmem((3, 64, 256), bf16),
        project_value=vmem((192, D), bf16),
        project_parts=vmem((length - 1, 192 // length, D), bf16),
        project_sum=vmem((192, D), bf16),
        query_value=vmem((64, wide), bf16),
        query_parts=vmem((length - 1, 64 // length, wide), bf16),
        query_sum=vmem((64, wide), bf16),
        small_value=vmem((64, 256), bf16),
        small_parts=vmem((length - 1, 64 // length, 256), bf16),
        small_sum=vmem((64, 256), bf16),
        pack_send=dma((7,)),
        pack_recv=dma((7,)),
        plane_send=dma((5, 9)),
        plane_recv=dma((5, 9)),
        plane_local=dma((6,)),
        line_send=dma((2, 2, length)),
        line_recv=dma((2, 2, length)),
        direct_sems=dma((13, length)),
        direct_recvs=dma((13, length)),
        return_send=dma((2, 5)),
        return_recv=dma((2, 5)),
        expert_send=dma((4, 5)),
        expert_recv=dma((4, 5)),
        dense_send=dma((3, 5)),
        dense_recv=dma((3, 5)),
    )
    in_vmem = pl.BlockSpec(memory_space=pltpu.VMEM)
    anywhere = pl.BlockSpec(memory_space=pl.ANY)
    names = (*inputs, *outputs, *scratch)
    results = pl.pallas_call(
        partial(whole_kernel, length, names),
        out_shape=tuple(outputs.values()),
        in_specs=[anywhere if name in in_place else in_vmem for name in inputs],
        out_specs=[in_vmem] * len(outputs),
        scratch_shapes=list(scratch.values()),
        compiler_params=pltpu.CompilerParams(
            collective_id=0, has_side_effects=True, vmem_limit_bytes=LIMIT_MIB * 2**20
        ),
        name="layer_step",
    )(*inputs.values())
    return write_out(tokens, *results)


def solution(mesh):
    in_specs = (
        P(("seq", "wsh"), "ctx", None),
        P(("seq", "wsh"), "ctx"),
        P(("seq", "wsh"), "ctx", None),
        P(("seq", "wsh"), "ctx", None),
        P(("seq", "wsh"), "ctx", None),
        P(("seq", "wsh"), "ctx"),
        P(("seq", "wsh"), None),
        P(("seq", "wsh"), None),
        P(("seq", "wsh"), None),
        P(("seq", "wsh"), None),
        P(("seq", "wsh"), None),
        P(("seq", "wsh")),
        P(("seq", "wsh")),
        P(("seq", "wsh")),
        P(("seq", "wsh")),
        P(("seq", "wsh")),
        P("ctx", ("seq", "wsh"), None),
        P("ctx", ("seq", "wsh"), None),
    )
    out_specs = (
        P(("seq", "wsh"), "ctx", None),
        P(("seq", "wsh"), "ctx"),
        P(("seq", "wsh"), "ctx", None),
        P(("seq", "wsh"), "ctx"),
        P(("seq", "wsh"), None),
        P(("seq", "wsh"), None),
        P(("seq", "wsh"), None),
        P(("seq", "wsh"), None),
        P(("seq", "wsh"), None),
        P(("seq", "wsh")),
        P(("seq", "wsh")),
        P(("seq", "wsh")),
        P(("seq", "wsh")),
        P(("seq", "wsh")),
        P("ctx", ("seq", "wsh"), None),
        P("ctx", ("seq", "wsh"), None),
    )
    body = fast_body if mesh.shape["ctx"] == 4 else general_body
    return jax.shard_map(body, mesh=mesh, in_specs=in_specs, out_specs=out_specs, check_vma=False)
```

```python
from functools import partial
from types import SimpleNamespace

import jax
import jax.numpy as jnp
from jax import lax
from jax.experimental import pallas as pl
from jax.experimental.pallas import tpu as pltpu
from jax.sharding import PartitionSpec as P

D = 512
HS = 64
MOA_EXPERTS = 24
MOA_TOP = 4
EXP_DEV = 2
FFN_TOP = 2
FF = 2048


EPS = 1e-05
HIGH = lax.Precision.HIGHEST


def shifted(x, axis, by):
    length = lax.axis_size(axis)
    return lax.ppermute(x, axis, [(i, (i + by) % length) for i in range(length)])


def layer_norm(values, gain, bias):
    centred = values - jnp.mean(values, -1, keepdims=True)
    inverse = lax.rsqrt(jnp.mean(centred * centred, -1, keepdims=True) + EPS)
    normal = centred * inverse
    return (normal * gain + bias, normal, inverse)


def norm_back(incoming, normal, inverse, gain):
    scaled = incoming * gain
    inner_term = (
        scaled
        - jnp.mean(scaled, -1, keepdims=True)
        - normal * jnp.mean(scaled * normal, -1, keepdims=True)
    )
    return (inverse * inner_term, jnp.sum(incoming * normal, 0), jnp.sum(incoming, 0))


def one_hot(index, count):
    return (index[..., None] == jnp.arange(count, dtype=jnp.int32)).astype(jnp.float32)


def choose_back(gates, upstream):
    return gates * (upstream - jnp.sum(gates * upstream, -1, keepdims=True))


def block_rows(row_count):
    if row_count > 512 and row_count % 512 == 0:
        return 512
    return row_count


def expert_slots(route_ids, experts):
    flat_ids = route_ids.reshape(-1)
    table = (flat_ids[:, None] == jnp.arange(experts, dtype=jnp.int32)[None, :]).astype(jnp.float32)
    place = jnp.arange(flat_ids.shape[0], dtype=jnp.int32)
    before = (place[None, :] < place[:, None]).astype(jnp.bfloat16)
    earlier = jnp.dot(before, table.astype(jnp.bfloat16), preferred_element_type=jnp.float32)
    return jnp.sum(earlier * table, 1).astype(jnp.int32).reshape(route_ids.shape)


def general_body(
    states,
    remaining,
    moa_ids,
    ffn_ids,
    out_cotangent,
    left_cotangent,
    query_weight,
    keyval_weight,
    project_weight,
    chooser,
    selector,
    gain_one,
    bias_one,
    gain_two,
    bias_two,
    halt_weight,
    expert_in,
    expert_out,
):
    tokens = states.shape[1]
    devices = lax.axis_size("ctx")
    experts = EXP_DEV * devices
    capacity = max(2, (4 * tokens + experts - 1) // experts)
    rows_total = tokens * MOA_TOP
    scaling = HS ** (-0.5)
    f32 = jnp.float32
    bf16 = jnp.bfloat16
    (
        query_full,
        keyval_full,
        project_full,
        chooser_full,
        selector_full,
        gainone_full,
        biasone_full,
        gaintwo_full,
        biastwo_full,
        halt_full,
    ) = (
        lax.all_gather(query_weight, ("seq", "wsh"), axis=0, tiled=True),
        lax.all_gather(keyval_weight, ("seq", "wsh"), axis=0, tiled=True),
        lax.all_gather(project_weight, ("seq", "wsh"), axis=0, tiled=True),
        lax.all_gather(chooser, ("seq", "wsh"), axis=0, tiled=True),
        lax.all_gather(selector, ("seq", "wsh"), axis=0, tiled=True),
        lax.all_gather(gain_one, ("seq", "wsh"), axis=0, tiled=True),
        lax.all_gather(bias_one, ("seq", "wsh"), axis=0, tiled=True),
        lax.all_gather(gain_two, ("seq", "wsh"), axis=0, tiled=True),
        lax.all_gather(bias_two, ("seq", "wsh"), axis=0, tiled=True),
        lax.all_gather(halt_weight, ("seq", "wsh"), axis=0, tiled=True),
    )
    inner_full, outer_full = (
        lax.all_gather(expert_in, ("seq", "wsh"), axis=1, tiled=True),
        lax.all_gather(expert_out, ("seq", "wsh"), axis=1, tiled=True),
    )
    gain_first = gainone_full.astype(f32)
    gain_second = gaintwo_full.astype(f32)
    halt_vector = halt_full.astype(f32)
    resident = states[0].astype(f32)
    normed_one, normal_one, inverse_one = layer_norm(resident, gain_first, biasone_full.astype(f32))
    acted = normed_one.astype(bf16)
    query_all = (
        jnp.dot(acted, query_full, preferred_element_type=f32)
        .astype(bf16)
        .reshape(tokens, MOA_EXPERTS, HS)
    )
    head_ids = moa_ids[0]
    query_sel = jnp.take_along_axis(query_all, head_ids[:, :, None], axis=1).reshape(rows_total, HS)
    keyval = jnp.dot(acted, keyval_full, preferred_element_type=f32).astype(bf16)
    chosen = one_hot(head_ids, MOA_EXPERTS)
    head_logits = jnp.sum(
        chosen * jnp.dot(acted, chooser_full, preferred_element_type=f32)[:, None, :], -1
    )
    head_gates = jax.nn.softmax(head_logits, -1)
    start_state = (
        jnp.full((rows_total,), -1e30, f32),
        jnp.zeros((rows_total,), f32),
        jnp.zeros((rows_total, HS), f32),
    )
    running = start_state
    shard_rows = lax.all_gather(keyval, "ctx", axis=0, tiled=True)
    block_size = block_rows(shard_rows.shape[0])
    grouped = shard_rows.reshape(shard_rows.shape[0] // block_size, block_size, 2 * HS)

    def absorb(carried, key_block):
        row_peak, row_total, gathered = carried
        scores = jnp.dot(query_sel, key_block[:, :HS].T, preferred_element_type=f32) * scaling
        new_peak = jnp.maximum(row_peak, jnp.max(scores, -1))
        fading = jnp.exp(row_peak - new_peak)
        weights = jnp.exp(scores - new_peak[:, None])
        row_total = row_total * fading + jnp.sum(weights, -1)
        gathered = gathered * fading[:, None] + jnp.dot(
            weights.astype(bf16), key_block[:, HS:], preferred_element_type=f32
        )
        return ((new_peak, row_total, gathered), None)

    running, unused = lax.scan(absorb, running, grouped)
    row_peak, row_total, gathered = running
    heads_out = gathered / row_total[:, None]
    log_total = row_peak + jnp.log(row_total)
    heads_view = heads_out.reshape(tokens, MOA_TOP, HS)
    mixed_sel = (head_gates[:, :, None] * heads_view).astype(bf16)
    chosen_low = chosen.astype(bf16)
    mixture = jnp.sum(chosen_low[:, :, :, None] * mixed_sel[:, :, None, :], 1).reshape(
        tokens, MOA_EXPERTS * HS
    )
    middle = resident + jnp.dot(mixture, project_full, preferred_element_type=f32)
    normed_two, normal_two, inverse_two = layer_norm(middle, gain_second, biastwo_full.astype(f32))
    entering = normed_two.astype(bf16)
    route_ids = ffn_ids[0]
    picked = one_hot(route_ids, experts)
    expert_logits = jnp.sum(
        picked * jnp.dot(entering, selector_full, preferred_element_type=f32)[:, None, :], -1
    )
    expert_gates = jax.nn.softmax(expert_logits, -1)
    slots = expert_slots(route_ids, experts)
    target = (route_ids * capacity + slots).reshape(-1)
    copies = jnp.broadcast_to(entering[:, None, :], (tokens, FFN_TOP, D)).reshape(-1, D)
    outgoing = (
        jnp.zeros((experts * capacity, D), bf16)
        .at[target]
        .set(copies)
        .reshape(devices, EXP_DEV, capacity, D)
    )
    arrived_rows = lax.all_to_all(outgoing, "ctx", split_axis=0, concat_axis=0, tiled=True)
    before = jnp.einsum("nekd,edf->nekf", arrived_rows, inner_full, preferred_element_type=f32)
    activated = jax.nn.gelu(before, approximate=False).astype(bf16)
    result_rows = jnp.einsum(
        "nekf,efd->nekd", activated, outer_full, preferred_element_type=f32
    ).astype(bf16)
    returned = lax.all_to_all(result_rows, "ctx", split_axis=0, concat_axis=0, tiled=True).reshape(
        experts * capacity, D
    )
    expert_rows = returned[target].reshape(tokens, FFN_TOP, D).astype(f32)
    final = middle + jnp.sum(expert_gates[:, :, None] * expert_rows, 1)
    halting = jax.nn.sigmoid(jnp.dot(final, halt_vector, precision=HIGH))
    left_mass = remaining[0]
    stopped = left_mass * halting
    new_states = (stopped[:, None] * resident + (1.0 - stopped)[:, None] * final).astype(bf16)
    remaining_next = left_mass * (1.0 - halting)
    out_grad = out_cotangent[0]
    left_grad = left_cotangent[0]
    stop_grad = jnp.sum(out_grad * (resident - final), -1)
    grad_remaining = stop_grad * halting + left_grad * (1.0 - halting)
    halt_logit_grad = (stop_grad - left_grad) * left_mass * halting * (1.0 - halting)
    grad_halt = jnp.sum(halt_logit_grad[:, None] * final, 0)
    grad_final = (1.0 - stopped)[:, None] * out_grad + halt_logit_grad[:, None] * halt_vector
    gate_grad = jnp.sum(grad_final[:, None, :] * expert_rows, -1)
    selector_logit_grad = jnp.sum(choose_back(expert_gates, gate_grad)[:, :, None] * picked, 1)
    entering_wide = entering.astype(f32)
    grad_selector = jnp.dot(entering_wide.T, selector_logit_grad, precision=HIGH)
    rows_grad = (expert_gates[:, :, None] * grad_final[:, None, :]).astype(bf16).reshape(-1, D)
    grad_outgoing = (
        jnp.zeros((experts * capacity, D), bf16)
        .at[target]
        .set(rows_grad)
        .reshape(devices, EXP_DEV, capacity, D)
    )
    grad_arrived = lax.all_to_all(grad_outgoing, "ctx", split_axis=0, concat_axis=0, tiled=True)
    grad_activated = jnp.einsum(
        "nekd,efd->nekf", grad_arrived, outer_full, preferred_element_type=f32
    )
    activated_again, gelu_back = jax.vjp(partial(jax.nn.gelu, approximate=False), before)
    before_grad = gelu_back(grad_activated)[0].astype(bf16)
    outer_grad = jnp.einsum(
        "nekf,nekd->efd", activated_again.astype(bf16), grad_arrived, preferred_element_type=f32
    )
    inner_grad = jnp.einsum("nekd,nekf->edf", arrived_rows, before_grad, preferred_element_type=f32)
    grad_sent = jnp.einsum(
        "nekf,edf->nekd", before_grad, inner_full, preferred_element_type=f32
    ).astype(bf16)
    grad_back = lax.all_to_all(grad_sent, "ctx", split_axis=0, concat_axis=0, tiled=True).reshape(
        experts * capacity, D
    )
    entering_grad = jnp.sum(grad_back[target].reshape(tokens, FFN_TOP, D).astype(f32), 1)
    entering_grad = entering_grad + jnp.dot(
        selector_logit_grad, selector_full.astype(f32).T, precision=HIGH
    )
    middle_extra, grad_gain_two, grad_bias_two = norm_back(
        entering_grad, normal_two, inverse_two, gain_second
    )
    middle_grad = grad_final + middle_extra
    attn_grad = middle_grad.astype(bf16)
    grad_project = jnp.dot(mixture.T, attn_grad, preferred_element_type=f32)
    mix_grad = jnp.dot(attn_grad, project_full.T, preferred_element_type=f32).reshape(
        tokens, MOA_EXPERTS, HS
    )
    mix_sel_grad = jnp.take_along_axis(mix_grad, head_ids[:, :, None], axis=1)
    head_gate_grad = jnp.sum(mix_sel_grad * heads_view, -1)
    chooser_logit_grad = jnp.sum(choose_back(head_gates, head_gate_grad)[:, :, None] * chosen, 1)
    acted_wide = acted.astype(f32)
    grad_chooser = jnp.dot(acted_wide.T, chooser_logit_grad, precision=HIGH)
    acted_grad = jnp.dot(chooser_logit_grad, chooser_full.astype(f32).T, precision=HIGH)
    heads_grad = (head_gates[:, :, None] * mix_sel_grad).astype(bf16).reshape(rows_total, HS)
    row_delta = jnp.sum(heads_grad.astype(f32) * heads_out, -1)

    def cycle_turn(turn_index, carried):
        visiting, grads_visiting, query_grad = carried
        block_size = block_rows(tokens)

        def per_block(query_acc, key_block):
            scores = jnp.dot(query_sel, key_block[:, :HS].T, preferred_element_type=f32) * scaling
            probability = jnp.exp(scores - log_total[:, None])
            prob_grad = jnp.dot(heads_grad, key_block[:, HS:].T, preferred_element_type=f32)
            score_grad = (probability * (prob_grad - row_delta[:, None])).astype(bf16)
            query_acc = (
                query_acc
                + jnp.dot(score_grad, key_block[:, :HS], preferred_element_type=f32) * scaling
            )
            keys_grad = jnp.dot(score_grad.T, query_sel, preferred_element_type=f32) * scaling
            values_grad = jnp.dot(
                probability.astype(bf16).T, heads_grad, preferred_element_type=f32
            )
            return (query_acc, jnp.concatenate([keys_grad, values_grad], -1))

        query_grad, block_grads = lax.scan(
            per_block, query_grad, visiting.reshape(tokens // block_size, block_size, 2 * HS)
        )
        grads_visiting = grads_visiting + block_grads.reshape(tokens, 2 * HS)
        visiting = shifted(visiting, "ctx", 1)
        grads_visiting = shifted(grads_visiting.astype(jnp.bfloat16), "ctx", 1).astype(
            grads_visiting.dtype
        )
        return (visiting, grads_visiting, query_grad)

    cycle_state = (keyval, jnp.zeros((tokens, 2 * HS), f32), jnp.zeros((rows_total, HS), f32))
    unused_keys, keyval_grad, query_grad = lax.fori_loop(0, devices, cycle_turn, cycle_state)
    query_sel_grad = query_grad.astype(bf16).reshape(tokens, MOA_TOP, HS)
    query_all_grad = jnp.sum(chosen_low[:, :, :, None] * query_sel_grad[:, :, None, :], 1).reshape(
        tokens, MOA_EXPERTS * HS
    )
    keyval_low = keyval_grad.astype(bf16)
    grad_query = jnp.dot(acted.T, query_all_grad, preferred_element_type=f32)
    grad_keyval = jnp.dot(acted.T, keyval_low, preferred_element_type=f32)
    acted_grad = acted_grad + jnp.dot(query_all_grad, query_full.T, preferred_element_type=f32)
    acted_grad = acted_grad + jnp.dot(keyval_low, keyval_full.T, preferred_element_type=f32)
    resident_grad, grad_gain_one, grad_bias_one = norm_back(
        acted_grad, normal_one, inverse_one, gain_first
    )
    grad_states = middle_grad + resident_grad + stopped[:, None] * out_grad
    dense_grads = (
        grad_query,
        grad_keyval,
        grad_project,
        grad_chooser,
        grad_selector,
        grad_gain_one,
        grad_bias_one,
        grad_gain_two,
        grad_bias_two,
        grad_halt,
    )
    totals = (
        lax.psum(dense_grads[0].astype(jnp.bfloat16), "ctx").astype(jnp.float32),
        lax.psum(dense_grads[1].astype(jnp.bfloat16), "ctx").astype(jnp.float32),
        lax.psum(dense_grads[2].astype(jnp.bfloat16), "ctx").astype(jnp.float32),
        lax.psum(dense_grads[3].astype(jnp.bfloat16), "ctx").astype(jnp.float32),
        lax.psum(dense_grads[4].astype(jnp.bfloat16), "ctx").astype(jnp.float32),
        lax.psum(dense_grads[5].astype(jnp.bfloat16), "ctx").astype(jnp.float32),
        lax.psum(dense_grads[6].astype(jnp.bfloat16), "ctx").astype(jnp.float32),
        lax.psum(dense_grads[7].astype(jnp.bfloat16), "ctx").astype(jnp.float32),
        lax.psum(dense_grads[8].astype(jnp.bfloat16), "ctx").astype(jnp.float32),
        lax.psum(dense_grads[9].astype(jnp.bfloat16), "ctx").astype(jnp.float32),
    )
    shards = (
        lax.psum_scatter(
            totals[0].astype(jnp.bfloat16), ("seq", "wsh"), scatter_dimension=0, tiled=True
        ).astype(jnp.float32),
        lax.psum_scatter(
            totals[1].astype(jnp.bfloat16), ("seq", "wsh"), scatter_dimension=0, tiled=True
        ).astype(jnp.float32),
        lax.psum_scatter(
            totals[2].astype(jnp.bfloat16), ("seq", "wsh"), scatter_dimension=0, tiled=True
        ).astype(jnp.float32),
        lax.psum_scatter(
            totals[3].astype(jnp.bfloat16), ("seq", "wsh"), scatter_dimension=0, tiled=True
        ).astype(jnp.float32),
        lax.psum_scatter(
            totals[4].astype(jnp.bfloat16), ("seq", "wsh"), scatter_dimension=0, tiled=True
        ).astype(jnp.float32),
        lax.psum_scatter(
            totals[5].astype(jnp.bfloat16), ("seq", "wsh"), scatter_dimension=0, tiled=True
        ).astype(jnp.float32),
        lax.psum_scatter(
            totals[6].astype(jnp.bfloat16), ("seq", "wsh"), scatter_dimension=0, tiled=True
        ).astype(jnp.float32),
        lax.psum_scatter(
            totals[7].astype(jnp.bfloat16), ("seq", "wsh"), scatter_dimension=0, tiled=True
        ).astype(jnp.float32),
        lax.psum_scatter(
            totals[8].astype(jnp.bfloat16), ("seq", "wsh"), scatter_dimension=0, tiled=True
        ).astype(jnp.float32),
        lax.psum_scatter(
            totals[9].astype(jnp.bfloat16), ("seq", "wsh"), scatter_dimension=0, tiled=True
        ).astype(jnp.float32),
    )
    inner_shard, outer_shard = (
        lax.psum_scatter(
            inner_grad.astype(jnp.bfloat16), ("seq", "wsh"), scatter_dimension=1, tiled=True
        ).astype(jnp.float32),
        lax.psum_scatter(
            outer_grad.astype(jnp.bfloat16), ("seq", "wsh"), scatter_dimension=1, tiled=True
        ).astype(jnp.float32),
    )
    return (
        new_states[None],
        remaining_next[None],
        grad_states[None],
        grad_remaining[None],
        shards[0],
        shards[1],
        shards[2],
        shards[3],
        shards[4],
        shards[5],
        shards[6],
        shards[7],
        shards[8],
        shards[9],
        inner_shard,
        outer_shard,
    )


MESH = pl.DeviceIdType.MESH
CAP = 192
LIMIT_MIB = 62
KEEP = 0.7071067811865476
SPREAD = 0.3989422804014327
ERF_P = 0.3275911
ERF_A = (0.254829592, -0.284496736, 1.421413741, -1.453152027, 1.061405429)


def remote(source, target, send_sem, recv_sem, device):
    return pltpu.make_async_remote_copy(
        src_ref=source,
        dst_ref=target,
        send_sem=send_sem,
        recv_sem=recv_sem,
        device_id=device,
        device_id_type=MESH,
    )


def places():
    ctx, seq, wsh = (lax.axis_index(name) for name in ("ctx", "seq", "wsh"))
    chip, core = seq // 2, seq % 2
    over = (1 - chip) * 2 + core
    twin = (ctx, chip * 2 + 1 - core, wsh)
    beside = (ctx, over, wsh)
    above = (ctx, seq, 1 - wsh)
    across = (ctx, over, 1 - wsh)
    return (ctx, seq, wsh), twin, beside, above, across


def shard_of(place):
    return place[1] * 2 + place[2]


def moved(place, offset, length):
    return ((place[0] + offset) % length, place[1], place[2])


def plane_peer(place, step):
    shard = (shard_of(place) + step) % 8
    return (place[0], shard // 2, shard % 2)


class PlaneGather:
    def __init__(self, shard, full, halves, send, recv, local):
        self.shard, self.full, self.halves = shard, full, halves
        self.send, self.recv, self.local = send, recv, local
        self.me, self.twin, self.beside, self.above, self.across = places()

    def pair(self, view, slot, device):
        return remote(view, view, self.send.at[slot], self.recv.at[slot], device)

    def own(self, slot, device):
        target = self.full(shard_of(self.me))
        return remote(self.shard, target, self.send.at[slot], self.recv.at[slot], device)

    def keep(self):
        return pltpu.make_async_copy(self.shard, self.full(shard_of(self.me)), self.local)

    def start(self):
        self.own(0, self.twin).start()
        self.own(1, self.beside).start()
        self.own(2, self.above).start()
        if self.halves is None:
            self.own(3, self.across).start()
        self.keep().start()

    def arrive(self, slot, place):
        self.pair(self.full(shard_of(place)), slot, self.twin).wait_recv()

    def relay(self):
        if self.halves is None:
            for slot, place in ((1, self.beside), (2, self.above), (3, self.across)):
                self.arrive(slot, place)
                self.pair(self.full(shard_of(place)), slot + 3, self.twin).start()
            return
        self.arrive(1, self.beside)
        self.pair(self.halves(shard_of(self.beside), 1), 7, self.above).start()
        self.pair(self.full(shard_of(self.beside)), 4, self.twin).start()
        self.arrive(2, self.above)
        self.pair(self.halves(shard_of(self.above), 0), 3, self.beside).start()
        self.pair(self.full(shard_of(self.above)), 5, self.twin).start()

    def relay_rest(self):
        shard = shard_of(self.across)
        for slot, half in ((3, 0), (7, 1)):
            view = self.halves(shard, half)
            self.pair(view, slot, self.twin).wait_recv()
            self.pair(view, 6 if half == 0 else 8, self.twin).start()

    def finish(self):
        self.keep().wait()
        ctx, seq, wsh = self.twin
        over = (1 - seq // 2) * 2 + seq % 2
        self.arrive(0, self.twin)
        self.arrive(4, (ctx, over, wsh))
        self.arrive(5, (ctx, seq, 1 - wsh))
        rest = shard_of((ctx, over, 1 - wsh))
        if self.halves is None:
            self.pair(self.full(rest), 6, self.twin).wait_recv()
        else:
            self.pair(self.halves(rest, 0), 6, self.twin).wait_recv()
            self.pair(self.halves(rest, 1), 8, self.twin).wait_recv()

    def drain(self):
        self.own(0, self.twin).wait_send()
        self.own(1, self.beside).wait_send()
        self.own(2, self.above).wait_send()
        beside, above, across = (shard_of(p) for p in (self.beside, self.above, self.across))
        self.pair(self.full(beside), 4, self.twin).wait_send()
        self.pair(self.full(above), 5, self.twin).wait_send()
        if self.halves is None:
            self.own(3, self.across).wait_send()
            self.pair(self.full(across), 6, self.twin).wait_send()
        else:
            self.pair(self.halves(above, 0), 3, self.beside).wait_send()
            self.pair(self.halves(beside, 1), 7, self.above).wait_send()
            self.pair(self.halves(across, 0), 6, self.twin).wait_send()
            self.pair(self.halves(across, 1), 8, self.twin).wait_send()


class PlaneShare:
    def __init__(self, blocks, send, recv):
        self.blocks, self.send, self.recv = blocks, send, recv
        self.me = places()[0]
        self.shard = shard_of(self.me)

    def copy(self, shard, step, device):
        view = self.blocks.at[shard]
        return remote(view, view, self.send.at[step - 1], self.recv.at[step - 1], device)

    def sends(self):
        return [self.copy(self.shard, step, plane_peer(self.me, step)) for step in range(1, 8)]

    def wait(self):
        for step in range(1, 8):
            source = plane_peer(self.me, 8 - step)
            self.copy(shard_of(source), step, source).wait_recv()


class LineGather:
    def __init__(self, length, blocks, send, recv):
        self.length, self.blocks, self.send, self.recv = length, blocks, send, recv
        self.me = places()[0]

    def hop(self, block, way, step, device):
        view = self.blocks(block)
        return remote(view, view, self.send.at[way, step], self.recv.at[way, step], device)

    def ways(self, step):
        ctx = self.me[0]
        left = (ctx - 1, self.me[1], self.me[2])
        right = (ctx + 1, self.me[1], self.me[2])
        return (
            (0, ctx - step, ctx - step >= 0, right, ctx + 1 < self.length),
            (1, ctx + step, ctx + step < self.length, left, ctx - 1 >= 0),
        )

    def start(self):
        for way, block, unused, device, there in self.ways(0):
            pl.when(there)(lambda b=block, w=way, d=device: self.hop(b, w, 0, d).start())

    def relay(self, step):
        for way, block, come, device, there in self.ways(step):

            def pass_on(way=way, block=block, device=device, there=there):
                self.hop(block, way, step - 1, device).wait_recv()
                if step < self.length - 1:
                    pl.when(there)(lambda: self.hop(block, way, step, device).start())

            pl.when(come)(pass_on)

    def drain(self):
        for step in range(self.length - 1):
            for way, block, come, device, there in self.ways(step):
                pl.when(jnp.logical_and(come, there))(
                    lambda b=block, w=way, d=device, s=step: self.hop(b, w, s, d).wait_send()
                )


def direct_send(view, send, recv, length):
    me = places()[0]
    return [
        remote(view, view, send.at[step - 1], recv.at[step - 1], moved(me, step, length))
        for step in range(1, length)
    ]


def direct_wait(view_of, send, recv, length):
    me = places()[0]
    for step in range(1, length):
        source = moved(me, length - step, length)
        view = view_of(source[0])
        remote(view, view, send.at[step - 1], recv.at[step - 1], source).wait_recv()


def lanes_of(shape):
    return lax.broadcasted_iota(jnp.int32, shape, 1)


def rows_of(shape):
    return lax.broadcasted_iota(jnp.int32, shape, 0)


def product(left, right, dims=((1,), (0,))):
    return lax.dot_general(left, right, (dims, ((), ())), preferred_element_type=jnp.float32)


def gelu_parts(values):
    near = jnp.abs(values) * KEEP
    turn = 1.0 / (1.0 + ERF_P * near)
    bell = jnp.exp(-near * near)
    series = ERF_A[4]
    for term in ERF_A[3::-1]:
        series = series * turn + term
    tail = 0.5 * series * turn * bell
    share = jnp.where(values >= 0, 1.0 - tail, tail)
    return values * share, share + values * bell * SPREAD


def picks(r, block, expert):
    tokens = r.states.shape[0]
    row = r.routes[block, pl.ds(EXP_DEV * lax.axis_index("ctx") + expert, 1), :]
    return (rows_of((CAP, tokens)).astype(jnp.float32) == row).astype(jnp.float32)


def slots(block):
    return pl.ds(pl.multiple_of(block * CAP, CAP), CAP)


def to_owner(length, r, view, target, row, block):
    me = places()[0]
    slot = (block - me[0] + length) % length - 1
    send, recv = r.direct_sems.at[row, slot], r.direct_recvs.at[row, slot]
    return remote(view, target.at[slot], send, recv, (block, me[1], me[2]))


def give_back(length, r, block):
    total = 0.0
    for expert in range(EXP_DEV):
        chosen = picks(r, block, expert).astype(jnp.bfloat16)
        total = total + product(chosen, r.result[expert, slots(block), :], ((0,), (0,)))
    r.cots[block] = total.astype(jnp.bfloat16)


def returns(length, r):
    return (
        LineReturn(length, r.cots, r.mix_in, r.return_send.at[0], r.return_recv.at[0]),
        LineReturn(length, r.entering, r.back_in, r.return_send.at[1], r.return_recv.at[1]),
    )


def forward_part(length, r):
    f32, bf16 = jnp.float32, jnp.bfloat16
    tokens = r.states.shape[0]
    me, twin, beside, above, across = places()
    ctx = me[0]
    peers = [plane_peer(me, k) for k in range(1, 8)] + [moved(me, k, length) for k in range(1, length)]
    barrier = pltpu.get_barrier_semaphore()
    for peer in peers:
        pl.semaphore_signal(barrier, inc=1, device_id=peer, device_id_type=MESH)

    def gather(index, shard, full, halves=None):
        return PlaneGather(
            shard, full, halves, r.plane_send.at[index], r.plane_recv.at[index], r.plane_local.at[index]
        )

    def rows_view(ref, rows):
        return lambda shard: ref.at[pl.ds(shard * rows, rows), :]

    def half_view(ref, rows):
        return lambda shard, half: ref.at[pl.ds(shard * rows + half * (rows // 2), rows // 2), :]

    pack_share = PlaneShare(r.packs, r.pack_send, r.pack_recv)
    query_gather = gather(0, r.query_part, rows_view(r.query, 64), half_view(r.query, 64))
    project_gather = gather(1, r.project_part, rows_view(r.project, 192), half_view(r.project, 192))
    inner_gather = gather(
        2,
        r.inner_part,
        lambda shard: r.inner.at[:, pl.ds(shard * 64, 64), :],
        lambda shard, half: r.inner.at[half, pl.ds(shard * 64, 64), :],
    )
    outer_gathers = [
        gather(
            3 + k, r.outer_part.at[k], rows_view(r.outer.at[k], 256), half_view(r.outer.at[k], 256)
        )
        for k in range(EXP_DEV)
    ]
    cot_gather = LineGather(length, lambda b: r.cots.at[b], r.line_send.at[0], r.line_recv.at[0])
    entering_gather = LineGather(length, lambda b: r.entering.at[b], r.line_send.at[1], r.line_recv.at[1])

    def keyval_view(block):
        return r.keyval.at[pl.ds(block * tokens, tokens), :]

    fetch = pltpu.make_async_copy(r.cotangent_part, r.cotangent, r.plane_local.at[5])
    fetch.start()
    shard = shard_of(me)
    r.packs[shard, 0:64, :] = r.keyval_part[...]
    rows = [r.chooser_part[...].astype(f32), r.selector_part[...].astype(f32), r.vectors[...].astype(f32)]
    rows = jnp.concatenate([*rows, jnp.zeros((8, 64), f32)], 0)
    r.packs[shard, 64:112, :] = jnp.concatenate([rows, jnp.zeros((48, 64), f32)], 1).astype(bf16)
    pl.semaphore_wait(barrier, len(peers))
    pack_sends = pack_share.sends()
    for copy in pack_sends:
        copy.start()
    query_gather.start()
    project_gather.start()
    fetch.wait()
    r.cots[ctx] = r.cotangent[...].astype(bf16)
    cot_gather.start()

    values = r.states[...].astype(f32)
    centred = values - jnp.mean(values, -1, keepdims=True)
    inverse = lax.rsqrt(jnp.mean(centred * centred, -1, keepdims=True) + EPS)
    r.grad_states[...] = centred * inverse

    lane = lanes_of((tokens, 128))
    turned = r.route_ids[...].astype(f32)
    expert_row = rows_of((8, tokens)).astype(f32)
    picked = jnp.logical_or(expert_row == turned[0:1], expert_row == turned[1:2])
    marks = jnp.concatenate([picked.astype(f32), jnp.zeros((8, tokens), f32)], 0).astype(bf16)
    earlier = (rows_of((tokens, tokens)) < lanes_of((tokens, tokens))).astype(f32).astype(bf16)
    ranks = product(marks, earlier)[0:8]
    r.routes[ctx, 0:8, :] = jnp.where(picked, ranks, -1.0)

    ids = jnp.concatenate([r.head_ids[...].astype(f32), jnp.zeros((124, tokens), f32)], 0)
    r.id_columns[...] = jnp.transpose(ids).astype(jnp.int32)
    r.small[48:128, :] = jnp.zeros((80, D), f32)
    pack_share.wait()
    for pair in range(4):
        sides = [r.packs[2 * pair + k, 64:112, :].astype(f32) for k in range(2)]
        both = jnp.where(lanes_of((48, 128)) < 64, sides[0], pltpu.roll(sides[1], 64, 1))
        r.small[0:48, pair * 128 : pair * 128 + 128] = both
    keyval_weight = r.packs[:, 0:64, :].reshape(D, 128)
    shaped = (r.grad_states[...] * r.small[32:33, :] + r.small[33:34, :]).astype(bf16)
    r.acted[...] = shaped
    keyval_view(ctx)[...] = product(shaped, keyval_weight).astype(bf16)
    keyval_sends = direct_send(keyval_view(ctx), r.direct_sems.at[0], r.direct_recvs.at[0], length)
    for copy in keyval_sends:
        copy.start()
    query_gather.relay()

    id_lanes = [r.id_columns[:, j : j + 1] for j in range(MOA_TOP)]
    choice = product(shaped, r.small[...].astype(bf16), ((1,), (1,)))
    logits = [
        jnp.sum(jnp.where(lane == id_lanes[j], choice, 0.0), -1, keepdims=True)
        for j in range(MOA_TOP)
    ]
    peak = jnp.maximum(jnp.maximum(logits[0], logits[1]), jnp.maximum(logits[2], logits[3]))
    powers = [jnp.exp(item - peak) for item in logits]
    total = powers[0] + powers[1] + powers[2] + powers[3]
    gates = [item / total for item in powers]
    r.columns[...] = jnp.where(
        lane == 8,
        gates[0],
        jnp.where(lane == 9, gates[1], jnp.where(lane == 10, gates[2], gates[3])),
    )

    query_gather.relay_rest()
    project_gather.relay()
    inner_gather.start()
    outer_gathers[0].start()
    query_gather.finish()
    for part in range(6):
        columns = slice(part * 256, part * 256 + 256)
        r.mixture[:, columns] = product(r.acted[...], r.query[:, columns]).astype(bf16)
    cot_gather.relay(1)

    low_half = lane < HS
    side = lane // HS
    for j in range(MOA_TOP):
        wanted = id_lanes[j] - side
        chosen = jnp.zeros((tokens, 128), f32)
        for pair in range(MOA_EXPERTS // 2):
            block = r.mixture[:, pair * 128 : pair * 128 + 128].astype(f32)
            chosen = chosen + jnp.where(wanted == 2 * pair, block, 0.0)
        folded = chosen + pltpu.roll(chosen, HS, 1)
        r.queries[j * tokens : (j + 1) * tokens, :] = (
            jnp.where(low_half, folded, 0.0) * HS ** (-0.5)
        ).astype(bf16)

    project_gather.relay_rest()
    direct_wait(keyval_view, r.direct_sems.at[0], r.direct_recvs.at[0], length)
    chunk = 256

    def attend(turn, carried):
        rows = pl.ds(pl.multiple_of(turn * chunk, chunk), chunk)
        scores = product(r.queries[rows, :], r.keyval[...], ((1,), (1,)))
        top = jnp.max(scores, -1, keepdims=True)
        weights = jnp.exp(scores - top)
        mass = jnp.sum(weights, -1, keepdims=True)
        seen = product(weights.astype(bf16), r.keyval[...]) / mass
        r.heads[rows, :] = jnp.where(lanes_of((chunk, 128)) < HS, top + jnp.log(mass), seen)
        return carried

    lax.fori_loop(0, MOA_TOP * tokens // chunk, attend, 0)

    spread = []
    for j in range(MOA_TOP):
        head = r.heads[j * tokens : (j + 1) * tokens, :]
        both = jnp.where(low_half, pltpu.roll(head, HS, 1), head)
        spread.append(both * r.columns[:, 8 + j : 9 + j])
    for pair in range(MOA_EXPERTS // 2):
        block = jnp.zeros((tokens, 128), f32)
        for j in range(MOA_TOP):
            block = jnp.where(id_lanes[j] - side == 2 * pair, spread[j], block)
        r.mixture[:, pair * 128 : pair * 128 + 128] = block.astype(bf16)

    project_gather.finish()
    between = r.states[...].astype(f32) + product(r.mixture[...], r.project[...])
    r.middle[...] = between
    reach = jnp.sum(between * r.small[36:37, :], -1, keepdims=True)
    gap = jnp.sum(r.cotangent[...] * (r.states[...].astype(f32) - between), -1, keepdims=True)
    centred = between - jnp.mean(between, -1, keepdims=True)
    inverse = lax.rsqrt(jnp.mean(centred * centred, -1, keepdims=True) + EPS)
    entry = (centred * inverse * r.small[34:35, :] + r.small[35:36, :]).astype(bf16)
    r.entering[ctx] = entry
    entering_gather.start()
    logits = product(r.small[16:32, :].astype(bf16), entry, ((1,), (1,)))[8:16]
    peak = jnp.max(jnp.where(picked, logits, -1e30), 0, keepdims=True)
    powers = jnp.where(picked, jnp.exp(jnp.where(picked, logits - peak, 0.0)), 0.0)
    r.routes[ctx, 8:16, :] = powers / jnp.sum(powers, 0, keepdims=True)
    r.routes[ctx, 16:24, :] = jnp.transpose(jnp.where(lane == 0, reach, gap))[0:8]
    r.routes[ctx, 18:19, :] = r.remaining[...]
    r.routes[ctx, 19:20, :] = r.left_cot[...]
    route_sends = direct_send(r.routes.at[ctx], r.direct_sems.at[1], r.direct_recvs.at[1], length)
    for copy in route_sends:
        copy.start()

    def first_half(source):
        def one(expert, carried):
            chosen = picks(r, source, expert).astype(bf16)
            rows = product(chosen, r.entering[source]).astype(bf16)
            r.slot_rows[expert, slots(source), :] = rows

            def part(index, kept):
                columns = pl.ds(pl.multiple_of(index * 512, 512), 512)
                before = product(rows, r.inner[expert, :, columns])
                value, gradient = gelu_parts(before)
                r.active[expert, slots(source), columns] = value.astype(bf16)
                r.slope[expert, slots(source), columns] = gradient.astype(bf16)
                return kept

            return lax.fori_loop(0, 4, part, carried)

        lax.fori_loop(0, EXP_DEV, one, 0)

    def second_half(first, count):
        rows = pl.ds(pl.multiple_of(first * CAP, CAP), count * CAP)

        def one(expert, carried):
            value = product(r.active[expert, rows, :], r.outer[expert])
            r.result[expert, rows, :] = value.astype(bf16)
            return carried

        lax.fori_loop(0, EXP_DEV, one, 0)

    def score(source, carried):
        lines = []
        for expert in range(EXP_DEV):
            chosen = picks(r, source, expert)
            cot_rows = product(chosen.astype(bf16), r.cots[source]).astype(bf16)
            r.slot_cot[expert, slots(source), :] = cot_rows
            rows = r.result[expert, slots(source), :].astype(f32)
            toward = jnp.sum(rows * r.small[36:37, :], -1, keepdims=True)
            against = jnp.sum(rows * cot_rows.astype(f32), -1, keepdims=True)
            gate_row = r.routes[source, pl.ds(8 + EXP_DEV * ctx + expert, 1), :]
            gate = jnp.sum(chosen * gate_row, -1, keepdims=True)
            r.result[expert, slots(source), :] = (rows * gate).astype(bf16)
            lines.append(jnp.sum(chosen * toward, 0, keepdims=True))
            lines.append(jnp.sum(chosen * against, 0, keepdims=True))
        lines.append(jnp.zeros((8 - 2 * EXP_DEV, tokens), f32))
        sheet = jnp.concatenate(lines, 0)

        r.scores[ctx, source] = sheet
        return carried

    lower = ctx < length // 2
    last = jnp.where(lower, length - 1, 0)
    at_end = jnp.logical_or(ctx == 0, ctx == length - 1)

    def arrival(turn):
        along = jnp.where(lower, turn, length - 1 - turn)
        around = jnp.where(turn == 0, ctx, jnp.where(turn == 1, ctx - 1, ctx + 1))
        return jnp.where(at_end, along, around)

    inner_gather.relay()
    outer_gathers[1].start()
    direct_wait(lambda b: r.routes.at[b], r.direct_sems.at[1], r.direct_recvs.at[1], length)
    entering_gather.relay(1)
    inner_gather.relay_rest()
    inner_gather.finish()
    outer_gathers[0].relay()

    def near(turn, carried):
        @pl.when(turn == 1)
        def _():
            entering_gather.relay(2)
            cot_gather.relay(2)

        @pl.when(turn == 2)
        def _():
            outer_gathers[1].relay()
            outer_gathers[0].relay_rest()

        first_half(arrival(turn))
        return carried

    lax.fori_loop(0, length - 1, near, 0)
    outer_gathers[1].relay_rest()
    for item in outer_gathers:
        item.finish()
    second_half(jnp.where(lower, 0, 1), length - 1)
    lax.fori_loop(0, length - 1, lambda turn, carried: score(arrival(turn), carried), 0)
    entering_gather.relay(length - 1)
    first_half(last)
    second_half(last, 1)
    cot_gather.relay(length - 1)
    score(last, 0)
    cot_gather.drain()
    score_sends = direct_send(r.scores.at[ctx], r.direct_sems.at[2], r.direct_recvs.at[2], length)
    for copy in score_sends:
        copy.start()
    mixed, unused = returns(length, r)
    for index in range(2):
        give_back(length, r, mixed.far + index)
    direct_wait(lambda b: r.scores.at[b], r.direct_sems.at[2], r.direct_recvs.at[2], length)
    for copy in keyval_sends + route_sends + score_sends:
        copy.wait_send()
    for copy in pack_sends:
        copy.wait_send()
    for item in (query_gather, project_gather, inner_gather, *outer_gathers):
        item.drain()
    entering_gather.drain()


class LineReturn:
    def __init__(self, length, parts, arrived, send, recv):
        self.length, self.parts, self.arrived = length, parts, arrived
        self.send, self.recv = send, recv
        self.me = places()[0]
        ctx = self.me[0]
        self.at_end = jnp.logical_or(ctx == 0, ctx == length - 1)
        self.inside = jnp.logical_not(self.at_end)
        self.next = (ctx + 1 - 2 * (ctx % 2), self.me[1], self.me[2])
        self.far = (1 - ctx // 2) * 2

    def copy(self, block, place, slot, device):
        return remote(
            self.parts.at[block], self.arrived.at[place], self.send.at[slot], self.recv.at[slot], device
        )

    def hand(self, index):
        return self.copy(self.far + index, index, index, self.next)

    def near(self):
        return self.copy(self.next[0], 2, 2, self.next)

    def across(self, index):
        block = self.far + index
        return self.copy(block, 3, 3 + index, (block, self.me[1], self.me[2]))

    def start_far(self, index):
        pl.when(self.at_end)(lambda: self.hand(index).start())

    def pass_on(self, index):
        @pl.when(self.inside)
        def _():
            self.hand(index).wait_recv()
            block = self.far + index
            both = self.parts[block].astype(jnp.float32) + self.arrived[index].astype(jnp.float32)
            self.parts[block] = both.astype(jnp.bfloat16)
            self.across(index).start()

    def start_near(self):
        self.near().start()

    def wait(self):
        self.near().wait_recv()
        self.across(self.me[0] % 2).wait_recv()

    def total(self):
        own = self.parts[self.me[0]].astype(jnp.float32)
        return own + self.arrived[2].astype(jnp.float32) + self.arrived[3].astype(jnp.float32)

    def drain(self):
        self.near().wait_send()
        for index in range(2):
            pl.when(self.at_end)(lambda i=index: self.hand(i).wait_send())
            pl.when(self.inside)(lambda i=index: self.across(i).wait_send())


class PlaneReduce:
    def __init__(self, piece, rows, halves, arrived, send, recv):
        self.piece, self.rows, self.halves, self.arrived = piece, rows, halves, arrived
        self.send, self.recv = send, recv
        self.me, self.twin, self.beside, self.above, self.across = places()
        self.chip, self.core, self.line = self.me[1] // 2, self.me[1] % 2, self.me[2]

    def half(self, chip, core):
        view, half = self.piece(chip, core), self.halves.at[chip]
        return remote(view, half, self.send.at[chip], self.recv.at[chip], self.twin)

    def shard(self, chip, line):
        return self.piece(chip, self.core).at[pl.ds(line * self.rows, self.rows), :]

    def start(self):
        for chip in range(2):
            self.half(chip, 1 - self.core).start()

    def spread(self, slot, chip, line, device):
        return remote(
            self.shard(chip, line),
            self.arrived.at[slot],
            self.send.at[2 + slot],
            self.recv.at[2 + slot],
            device,
        )

    def sends(self):
        return (
            self.spread(0, 1 - self.chip, self.line, self.beside),
            self.spread(1, self.chip, 1 - self.line, self.above),
            self.spread(2, 1 - self.chip, 1 - self.line, self.across),
        )

    def add_halves(self):
        for chip in range(2):
            self.half(chip, self.core).wait_recv()
            view = self.piece(chip, self.core)
            both = view[...].astype(jnp.float32) + self.halves[chip].astype(jnp.float32)
            view[...] = both.astype(jnp.bfloat16)
        for copy in self.sends():
            copy.start()

    def total(self):
        for copy in self.sends():
            copy.wait_recv()
        value = self.shard(self.chip, self.line)[...].astype(jnp.float32)
        for slot in range(3):
            value = value + self.arrived[slot].astype(jnp.float32)
        return value

    def drain(self):
        for chip in range(2):
            self.half(chip, 1 - self.core).wait_send()
        for copy in self.sends():
            copy.wait_send()


class LineSum:
    def __init__(self, length, value, parts, summed, reduce_sems, gather_sems):
        self.length, self.value, self.parts, self.summed = length, value, parts, summed
        self.reduce_sems, self.gather_sems = reduce_sems, gather_sems
        self.me = places()[0]
        self.share = value.shape[0] // length

    def rows(self, block):
        return pl.ds(pl.multiple_of(block * self.share, self.share), self.share)

    def part(self, step):
        target = moved(self.me, step, self.length)
        send, recv = self.reduce_sems
        return remote(
            self.value.at[self.rows(target[0]), :],
            self.parts.at[step - 1],
            send.at[step - 1],
            recv.at[step - 1],
            target,
        )

    def start(self, value):
        self.value[...] = value.astype(jnp.bfloat16)
        for step in range(1, self.length):
            self.part(step).start()

    def view(self, block):
        return self.summed.at[self.rows(block), :]

    def share_out(self):
        for step in range(1, self.length):
            self.part(step).wait_recv()
        value = self.value[self.rows(self.me[0]), :].astype(jnp.float32)
        for step in range(1, self.length):
            value = value + self.parts[step - 1].astype(jnp.float32)
        self.view(self.me[0])[...] = value.astype(jnp.bfloat16)
        for copy in direct_send(self.view(self.me[0]), *self.gather_sems, self.length):
            copy.start()

    def finish(self):
        direct_wait(self.view, *self.gather_sems, self.length)
        return self.summed[...]

    def drain(self):
        for step in range(1, self.length):
            self.part(step).wait_send()
        for copy in direct_send(self.view(self.me[0]), *self.gather_sems, self.length):
            copy.wait_send()


class ExpertReduce:
    def __init__(self, inner, outer, half_in, half_out, side_in, side_out, last_in, last_out, send, recv):
        self.arrays = (inner, outer)
        self.halves = (half_in, half_out)
        self.sides = (side_in, side_out)
        self.lasts = (last_in, last_out)
        self.counts = (64, 256)
        self.send, self.recv = send, recv
        self.me, self.twin, self.beside, self.above, unused = places()
        self.chip, self.core, self.line = self.me[1] // 2, self.me[1] % 2, self.me[2]

    def rows(self, which, expert, chip, core, line, count):
        size = self.counts[which]
        start = pl.multiple_of(((chip * 2 + core) * 2 + line) * size, size)
        return self.arrays[which].at[expert, pl.ds(start, count * size), :]

    def copy(self, source, target, which, expert, slot, device):
        unit = 2 * which + expert
        return remote(source, target, self.send.at[unit, slot], self.recv.at[unit, slot], device)

    def half(self, which, expert, chip, core):
        source = self.rows(which, expert, chip, core, 0, 2)
        return self.copy(source, self.halves[which].at[chip, expert], which, expert, chip, self.twin)

    def start(self, which):
        for expert in range(EXP_DEV):
            for chip in range(2):
                self.half(which, expert, chip, 1 - self.core).start()

    def side(self, which, expert, index):
        if expert == 0:
            source, device = self.rows(which, 0, 1 - self.chip, self.core, index, 1), self.beside
        else:
            source, device = self.rows(which, 1, index, self.core, 1 - self.line, 1), self.above
        return self.copy(source, self.sides[which].at[expert, index], which, expert, 2 + index, device)

    def add(self, view, other):
        view[...] = (view[...].astype(jnp.float32) + other[...].astype(jnp.float32)).astype(jnp.bfloat16)

    def add_halves(self, which):
        for expert in range(EXP_DEV):
            for chip in range(2):
                self.half(which, expert, chip, self.core).wait_recv()
                self.add(self.rows(which, expert, chip, self.core, 0, 2), self.halves[which].at[chip, expert])
            for index in range(2):
                self.side(which, expert, index).start()

    def last(self, which, expert):
        if expert == 0:
            source, device = self.rows(which, 0, self.chip, self.core, 1 - self.line, 1), self.above
        else:
            source, device = self.rows(which, 1, 1 - self.chip, self.core, self.line, 1), self.beside
        return self.copy(source, self.lasts[which].at[expert], which, expert, 4, device)

    def add_sides(self, which):
        for expert in range(EXP_DEV):
            for index in range(2):
                self.side(which, expert, index).wait_recv()
                chip, line = (self.chip, index) if expert == 0 else (index, self.line)
                self.add(
                    self.rows(which, expert, chip, self.core, line, 1), self.sides[which].at[expert, index]
                )
            self.last(which, expert).start()

    def total(self, which, result):
        for expert in range(EXP_DEV):
            self.last(which, expert).wait_recv()
            view = self.rows(which, expert, self.chip, self.core, self.line, 1)
            both = view[...].astype(jnp.float32) + self.lasts[which][expert].astype(jnp.float32)
            result[expert] = both.astype(jnp.bfloat16)

    def drain(self):
        for which in range(2):
            for expert in range(EXP_DEV):
                for chip in range(2):
                    self.half(which, expert, chip, 1 - self.core).wait_send()
                for index in range(2):
                    self.side(which, expert, index).wait_send()
                self.last(which, expert).wait_send()


def backward_part(length, r):
    f32, bf16 = jnp.float32, jnp.bfloat16
    tokens = r.states.shape[0]
    me = places()[0]
    ctx = me[0]
    lane = lanes_of((tokens, 128))
    low_half = lane < HS
    side = lane // HS
    id_lanes = [r.id_columns[:, j : j + 1] for j in range(MOA_TOP)]

    def sems(row):
        return r.direct_sems.at[row], r.direct_recvs.at[row]

    def from_all(target_ref, row):
        send, recv = sems(row)
        for step in range(1, length):
            view = target_ref.at[step - 1]
            source = moved(me, length - step, length)
            remote(view, view, send.at[step - 1], recv.at[step - 1], source).wait_recv()

    def sent_all(view_of, target_ref, row):
        for step in range(1, length):
            block = moved(me, step, length)[0]
            to_owner(length, r, view_of(block), target_ref, row, block).wait_send()

    r.gsmall[...] = jnp.zeros_like(r.gsmall)
    mid = r.middle[...]
    halt_row = r.small[36:37, :]

    def scalars(block):
        gates = r.routes[block, 8:16, :]
        lines = [
            [r.scores[d, block, 2 * e + k : 2 * e + k + 1, :] for d in range(length) for e in range(EXP_DEV)]
            for k in range(2)
        ]
        toward, against = (jnp.concatenate(item, 0) for item in lines)
        own = r.routes[block, 16:24, :]
        halting = jax.nn.sigmoid(own[0:1] + jnp.sum(gates * toward, 0, keepdims=True))
        stop_grad = own[1:2] - jnp.sum(gates * against, 0, keepdims=True)
        mass, left = own[2:3], own[3:4]
        stopped = mass * halting
        halt_grad = (stop_grad - left) * mass * halting * (1.0 - halting)
        sheet = jnp.concatenate([1.0 - stopped, halt_grad, stopped, jnp.zeros((5, tokens), f32)], 0)
        r.factors[block] = sheet
        return gates, toward, against, halting, stop_grad, mass, left, stopped, halt_grad, sheet

    def other(step, carried):
        scalars((ctx + step) % length)
        return carried

    lax.fori_loop(1, length, other, 0)
    gates, toward, against, halting, stop_grad, mass, left, stopped, halt_grad, sheet = scalars(ctx)
    mixed, backs = returns(length, r)
    mixed.start_far(0)
    r.rows_out[0:1, :] = mass * (1.0 - halting)
    r.rows_out[1:2, :] = stop_grad * halting + left * (1.0 - halting)
    turned = jnp.transpose(jnp.concatenate([sheet, jnp.zeros((120, tokens), f32)], 0))
    r.columns[...] = jnp.where(lane < 8, turned, r.columns[...])
    gate_grad = (1.0 - stopped) * against + halt_grad * toward
    pick_grad = gates * (gate_grad - jnp.sum(gates * gate_grad, 0, keepdims=True))
    coarse = pick_grad.astype(bf16).astype(f32)
    r.pick_grads[...] = jnp.concatenate([coarse, pick_grad - coarse], 0).astype(bf16)
    sums = product(r.pick_grads[...], r.entering[ctx])
    r.gsmall[24:32, :] = sums[0:8] + sums[8:16]
    halt_col = r.columns[:, 1:2]
    r.gsmall[36:37, :] = jnp.sum(halt_col * mid, 0, keepdims=True)

    def rows_back(block):
        for expert in range(EXP_DEV):
            chosen = picks(r, block, expert)
            keep = jnp.sum(chosen * r.factors[block, 0:1, :], -1, keepdims=True)
            halt = jnp.sum(chosen * r.factors[block, 1:2, :], -1, keepdims=True)
            gate_row = r.routes[block, pl.ds(8 + EXP_DEV * ctx + expert, 1), :]
            gate = jnp.sum(chosen * gate_row, -1, keepdims=True)
            rows = r.result[expert, slots(block), :].astype(f32)
            r.gsmall[36:37, :] += jnp.sum(halt * rows, 0, keepdims=True)
            incoming = r.slot_cot[expert, slots(block), :].astype(f32)
            rows_grad = (gate * (keep * incoming + halt * halt_row)).astype(bf16)
            r.slot_cot[expert, slots(block), :] = rows_grad

    side_blocks = length // 2
    side_rows = side_blocks * CAP

    def prepare(turn, carried):
        rows_back((ctx + turn) % length)
        return carried

    def rows_of_half(half):
        return pl.ds(pl.multiple_of(half * side_rows, side_rows), side_rows)

    def hidden_back(half):
        rows = rows_of_half(half)

        def part(turn, carried):
            expert, index = turn // 2, turn % 2
            columns = pl.ds(pl.multiple_of(index * 1024, 1024), 1024)
            back = product(r.slot_cot[expert, rows, :], r.outer[expert, columns, :], ((1,), (1,)))
            slope = r.slope[expert, rows, columns].astype(f32)
            r.slope[expert, rows, columns] = (back * slope).astype(bf16)
            return carried

        lax.fori_loop(0, 2 * EXP_DEV, part, 0)

    def entering_back(half):
        rows = rows_of_half(half)

        def one(expert, carried):
            sent = product(r.slope[expert, rows, :], r.inner[expert], ((1,), (1,)))
            r.slot_back[expert] = sent.astype(bf16)
            return carried

        lax.fori_loop(0, EXP_DEV, one, 0)

        def gather_up(index, carried):
            block = half * side_blocks + index
            total = 0.0
            for expert in range(EXP_DEV):
                chosen = picks(r, block, expert).astype(bf16)
                total = total + product(chosen, r.slot_back[expert, slots(index), :], ((0,), (0,)))
            r.entering[block] = total.astype(bf16)
            return carried

        lax.fori_loop(0, side_blocks, gather_up, 0)

    def outer_grad(turn, carried):
        expert, part = turn // 4, turn % 4
        columns = pl.ds(pl.multiple_of(part * 512, 512), 512)
        value = product(r.active[expert, :, columns], r.slot_cot[expert], ((0,), (0,)))
        r.outer[expert, columns, :] = value.astype(bf16)
        return carried

    def inner_grad(turn, carried):
        expert, part = turn // 4, turn % 4
        columns = pl.ds(pl.multiple_of(part * 512, 512), 512)
        value = product(r.slot_rows[expert], r.slope[expert, :, columns], ((0,), (0,)))
        r.inner[expert, :, columns] = value.astype(bf16)
        return carried

    near, far = ctx // side_blocks, 1 - ctx // side_blocks
    experts = ExpertReduce(
        r.inner, r.outer, r.half_in, r.half_out, r.side_in, r.side_out, r.last_in, r.last_out,
        r.expert_send, r.expert_recv,
    )
    lax.fori_loop(0, length, prepare, 0)
    hidden_back(far)
    entering_back(far)
    for index in range(2):
        backs.start_far(index)
    hidden_back(near)
    lax.fori_loop(0, 4 * EXP_DEV, outer_grad, 0)
    experts.start(1)
    entering_back(near)
    backs.start_near()
    mixed.start_far(1)
    experts.add_halves(1)
    give_back(length, r, backs.next[0])
    mixed.start_near()
    give_back(length, r, ctx)
    backs.pass_on(0)
    lax.fori_loop(0, 4 * EXP_DEV, inner_grad, 0)
    experts.start(0)
    backs.pass_on(1)
    mixed.pass_on(0)
    experts.add_halves(0)
    experts.add_sides(1)

    backs.wait()
    mid = r.middle[...]
    selector = r.small[24:32, :]
    double = jnp.concatenate([selector, selector], 0).astype(bf16)
    back = product(r.pick_grads[...], double, ((0,), (0,))) + backs.total()
    centred = mid - jnp.mean(mid, -1, keepdims=True)
    inverse = lax.rsqrt(jnp.mean(centred * centred, -1, keepdims=True) + EPS)
    plain = centred * inverse
    r.gsmall[34:35, :] = jnp.sum(back * plain, 0, keepdims=True)
    r.gsmall[35:36, :] = jnp.sum(back, 0, keepdims=True)
    scaled = back * r.small[34:35, :]
    level = jnp.mean(scaled, -1, keepdims=True)
    tilt = jnp.mean(scaled * plain, -1, keepdims=True)
    cot = r.cotangent[...]
    flow = r.columns[:, 0:1] * cot + r.columns[:, 1:2] * halt_row
    flow = flow + inverse * (scaled - level - plain * tilt)
    r.grad_states[...] = flow + r.columns[:, 2:3] * cot
    attn_grad = flow.astype(bf16)

    def project_piece(chip, core):
        column = pl.multiple_of((chip * 2 + core) * 512, 512)
        return r.active.at[1, pl.ds(0, 384), pl.ds(column, 512)]

    for part in range(4):
        value = product(r.mixture[:, part * 384 : part * 384 + 384], attn_grad, ((0,), (0,)))
        r.active[1, 0:384, part * 512 : part * 512 + 512] = value.astype(bf16)

    def reducer(index, piece, rows, halves, arrived):
        return PlaneReduce(piece, rows, halves, arrived, r.dense_send.at[index], r.dense_recv.at[index])

    project_reduce = reducer(0, project_piece, 192, r.project_half, r.project_in)
    project_reduce.start()

    chosen = [jnp.zeros((tokens, 128), f32) for unused in range(MOA_TOP)]
    for part in range(6):
        value = product(attn_grad, r.project[part * 256 : part * 256 + 256, :], ((1,), (1,)))
        for pair in range(2):
            block = value[:, pair * 128 : pair * 128 + 128]
            for j in range(MOA_TOP):
                wanted = id_lanes[j] - side == 2 * (2 * part + pair)
                chosen[j] = chosen[j] + jnp.where(wanted, block, 0.0)
    gate_lanes = [r.columns[:, 8 + j : 9 + j] for j in range(MOA_TOP)]
    gate_grads = []
    for j in range(MOA_TOP):
        rows = slice(j * tokens, (j + 1) * tokens)
        head = r.heads[rows, :]
        folded = jnp.where(low_half, 0.0, chosen[j] + pltpu.roll(chosen[j], HS, 1))
        gate_grads.append(jnp.sum(folded * head, -1, keepdims=True))
        grads = (gate_lanes[j] * folded).astype(bf16)
        r.heads_grad[rows, :] = grads
        delta = jnp.sum(grads.astype(f32) * head, -1, keepdims=True)
        pair = jnp.transpose(jnp.where(lane == 0, head[:, 0:1], delta))
        r.stats[:, rows] = pair[0:8]
    common = sum(g * v for g, v in zip(gate_lanes, gate_grads))
    logit = jnp.zeros((tokens, 128), f32)
    for j in range(MOA_TOP):
        logit = jnp.where(lane == id_lanes[j], gate_lanes[j] * (gate_grads[j] - common), logit)
    coarse = logit.astype(bf16)
    fine = (logit - coarse.astype(f32)).astype(bf16)
    sums = product(coarse, r.acted[...], ((0,), (0,))) + product(fine, r.acted[...], ((0,), (0,)))
    r.gsmall[0:24, :] = sums[0:24]
    chooser = r.small[...].astype(bf16)
    r.cotangent[...] = product(coarse, chooser) + product(fine, chooser)
    project_reduce.add_halves()
    mixed.pass_on(1)
    experts.add_sides(0)

    r.kv_grad[...] = jnp.zeros_like(r.kv_grad)
    chunk = 512

    half_keys = tokens

    def attend_back(turn, carried):
        rows = pl.ds(pl.multiple_of((turn // length) * chunk, chunk), chunk)
        keys = pl.ds(pl.multiple_of((turn % length) * half_keys, half_keys), half_keys)
        query, grads, keyval = r.queries[rows, :], r.heads_grad[rows, :], r.keyval[keys, :]
        scores = product(keyval, query, ((1,), (1,)))
        weights = jnp.exp(scores - r.stats[0:1, rows])
        upward = product(keyval, grads, ((1,), (1,)))
        score_grad = (weights * (upward - r.stats[1:2, rows])).astype(bf16)
        r.kv_grad[keys, :] += product(score_grad, query) + product(weights.astype(bf16), grads)
        down = product(score_grad, keyval, ((0,), (0,))) * HS ** (-0.5)

        @pl.when(turn % length == 0)
        def _():
            r.heads[rows, :] = down

        @pl.when(turn % length > 0)
        def _():
            r.heads[rows, :] += down

        return carried

    lax.fori_loop(0, length * MOA_TOP * tokens // chunk, attend_back, 0)

    def send_keyval(turn, carried):
        block = (ctx + turn) % length
        rows = pl.ds(pl.multiple_of(block * tokens, tokens), tokens)

        @pl.when(turn > 0)
        def _():
            r.heads_grad[rows, :] = r.kv_grad[rows, :].astype(bf16)
            to_owner(length, r, r.heads_grad.at[rows, :], r.kv_in, 6, block).start()

        return carried

    lax.fori_loop(0, length, send_keyval, 0)
    spread = []
    for j in range(MOA_TOP):
        piece = r.heads[j * tokens : (j + 1) * tokens, :]
        spread.append(jnp.where(low_half, piece, pltpu.roll(piece, HS, 1)))
    for pair in range(MOA_EXPERTS // 2):
        block = jnp.zeros((tokens, 128), f32)
        for j in range(MOA_TOP):
            block = jnp.where(id_lanes[j] - side == 2 * pair, spread[j], block)
        r.mixture[:, pair * 128 : pair * 128 + 128] = block.astype(bf16)
    for part in range(4):
        columns = slice(part * 384, part * 384 + 384)
        value = product(r.acted[...], r.mixture[:, columns], ((0,), (0,)))
        r.active[0, 0:512, columns] = value.astype(bf16)

    def wide_piece(first, width):
        def piece(chip, core):
            start = pl.multiple_of((chip * 2 + core) * 128, 128)
            return r.active.at[0, pl.ds(start, 128), pl.ds(first, width)]

        return piece

    query_reduce = reducer(1, wide_piece(0, 1536), 64, r.query_half, r.query_in)
    query_reduce.start()
    r.cotangent[...] += product(r.mixture[...], r.query[...], ((1,), (1,)))
    project_line = LineSum(length, r.project_value, r.project_parts, r.project_sum, sems(7), sems(8))
    project_line.start(project_reduce.total())
    query_reduce.add_halves()

    own_rows = pl.ds(pl.multiple_of(ctx * tokens, tokens), tokens)
    from_all(r.kv_in, 6)
    keyval_grad = r.kv_grad[own_rows, :]
    for step in range(length - 1):
        keyval_grad = keyval_grad + r.kv_in[step].astype(f32)
    keyval_grad = keyval_grad.astype(bf16)
    back = r.cotangent[...] + product(keyval_grad, r.packs[:, 0:64, :].reshape(D, 128), ((1,), (1,)))
    values = r.states[...].astype(f32)
    centred = values - jnp.mean(values, -1, keepdims=True)
    inverse = lax.rsqrt(jnp.mean(centred * centred, -1, keepdims=True) + EPS)
    plain = centred * inverse
    r.gsmall[32:33, :] = jnp.sum(back * plain, 0, keepdims=True)
    r.gsmall[33:34, :] = jnp.sum(back, 0, keepdims=True)
    r.active[0, 0:512, 1536:1664] = product(r.acted[...], keyval_grad, ((0,), (0,))).astype(bf16)
    r.active[0, 0:512, 1664:1792] = jnp.transpose(r.gsmall[...]).astype(bf16)
    small_reduce = reducer(2, wide_piece(1536, 256), 64, r.small_half, r.small_in)
    small_reduce.start()
    scaled = back * r.small[32:33, :]
    level = jnp.mean(scaled, -1, keepdims=True)
    tilt = jnp.mean(scaled * plain, -1, keepdims=True)
    r.grad_states[...] = (
        r.grad_states[...] + inverse * (scaled - level - plain * tilt)
    )
    small_reduce.add_halves()
    project_line.share_out()
    query_line = LineSum(length, r.query_value, r.query_parts, r.query_sum, sems(9), sems(10))
    query_line.start(query_reduce.total())
    small_line = LineSum(length, r.small_value, r.small_parts, r.small_sum, sems(11), sems(12))
    small_line.start(small_reduce.total())

    experts.total(1, r.grad_outer)
    experts.total(0, r.grad_inner)
    mixed.wait()
    final = r.middle[...] + mixed.total()
    r.new_states[...] = (
        r.columns[:, 2:3] * r.states[...].astype(f32) + r.columns[:, 0:1] * final
    ).astype(bf16)
    query_line.share_out()
    small_line.share_out()
    r.grad_project[...] = project_line.finish()
    r.grad_query[...] = query_line.finish()
    r.grad_small[...] = small_line.finish()

    mixed.drain()
    backs.drain()
    sent_all(
        lambda b: r.heads_grad.at[pl.ds(pl.multiple_of(b * tokens, tokens), tokens), :], r.kv_in, 6
    )
    for item in (project_reduce, query_reduce, small_reduce, experts):
        item.drain()
    for item in (project_line, query_line, small_line):
        item.drain()


def whole_kernel(length, names, *refs):
    r = SimpleNamespace(**dict(zip(names, refs)))
    forward_part(length, r)
    backward_part(length, r)


def write_kernel(
    new_states, rows_out, grad_states, grad_query, grad_project, grad_small, grad_inner, grad_outer, *outs
):
    f32 = jnp.float32
    outs[0][0] = new_states[...]
    outs[1][...] = rows_out[0:1, :]
    outs[2][0] = grad_states[...]
    outs[3][...] = rows_out[1:2, :]
    outs[4][...] = grad_query[...].astype(f32)
    outs[5][...] = grad_small[:, 0:128].astype(f32)
    outs[6][...] = grad_project[...].astype(f32)
    turned = jnp.transpose(grad_small[:, 128:256].astype(f32))
    outs[7][...] = turned[0:24]
    outs[8][...] = turned[24:32]
    for index in range(5):
        outs[9 + index][...] = turned[32 + index : 33 + index]
    outs[14][...] = grad_inner[...].astype(f32)
    outs[15][...] = grad_outer[...].astype(f32)


def write_out(tokens, *results):
    f32, bf16 = jnp.float32, jnp.bfloat16
    shape = jax.ShapeDtypeStruct
    outs = (
        shape((1, tokens, D), bf16),
        shape((1, tokens), f32),
        shape((1, tokens, D), f32),
        shape((1, tokens), f32),
        shape((64, MOA_EXPERTS * HS), f32),
        shape((64, 128), f32),
        shape((192, D), f32),
        shape((MOA_EXPERTS, 64), f32),
        shape((8, 64), f32),
        *[shape((1, 64), f32)] * 5,
        shape((EXP_DEV, 64, FF), f32),
        shape((EXP_DEV, 256, D), f32),
    )
    in_vmem = pl.BlockSpec(memory_space=pltpu.VMEM)
    final = pl.pallas_call(
        write_kernel,
        out_shape=outs,
        in_specs=[in_vmem] * len(results),
        out_specs=[in_vmem] * len(outs),
        compiler_params=pltpu.CompilerParams(vmem_limit_bytes=LIMIT_MIB * 2**20),
        name="write_out",
    )(*results)
    vectors = [item.reshape(64) for item in final[9:14]]
    return (*final[0:7], final[7].T, final[8].T, *vectors, *final[14:16])


def fast_body(
    states,
    remaining,
    moa_ids,
    ffn_ids,
    out_cotangent,
    left_cotangent,
    query_weight,
    keyval_weight,
    project_weight,
    chooser,
    selector,
    gain_one,
    bias_one,
    gain_two,
    bias_two,
    halt_weight,
    expert_in,
    expert_out,
):
    f32, bf16 = jnp.float32, jnp.bfloat16
    length = lax.axis_size("ctx")
    tokens = states.shape[1]
    rows = length * CAP
    wide = MOA_EXPERTS * HS
    nothing = jnp.zeros_like(gain_one)
    vectors = jnp.stack(
        [gain_one, bias_one, gain_two, bias_two, halt_weight, nothing, nothing, nothing], 0
    )
    inputs = dict(
        states=states[0],
        cotangent_part=out_cotangent[0],
        head_ids=moa_ids[0].T,
        route_ids=ffn_ids[0].T,
        remaining=remaining,
        left_cot=left_cotangent,
        keyval_part=keyval_weight,
        chooser_part=chooser.T,
        selector_part=selector.T,
        vectors=vectors,
        query_part=query_weight,
        project_part=project_weight,
        inner_part=expert_in,
        outer_part=expert_out,
    )
    in_place = ("cotangent_part", "query_part", "project_part", "inner_part", "outer_part")
    shape = jax.ShapeDtypeStruct
    outputs = dict(
        new_states=shape((tokens, D), bf16),
        rows_out=shape((8, tokens), f32),
        grad_states=shape((tokens, D), f32),
        grad_query=shape((64, wide), bf16),
        grad_project=shape((192, D), bf16),
        grad_small=shape((64, 256), bf16),
        grad_inner=shape((EXP_DEV, 64, FF), bf16),
        grad_outer=shape((EXP_DEV, 256, D), bf16),
    )
    vmem, dma = pltpu.VMEM, pltpu.SemaphoreType.DMA
    scratch = dict(
        slot_rows=vmem((EXP_DEV, rows, D), bf16),
        active=vmem((EXP_DEV, rows, FF), bf16),
        slope=vmem((EXP_DEV, rows, FF), bf16),
        result=vmem((EXP_DEV, rows, D), bf16),
        slot_cot=vmem((EXP_DEV, rows, D), bf16),
        inner=vmem((EXP_DEV, D, FF), bf16),
        outer=vmem((EXP_DEV, FF, D), bf16),
        query=vmem((D, wide), bf16),
        project=vmem((wide, D), bf16),
        packs=vmem((8, 112, 128), bf16),
        id_columns=vmem((tokens, 128), jnp.int32),
        cotangent=vmem((tokens, D), f32),
        acted=vmem((tokens, D), bf16),
        mixture=vmem((tokens, wide), bf16),
        queries=vmem((MOA_TOP * tokens, 128), bf16),
        heads=vmem((MOA_TOP * tokens, 128), f32),
        keyval=vmem((length * tokens, 128), bf16),
        middle=vmem((tokens, D), f32),
        entering=vmem((length, tokens, D), bf16),
        cots=vmem((length, tokens, D), bf16),
        routes=vmem((length, 24, tokens), f32),
        scores=vmem((length, length, 8, tokens), f32),
        small=vmem((128, D), f32),
        factors=vmem((length, 8, tokens), f32),
        columns=vmem((tokens, 128), f32),
        pick_grads=vmem((16, tokens), bf16),
        gsmall=vmem((128, D), f32),
        slot_back=vmem((EXP_DEV, rows // 2, D), bf16),
        back_in=vmem((4, tokens, D), bf16),
        mix_in=vmem((4, tokens, D), bf16),
        half_in=vmem((2, EXP_DEV, 128, FF), bf16),
        half_out=vmem((2, EXP_DEV, 512, D), bf16),
        side_in=vmem((EXP_DEV, 2, 64, FF), bf16),
        side_out=vmem((EXP_DEV, 2, 256, D), bf16),
        last_in=vmem((EXP_DEV, 64, FF), bf16),
        last_out=vmem((EXP_DEV, 256, D), bf16),
        heads_grad=vmem((MOA_TOP * tokens, 128), bf16),
        stats=vmem((8, MOA_TOP * tokens), f32),
        kv_grad=vmem((length * tokens, 128), f32),
        kv_in=vmem((length - 1, tokens, 128), bf16),
        project_half=vmem((2, 384, D), bf16),
        project_in=vmem((3, 192, D), bf16),
        query_half=vmem((2, 128, wide), bf16),
        query_in=vmem((3, 64, wide), bf16),
        small_half=vmem((2, 128, 256), bf16),
        small_in=vmem((3, 64, 256), bf16),
        project_value=vmem((192, D), bf16),
        project_parts=vmem((length - 1, 192 // length, D), bf16),
        project_sum=vmem((192, D), bf16),
        query_value=vmem((64, wide), bf16),
        query_parts=vmem((length - 1, 64 // length, wide), bf16),
        query_sum=vmem((64, wide), bf16),
        small_value=vmem((64, 256), bf16),
        small_parts=vmem((length - 1, 64 // length, 256), bf16),
        small_sum=vmem((64, 256), bf16),
        pack_send=dma((7,)),
        pack_recv=dma((7,)),
        plane_send=dma((5, 9)),
        plane_recv=dma((5, 9)),
        plane_local=dma((6,)),
        line_send=dma((2, 2, length)),
        line_recv=dma((2, 2, length)),
        direct_sems=dma((13, length)),
        direct_recvs=dma((13, length)),
        return_send=dma((2, 5)),
        return_recv=dma((2, 5)),
        expert_send=dma((4, 5)),
        expert_recv=dma((4, 5)),
        dense_send=dma((3, 5)),
        dense_recv=dma((3, 5)),
    )
    in_vmem = pl.BlockSpec(memory_space=pltpu.VMEM)
    anywhere = pl.BlockSpec(memory_space=pl.ANY)
    names = (*inputs, *outputs, *scratch)
    results = pl.pallas_call(
        partial(whole_kernel, length, names),
        out_shape=tuple(outputs.values()),
        in_specs=[anywhere if name in in_place else in_vmem for name in inputs],
        out_specs=[in_vmem] * len(outputs),
        scratch_shapes=list(scratch.values()),
        compiler_params=pltpu.CompilerParams(
            collective_id=0, has_side_effects=True, vmem_limit_bytes=LIMIT_MIB * 2**20
        ),
        name="layer_step",
    )(*inputs.values())
    return write_out(tokens, *results)


def solution(mesh):
    in_specs = (
        P(("seq", "wsh"), "ctx", None),
        P(("seq", "wsh"), "ctx"),
        P(("seq", "wsh"), "ctx", None),
        P(("seq", "wsh"), "ctx", None),
        P(("seq", "wsh"), "ctx", None),
        P(("seq", "wsh"), "ctx"),
        P(("seq", "wsh"), None),
        P(("seq", "wsh"), None),
        P(("seq", "wsh"), None),
        P(("seq", "wsh"), None),
        P(("seq", "wsh"), None),
        P(("seq", "wsh")),
        P(("seq", "wsh")),
        P(("seq", "wsh")),
        P(("seq", "wsh")),
        P(("seq", "wsh")),
        P("ctx", ("seq", "wsh"), None),
        P("ctx", ("seq", "wsh"), None),
    )
    out_specs = (
        P(("seq", "wsh"), "ctx", None),
        P(("seq", "wsh"), "ctx"),
        P(("seq", "wsh"), "ctx", None),
        P(("seq", "wsh"), "ctx"),
        P(("seq", "wsh"), None),
        P(("seq", "wsh"), None),
        P(("seq", "wsh"), None),
        P(("seq", "wsh"), None),
        P(("seq", "wsh"), None),
        P(("seq", "wsh")),
        P(("seq", "wsh")),
        P(("seq", "wsh")),
        P(("seq", "wsh")),
        P(("seq", "wsh")),
        P("ctx", ("seq", "wsh"), None),
        P("ctx", ("seq", "wsh"), None),
    )
    body = fast_body if mesh.shape["ctx"] == 4 else general_body
    return jax.shard_map(body, mesh=mesh, in_specs=in_specs, out_specs=out_specs, check_vma=False)
```
